128 devices in a mesh: lat: 32 (over x, z, core), rad: 4 (over y).
Axes of the slice: x: 4, y: 4, z: 4, core: 2. Of those that a mesh axis runs over, the one named last changes fastest.
Arguments:
- kernel: bfloat16 [4096, 4, 64, 256], P(('lat', 'rad')), may hold values from -0.1875 to 0.1875
- target_device: int32 [4096, 4], P(('lat', 'rad')), may hold values from 0 to 127, all different within a row; in each aligned block of 32 rows (0 to 31, 32 to 63, ...) at most 2 rows name the same one
- target_block: int32 [4096, 4], P(('lat', 'rad')), may hold values from 0 to 127
- counts: int32 [4096], P(('lat', 'rad')), may hold values from 16 to 64
- traveltimes: float32 [4096, 64], P(('lat', 'rad')), may hold values from -6 to 6
- prior_residual: float32 [4096, 64], P(('lat', 'rad')), may hold values from -12 to 12
Outputs:
- model_update: float32 [32, 512, 256], P('rad', 'lat')
- data_vector: float32 [4096, 64], P(('lat', 'rad'))
The draws below stay inside these ranges and needn't reach their ends.
Inputs may be any that keep to these rules, and one draw needn't show every extreme that they name: `target_device`: each ray block names 4 different devices; among the ray blocks of one device at most 2 name the same device, and some device is named by exactly 2 of them.
All inputs are finite; a program needn't handle non-finite values.
Results may differ from the reference program's by a relative error of at most 0.007.
Values may be sent and summed in bfloat16 or wider, within the bound.
No kernel may reach another device: no remote copies, remote signals or barrier semaphores. Data moves between devices by JAX's collectives and lax.ppermute only.
A program may use at most 128 MiB of HBM per device.

```python
import math
import jax
import jax.numpy as jnp
import numpy as np
from jax import lax

RAYS = 64
CELLS = 256
K = 4
ITERS = 3
RB_DEV = 32
MB_R = 8
MB_L = 16
CAP = 2
NRB = 4096
N_LAT = 32
N_RAD = 4
DEVICES = 128


def place_ends(drawn, own_key, least, high):
    index_at = [jax.random.randint(jax.random.fold_in(own_key, axis), (), 0, length) for axis, length in enumerate(drawn.shape)]
    main_axis = drawn.shape.index(max(drawn.shape))
    beside = index_at[:main_axis] + [(index_at[main_axis] + 1) % drawn.shape[main_axis]] + index_at[main_axis + 1:]
    return drawn.at[tuple(index_at)].set(least).at[tuple(beside)].set(high)


def block_scale(rng, shape, split, low, high):
    level, own = 1.0, jax.random.fold_in(rng, 6)
    for dim, blocks in split:
        heights = jnp.exp(jax.random.uniform(jax.random.fold_in(own, dim), (blocks,), jnp.float32, low / len(split), high / len(split)))
        level = level * jnp.repeat(heights, shape[dim] // blocks).reshape([-1 if axis == dim else 1 for axis in range(len(shape))])
    return level


def routed_block(key, own, number, rows, count, top, bound, skew):
    sequence = jax.random.permutation(key, count)
    crowded, usual = shares(count, rows * top, bound, skew, True), shares(count, rows * top, bound, skew, False)
    places = jnp.arange(count)

    def named(lengths, turn):
        used = int((lengths > 0).sum())
        fixed = max(1, used // 4)
        passed = fixed + (places - fixed + turn * (used - fixed)) % max(1, count - fixed)
        return jnp.zeros((count,), jnp.int32).at[sequence[jnp.where(places < fixed, places, passed)]].set(jnp.asarray(lengths, jnp.int32))

    lengths = jnp.where(number % 4 == 0, named(crowded, number // 4), named(usual, number - number // 4 - 1))
    mixed = jax.random.permutation(jax.random.fold_in(own, 3), count)
    source_of, taker = mixed[0:count // 2 * 2:2], mixed[1:count // 2 * 2:2]
    slack = jnp.minimum(lengths[source_of] - 1, bound - lengths[taker]) // 2
    slack = jnp.where((source_of == sequence[0]) | (taker == sequence[0]) | (lengths[taker] == 0), 0, jnp.maximum(slack, 0))
    passed = jax.random.randint(jax.random.fold_in(own, 4), (count // 2,), 0, 1 << 20) % (slack + 1)
    lengths = lengths.at[source_of].add(-passed).at[taker].add(passed)
    labels = jnp.searchsorted(jnp.cumsum(lengths), jnp.arange(rows * top), side="right").astype(jnp.int32)
    table = labels.reshape(top, rows).T
    table = table[jax.random.permutation(jax.random.fold_in(own, 1), rows)]
    turn = jax.random.randint(jax.random.fold_in(own, 2), (rows, 1), 0, top)
    return jnp.take_along_axis(table, (jnp.arange(top)[None, :] + turn) % top, axis=1)


def shares(number_of, total, most, skew, full):
    loads = [(1 << 20) // math.isqrt(standing ** skew) + 1 for standing in range(1, number_of + 1)]
    largest = most if full else min(most, max(-(-total // number_of), total * loads[0] // sum(loads)))
    least = 1 if total - largest >= number_of - 1 else 0
    given, spare = [largest] + [least] * (number_of - 1), total - largest - least * (number_of - 1)
    while spare > 0:
        free = [i for i in range(1, number_of) if given[i] < largest] or [i for i in range(1, number_of) if given[i] < most]
        mass, left = sum([loads[i] for i in free]), spare
        for i in free:
            addition = min(most - given[i], max(1, left * loads[i] // mass), spare)
            given[i] = given[i] + addition
            spare = spare - addition
    return np.array(given)


def normal_values(rng, extent, spread, reach, shards=(), kind=jnp.bfloat16):
    entries = jax.random.normal(rng, extent, jnp.float32) * spread
    if len(shards) > 0:
        entries = block_scale(rng, extent, shards, -0.22, 0.18) * entries
    return jnp.clip(entries, min=-reach, max=reach).astype(kind)


def setup_inputs(seed: int = 0) -> dict:
    key_of = jax.random.split(jax.random.key(seed), 7)
    kernel = normal_values(key_of[0], (NRB, K, RAYS, CELLS), (K * CELLS) ** -0.5, 0.1875, ((0, 128),))
    target_device_keys = jax.random.split(jax.random.fold_in(key_of[1], 1), NRB // RB_DEV)
    target_device_turns = jax.random.permutation(jax.random.fold_in(key_of[1], 3), NRB // RB_DEV)
    target_device = jax.vmap(lambda own, number: routed_block(jax.random.fold_in(key_of[1], 2), own, number, RB_DEV, DEVICES, K, CAP, 2))(target_device_keys, target_device_turns).reshape((NRB, K))
    target_block = place_ends(jax.random.randint(key_of[2], (NRB, K), 0, MB_R * MB_L), jax.random.fold_in(key_of[2], 1), 0, (MB_R * MB_L) - 1).astype(jnp.int32)
    counts = place_ends(jax.random.randint(key_of[3], (NRB,), RAYS // 4, RAYS + 1), jax.random.fold_in(key_of[3], 1), RAYS // 4, RAYS).astype(jnp.int32)
    traveltimes = normal_values(key_of[4], (NRB, RAYS), 1.0, 6.0, ((0, 128),), jnp.float32)
    prior_residual = normal_values(key_of[5], (NRB, RAYS), 2.0, 12.0, ((0, 128),), jnp.float32)
    return dict(kernel=kernel, target_device=target_device, target_block=target_block, counts=counts, traveltimes=traveltimes, prior_residual=prior_residual)


FREEDOM = 4.0
DAMPING = 0.3

def block_index(target_device, target_block):
    lat_pos = target_device // N_RAD
    rad_pos = target_device % N_RAD
    row_index = rad_pos * MB_R + target_block // MB_L
    col_index = lat_pos * MB_L + target_block % MB_L
    return (row_index * (MB_L * N_LAT) + col_index).astype(jnp.int32)

def forward(kernel, index, model_field):
    flat_model = model_field.reshape(-1, CELLS).astype(jnp.bfloat16)
    groups = kernel.reshape(N_LAT * N_RAD, RB_DEV, K, RAYS, CELLS)
    lists = index.reshape(N_LAT * N_RAD, RB_DEV, K)

    def per_group(inputs_pair):
        tile_group, id_group = inputs_pair
        blocks = flat_model[id_group]
        return jnp.einsum('bkrc,bkc->br', tile_group.astype(jnp.float32), blocks.astype(jnp.float32))
    return lax.map(per_group, (groups, lists)).reshape(N_LAT * N_RAD * RB_DEV, RAYS)

def adjoint(kernel, index, ray_values):
    rounded = ray_values.astype(jnp.bfloat16).reshape(N_LAT * N_RAD, RB_DEV, RAYS)
    groups = kernel.reshape(N_LAT * N_RAD, RB_DEV, K, RAYS, CELLS)

    def per_group(inputs_pair):
        tile_group, row_group = inputs_pair
        return jnp.einsum('bkrc,br->bkc', tile_group.astype(jnp.float32), row_group.astype(jnp.float32))
    partial_value = lax.map(per_group, (groups, rounded))
    summed = jax.ops.segment_sum(partial_value.reshape(-1, CELLS), index.reshape(-1), num_segments=MB_R * N_RAD * MB_L * N_LAT)
    return summed.reshape(MB_R * N_RAD, MB_L * N_LAT, CELLS)

def roughen(model_field):
    padded = jnp.pad(model_field, ((1, 1), (1, 1), (0, 0)))
    beside = padded[2:, 1:-1] + padded[:-2, 1:-1] + padded[1:-1, 2:] + padded[1:-1, :-2]
    return 4.0 * model_field - beside

def reference(kernel, target_device, target_block, counts, traveltimes, prior_residual):
    index = block_index(target_device, target_block)
    ray_mask = (jnp.arange(RAYS, dtype=jnp.int32)[None, :] < counts[:, None]).astype(jnp.float32)
    weights = ray_mask * jnp.sqrt((FREEDOM + 1.0) / (FREEDOM + prior_residual * prior_residual))
    data_vector = weights * traveltimes
    beta_norm = jnp.sqrt(jnp.sum(data_vector * data_vector))
    data_vector = data_vector / beta_norm
    model_dir = adjoint(kernel, index, weights * data_vector)
    alpha_norm = jnp.sqrt(jnp.sum(model_dir * model_dir))
    model_dir = model_dir / alpha_norm
    pen_vec = jnp.zeros_like(model_dir)
    search_dir = model_dir
    model_update = jnp.zeros_like(model_dir)
    phi_bar = beta_norm
    rho_bar = alpha_norm
    for sweep in range(ITERS):
        data_vector = weights * forward(kernel, index, model_dir) - alpha_norm * data_vector
        pen_vec = DAMPING * roughen(model_dir) - alpha_norm * pen_vec
        beta_norm = jnp.sqrt(jnp.sum(data_vector * data_vector) + jnp.sum(pen_vec * pen_vec))
        data_vector = data_vector / beta_norm
        pen_vec = pen_vec / beta_norm
        model_dir = adjoint(kernel, index, weights * data_vector) + DAMPING * roughen(pen_vec) - beta_norm * model_dir
        alpha_norm = jnp.sqrt(jnp.sum(model_dir * model_dir))
        model_dir = model_dir / alpha_norm
        rho_value = jnp.sqrt(rho_bar * rho_bar + beta_norm * beta_norm)
        cosine = rho_bar / rho_value
        sine = beta_norm / rho_value
        theta_value = sine * alpha_norm
        rho_bar = -cosine * alpha_norm
        phi_value = cosine * phi_bar
        phi_bar = sine * phi_bar
        model_update = model_update + phi_value / rho_value * search_dir
        search_dir = model_dir - theta_value / rho_value * search_dir
    return (model_update, data_vector)
```

```python
import functools

import jax
import jax.numpy as jnp
from jax import lax
from jax.experimental import pallas as pl
from jax.experimental.pallas import tpu as pltpu
from jax.sharding import PartitionSpec as P

ITERS = 3
MB_R = 8
MB_L = 16
FREEDOM = 4.0
DAMPING = 0.3

AXES = ("lat", "rad")
CHUNK = 8
NORM_ROW = 4
ID_ROW = 5
LANES = 128

F32 = jnp.float32
BF16 = jnp.bfloat16
NT = (((1,), (1,)), ((), ()))


def iota(shape, dim):
    return lax.broadcasted_iota(jnp.int32, shape, dim)


def matmul(a, b):
    return jnp.dot(a, b, preferred_element_type=F32)


def total(x):
    return jnp.sum(jnp.sum(x, axis=1, keepdims=True), axis=0, keepdims=True)


def norm_row(partial):
    high = partial.astype(BF16).astype(F32)
    middle = (partial - high).astype(BF16).astype(F32)
    low = partial - high - middle
    lane = iota((1, LANES), 1)
    return jnp.where(lane == 0, high, jnp.where(lane == 1, middle, jnp.where(lane == 2, low, 0.0)))


def with_norm(packed, partial):
    rows = iota(packed.shape, 0) % CHUNK
    return jnp.where(rows == NORM_ROW, norm_row(partial), packed).astype(BF16)


def received_norm(received):
    rows = received.shape[0]
    picks = jnp.where(iota((8, rows), 1) % CHUNK == NORM_ROW, 1.0, 0.0).astype(BF16)
    sums = matmul(picks, received)[0:1, :]
    return jnp.sqrt(jnp.sum(jnp.where(iota((1, LANES), 1) < 3, sums, 0.0), axis=1, keepdims=True))


def stacked(x):
    return jnp.concatenate([x[:, :LANES], x[:, LANES:]], axis=0)


def unstacked(x):
    half = x.shape[0] // 2
    return jnp.concatenate([x[:half], x[half:]], axis=1)


def adjoint_products(kernel_ref, y, out_ref, ray_blocks, fanout):
    high = y.astype(BF16).astype(F32)
    low = y - high
    high = jnp.concatenate([high] * fanout, axis=1)
    low = jnp.concatenate([low] * fanout, axis=1)
    width = high.shape[1]
    ray_len = width // fanout
    row, lane = iota((2 * fanout, width), 0), iota((2 * fanout, width), 1)
    own = lane // ray_len == row % fanout
    for b in range(ray_blocks):
        lhs = jnp.where(row < fanout, high[b : b + 1], low[b : b + 1])
        lhs = jnp.where(own, lhs, 0.0).astype(BF16)
        both = matmul(lhs, kernel_ref[b * width : (b + 1) * width, :])
        out_ref[b * fanout : (b + 1) * fanout, :] = both[:fanout] + both[fanout:]


def forward_products(kernel_ref, blocks, ray_blocks, fanout, ray_len):
    entries = ray_blocks * fanout
    lane = iota((ray_len, entries), 1)
    picked = jnp.zeros((ray_len, entries), F32)
    group = 16
    for start in range(0, entries, group):
        products = lax.dot_general(
            kernel_ref[start * ray_len : (start + group) * ray_len, :], blocks, NT, preferred_element_type=F32
        )
        for i in range(group):
            picked = jnp.where(lane == start + i, products[i * ray_len : (i + 1) * ray_len], picked)
    member = jnp.where(iota((ray_blocks, entries), 1) // fanout == iota((ray_blocks, entries), 0), 1.0, 0.0)
    return lax.dot_general(member, picked, NT, preferred_element_type=F32, precision=lax.Precision.HIGHEST)


def roughen(field, up, down, left, right):
    rows = field.shape[0]
    place = iota(field.shape, 0) % MB_L
    spread = lambda side: jnp.concatenate(
        [jnp.broadcast_to(side[r : r + 1], (MB_L, side.shape[1])) for r in range(MB_R)], axis=0
    )
    north = jnp.concatenate([up, field[: rows - MB_L]], axis=0)
    south = jnp.concatenate([field[MB_L:], down], axis=0)
    west = jnp.where(place == 0, spread(left), pltpu.roll(field, 1, 0))
    east = jnp.where(place == MB_L - 1, spread(right), pltpu.roll(field, rows - 1, 0))
    return 4.0 * field - (south + north + east + west)


def write_edges(field, first, last, lefts, rights):
    rows = field.shape[0]
    first[...] = field[:MB_L]
    last[...] = field[rows - MB_L :]
    for r in range(MB_R):
        lefts[r : r + 1, :] = field[r * MB_L : r * MB_L + 1]
        rights[r : r + 1, :] = field[(r + 1) * MB_L - 1 : (r + 1) * MB_L]


def start_kernel(
    kernel_ref, device_ref, block_ref, counts_ref, times_ref, prior_ref,
    send_ref, weights_ref, data_ref, pick_ref, place_ref, partial_ref,
):
    ray_blocks, fanout = device_ref.shape
    ray_len = times_ref.shape[1]
    entries = ray_blocks * fanout
    rows = send_ref.shape[0]

    member = jnp.where(iota((entries, ray_blocks), 0) // fanout == iota((entries, ray_blocks), 1), 1.0, 0.0)
    turn = iota((entries, fanout), 0) % fanout == iota((entries, fanout), 1)

    def column(table_ref):
        spread = matmul(member.astype(BF16), table_ref[...].astype(F32).astype(BF16))
        return jnp.sum(jnp.where(turn, spread, 0.0), axis=1, keepdims=True)

    diagonal = iota((entries, entries), 0) == iota((entries, entries), 1)

    def as_row(col):
        return jnp.sum(jnp.where(diagonal, col, 0.0), axis=0, keepdims=True)

    target = column(device_ref)
    block = column(block_ref)
    target_row = as_row(target)
    earlier = iota((entries, entries), 1) < iota((entries, entries), 0)
    rank = jnp.sum(jnp.where(earlier & (target == target_row), 1.0, 0.0), axis=1, keepdims=True)
    first = target * CHUNK + 2.0 * rank
    first_row = as_row(first)

    to_col = jnp.concatenate([first, first + 1.0], axis=0).astype(jnp.int32)
    pick_ref[...] = jnp.where(iota((2 * entries, rows), 1) == to_col, 1.0, 0.0).astype(BF16)
    to_row = jnp.concatenate([first_row, first_row + 1.0], axis=1).astype(jnp.int32)
    place_ref[...] = jnp.where(iota((rows, 2 * entries), 0) == to_row, 1.0, 0.0).astype(BF16)

    same = iota((ray_blocks, ray_blocks), 0) == iota((ray_blocks, ray_blocks), 1)
    counts = jnp.sum(jnp.where(same, counts_ref[...].astype(F32), 0.0), axis=1, keepdims=True)
    mask = jnp.where(iota((ray_blocks, ray_len), 1).astype(F32) < counts, 1.0, 0.0)
    prior = prior_ref[...]
    weights = mask * jnp.sqrt((FREEDOM + 1.0) / (FREEDOM + prior * prior))
    weights_ref[...] = weights
    data = weights * times_ref[...]
    data_ref[...] = data

    adjoint_products(kernel_ref, weights * data, partial_ref, ray_blocks, fanout)
    ids = jnp.where(iota((entries, LANES), 1).astype(F32) == rank, block + 1.0, 0.0).astype(BF16)
    id_rows = (target_row * CHUNK + ID_ROW).astype(jnp.int32)
    id_place = jnp.where(iota((rows, entries), 0) == id_rows, 1.0, 0.0).astype(BF16)
    packed = matmul(place_ref[...], stacked(partial_ref[...].astype(BF16))) + matmul(id_place, ids)
    send_ref[...] = with_norm(packed, total(data * data))


def scalars_row(*values):
    lane = iota((8, LANES), 1)
    out = jnp.zeros((8, LANES), F32)
    for i, value in enumerate(values):
        out = jnp.where(lane == i, value, out)
    return out


def first_model_kernel(
    received_ref,
    send_ref, field_ref, scalar_ref, gather_ref, scatter_ref, first_ref, last_ref, left_ref, right_ref,
):
    received = received_ref[...]
    rows = received.shape[0]
    devices = rows // CHUNK
    blocks = MB_R * MB_L
    pick = jnp.where(iota((devices, rows), 1) == iota((devices, rows), 0) * CHUNK + ID_ROW, 1.0, 0.0).astype(BF16)
    ids = matmul(pick, received).astype(BF16)
    owner = jnp.where(iota((rows, devices), 0) // CHUNK == iota((rows, devices), 1), 1.0, 0.0).astype(BF16)
    spread = matmul(owner, ids)
    place = iota((rows, LANES), 0) % CHUNK
    slot = (place < NORM_ROW) & (iota((rows, LANES), 1) == place // 2)
    ident = jnp.sum(jnp.where(slot, spread, 0.0), axis=1, keepdims=True) - 1.0
    wide = jnp.broadcast_to(ident, (rows, LANES))
    lane = iota((rows, LANES), 1)
    hit = wide == lane.astype(F32)
    for half in range(2):
        chosen = jnp.where(hit & (place % 2 == half), 1.0, 0.0)
        gather_ref[:, half * LANES : (half + 1) * LANES] = chosen.astype(BF16)
        scatter_ref[half * blocks : (half + 1) * blocks, :] = chosen.T.astype(BF16)

    beta = received_norm(received)
    field = unstacked(matmul(scatter_ref[...], received)) / beta
    field_ref[...] = field
    write_edges(field, first_ref, last_ref, left_ref, right_ref)
    scalar_ref[...] = scalars_row(beta)
    send_ref[...] = with_norm(matmul(gather_ref[...], stacked(field.astype(BF16))), total(field * field))


def ray_step(
    sweep, received_ref, kernel_ref, pick_ref, weights_ref, data_ref, field_ref, scalar_ref,
    up_ref, down_ref, west_ref, east_ref, pen_ref, search_ref, state_ref,
):
    received = received_ref[...]
    ray_blocks, ray_len = data_ref.shape
    fanout = pick_ref.shape[0] // 2 // ray_blocks
    alpha = received_norm(received)
    blocks = unstacked(matmul(pick_ref[...], received)).astype(BF16)
    products = forward_products(kernel_ref, blocks, ray_blocks, fanout, ray_len)
    beta = scalar_ref[0:1, 0:1]
    data = weights_ref[...] * (products / alpha) - alpha * (data_ref[...] / beta)
    field = field_ref[...]
    pen = DAMPING * (roughen(field, up_ref[...], down_ref[...], west_ref[...], east_ref[...]) / alpha)
    if sweep:
        pen = pen - alpha * (pen_ref[...] / beta)
    direction = field / alpha
    if sweep:
        phi_bar, rho, cosine, sine = [state_ref[0:1, i : i + 1] for i in range(4)]
        search = direction - (sine * alpha / rho) * search_ref[...]
        rho_bar = -cosine * alpha
    else:
        phi_bar, rho_bar = beta, alpha
        search = direction
    partial = total(data * data) + total(pen * pen)
    return data, pen, direction, search, phi_bar, rho_bar, partial


def ray_kernel(sweep, *refs):
    inputs = 15 if sweep else 12
    if sweep:
        (received_ref, kernel_ref, pick_ref, place_ref, weights_ref, data_ref, field_ref, scalar_ref,
         up_ref, down_ref, west_ref, east_ref, pen_ref, search_ref, state_ref) = refs[:inputs]
    else:
        (received_ref, kernel_ref, pick_ref, place_ref, weights_ref, data_ref, field_ref, scalar_ref,
         up_ref, down_ref, west_ref, east_ref) = refs[:inputs]
        pen_ref = search_ref = state_ref = None
    (send_ref, data_out, pen_out, direction_out, search_out, state_out,
     first_ref, last_ref, left_ref, right_ref, partial_ref) = refs[inputs:]
    data, pen, direction, search, phi_bar, rho_bar, partial = ray_step(
        sweep, received_ref, kernel_ref, pick_ref, weights_ref, data_ref, field_ref, scalar_ref,
        up_ref, down_ref, west_ref, east_ref, pen_ref, search_ref, state_ref,
    )
    data_out[...] = data
    pen_out[...] = pen
    direction_out[...] = direction
    search_out[...] = search
    state_out[...] = scalars_row(phi_bar, rho_bar)
    write_edges(pen, first_ref, last_ref, left_ref, right_ref)
    ray_blocks = data.shape[0]
    fanout = pick_ref.shape[0] // 2 // ray_blocks
    adjoint_products(kernel_ref, weights_ref[...] * data, partial_ref, ray_blocks, fanout)
    send_ref[...] = with_norm(matmul(place_ref[...], stacked(partial_ref[...].astype(BF16))), partial)


def last_ray_kernel(
    sweep, received_ref, kernel_ref, pick_ref, weights_ref, data_ref, field_ref, scalar_ref,
    up_ref, down_ref, west_ref, east_ref, pen_ref, search_ref, state_ref,
    send_ref, data_out, search_out, state_out,
):
    data, pen, direction, search, phi_bar, rho_bar, partial = ray_step(
        sweep, received_ref, kernel_ref, pick_ref, weights_ref, data_ref, field_ref, scalar_ref,
        up_ref, down_ref, west_ref, east_ref, pen_ref, search_ref, state_ref,
    )
    data_out[...] = data
    search_out[...] = search
    state_out[...] = scalars_row(phi_bar, rho_bar)
    send_ref[...] = jnp.broadcast_to(partial, send_ref.shape)


def rotate(beta, state_ref):
    phi_bar, rho_bar = state_ref[0:1, 0:1], state_ref[0:1, 1:2]
    rho = jnp.sqrt(rho_bar * rho_bar + beta * beta)
    cosine, sine = rho_bar / rho, beta / rho
    return cosine * phi_bar / rho, sine * phi_bar, rho, cosine, sine


def model_kernel(
    sweep, received_ref, scatter_ref, gather_ref, pen_ref, direction_ref, search_ref, update_ref, state_ref,
    up_ref, down_ref, west_ref, east_ref,
    send_ref, field_ref, scalar_ref, update_out, state_out, first_ref, last_ref, left_ref, right_ref,
):
    received = received_ref[...]
    beta = received_norm(received)
    gathered = unstacked(matmul(scatter_ref[...], received))
    rough = roughen(pen_ref[...], up_ref[...], down_ref[...], west_ref[...], east_ref[...])
    field = (gathered + DAMPING * rough) / beta - beta * direction_ref[...]
    field_ref[...] = field
    write_edges(field, first_ref, last_ref, left_ref, right_ref)
    send_ref[...] = with_norm(matmul(gather_ref[...], stacked(field.astype(BF16))), total(field * field))
    scalar_ref[...] = scalars_row(beta)
    step, phi_bar, rho, cosine, sine = rotate(beta, state_ref)
    update = step * search_ref[...]
    update_out[...] = update if sweep == 0 else update_ref[...] + update
    state_out[...] = scalars_row(phi_bar, rho, cosine, sine)


def last_kernel(norms_ref, data_ref, search_ref, update_ref, state_ref, update_out, data_out):
    beta = jnp.sqrt(jnp.sum(norms_ref[...], axis=0, keepdims=True)[:, 0:1])
    step = rotate(beta, state_ref)[0]
    update_out[...] = update_ref[...] + step * search_ref[...]
    data_out[...] = data_ref[...] / beta


def call(kernel, name, outputs, scratch, operands, flops=0):
    bytes_accessed = sum(x.size * x.dtype.itemsize for x in operands)
    return pl.pallas_call(
        kernel,
        name=name,
        out_shape=[jax.ShapeDtypeStruct(shape, dtype) for shape, dtype in outputs],
        in_specs=[pl.BlockSpec(memory_space=pltpu.VMEM)] * len(operands),
        out_specs=[pl.BlockSpec(memory_space=pltpu.VMEM)] * len(outputs),
        scratch_shapes=scratch,
        compiler_params=pltpu.CompilerParams(vmem_limit_bytes=40 << 20),
        cost_estimate=pl.CostEstimate(flops=flops, bytes_accessed=bytes_accessed, transcendentals=0),
    )(*operands)


def exchange(packed, devices):
    rows, lanes = packed.shape
    chunks = packed.reshape(devices, rows // devices, lanes)
    return lax.all_to_all(chunks, AXES, split_axis=0, concat_axis=0, tiled=True).reshape(rows, lanes)


def halos(first, last, left, right):
    def shift(x, axis, step):
        count = lax.axis_size(axis)
        pairs = [(i, i + step) for i in range(count) if 0 <= i + step < count]
        return lax.ppermute(x, axis, pairs)
    return shift(last, "rad", 1), shift(first, "rad", -1), shift(right, "lat", 1), shift(left, "lat", -1)


def body(kernel, target_device, target_block, counts, traveltimes, prior_residual):
    devices = lax.axis_size("lat") * lax.axis_size("rad")
    ray_blocks, fanout, ray_len, cells = kernel.shape
    entries = ray_blocks * fanout
    rows = devices * CHUNK
    blocks = MB_R * MB_L
    tiles = kernel.reshape(entries * ray_len, cells)
    flops = 4 * entries * ray_len * cells

    packet = ((rows, LANES), BF16)
    ray = ((ray_blocks, ray_len), F32)
    model = ((blocks, cells), F32)
    scalar = ((8, LANES), F32)
    edges = [((MB_L, cells), F32)] * 2 + [((MB_R, cells), F32)] * 2
    partials = [pltpu.VMEM((entries, cells), F32)]

    send, weights, data, pick, place = call(
        start_kernel, "start",
        [packet, ray, ray, ((2 * entries, rows), BF16), ((rows, 2 * entries), BF16)], partials,
        (tiles, target_device, target_block, counts.reshape(1, ray_blocks), traveltimes, prior_residual), flops,
    )
    received = exchange(send, devices)
    send, field, scalars, gather, scatter, *edge = call(
        first_model_kernel, "first_model",
        [packet, model, scalar, ((rows, 2 * blocks), BF16), ((2 * blocks, rows), BF16)] + edges, [],
        (received,), flops,
    )
    pen = search = update = state = None
    for sweep in range(ITERS):
        around = halos(*edge)
        received = exchange(send, devices)
        carried = (pen, search, state) if sweep else ()
        if sweep == ITERS - 1:
            send, data, search, state = call(
                functools.partial(last_ray_kernel, sweep), "last_ray",
                [((devices, LANES), F32), ray, model, scalar], [],
                (received, tiles, pick, weights, data, field, scalars, *around, *carried), flops,
            )
            norms = lax.all_to_all(
                send.reshape(devices, 1, LANES), AXES, split_axis=0, concat_axis=0, tiled=True
            ).reshape(devices, LANES)
            update, data = call(last_kernel, "last", [model, ray], [], (norms, data, search, update, state))
            break
        send, data, pen, direction, search, state, *edge = call(
            functools.partial(ray_kernel, sweep), "ray",
            [packet, ray, model, model, model, scalar] + edges, partials,
            (received, tiles, pick, place, weights, data, field, scalars, *around, *carried), flops,
        )
        around = halos(*edge)
        received = exchange(send, devices)
        before = update if sweep else search
        send, field, scalars, update, state, *edge = call(
            functools.partial(model_kernel, sweep), "model",
            [packet, model, scalar, model, scalar] + edges, [],
            (received, scatter, gather, pen, direction, search, before, state, *around), flops,
        )
    return (update.reshape(MB_R, MB_L, cells), data)


def solution(mesh):
    in_specs = (
        P(("lat", "rad"), None, None, None),
        P(("lat", "rad"), None),
        P(("lat", "rad"), None),
        P(("lat", "rad")),
        P(("lat", "rad"), None),
        P(("lat", "rad"), None),
    )
    out_specs = (P("rad", "lat", None), P(("lat", "rad"), None))
    return jax.shard_map(body, mesh=mesh, in_specs=in_specs, out_specs=out_specs, check_vma=False)
```

```python
import functools

import jax
import jax.numpy as jnp
from jax import lax
from jax.experimental import pallas as pl
from jax.experimental.pallas import tpu as pltpu
from jax.sharding import PartitionSpec as P

ITERS = 3
MB_R = 8
MB_L = 16
FREEDOM = 4.0
DAMPING = 0.3

AXES = ("lat", "rad")
CHUNK = 8
NORM_ROW = 4
ID_ROW = 5
CELL_ROW = 6
LANES = 128
PARTS = 4

F32 = jnp.float32
BF16 = jnp.bfloat16
NT = (((1,), (1,)), ((), ()))


def iota(shape, dim):
    return lax.broadcasted_iota(jnp.int32, shape, dim)


def matmul(a, b):
    return jnp.dot(a, b, preferred_element_type=F32)


def total(x):
    return jnp.sum(jnp.sum(x, axis=1, keepdims=True), axis=0, keepdims=True)


def norm_row(partial):
    high = partial.astype(BF16).astype(F32)
    middle = (partial - high).astype(BF16).astype(F32)
    low = partial - high - middle
    lane = iota((1, LANES), 1)
    return jnp.where(lane == 0, high, jnp.where(lane == 1, middle, jnp.where(lane == 2, low, 0.0)))


def with_norm(packed, partial):
    rows = iota(packed.shape, 0) % CHUNK
    return jnp.where(rows == NORM_ROW, norm_row(partial), packed).astype(BF16)


def norm_of(sums):
    lane = iota((1, LANES), 1)
    return jnp.sqrt(jnp.sum(jnp.where(lane < 3, sums[0:1, :], 0.0), axis=1, keepdims=True))


def ones_where(condition):
    return jnp.where(condition, 1.0, 0.0).astype(BF16)


def write_cell_picks(ref, start, devices):
    rows = devices * CHUNK
    device, row = iota((devices, rows), 0), iota((devices, rows), 1)
    for j in range(2):
        ref[start + j * devices : start + (j + 1) * devices, :] = ones_where(row == device * CHUNK + CELL_ROW + j)
    ref[start + 2 * devices :, :] = ones_where(iota((16, rows), 1) % CHUNK == NORM_ROW)


def write_cell_places(ref, start, devices):
    rows = devices * CHUNK
    row, device = iota((rows, devices), 0), iota((rows, devices), 1)
    for j in range(2):
        ref[:, start + j * devices : start + (j + 1) * devices] = ones_where(row == device * CHUNK + CELL_ROW + j)


def stacked(x):
    return jnp.concatenate([x[:, :LANES], x[:, LANES:]], axis=0)


def unstacked(x):
    half = x.shape[0] // 2
    return jnp.concatenate([x[:half], x[half:]], axis=1)


def adjoint_products(kernel_ref, y, out_ref, ray_blocks, fanout, ready=None):
    high = y.astype(BF16).astype(F32)
    low = y - high
    high = jnp.concatenate([high] * fanout, axis=1)
    low = jnp.concatenate([low] * fanout, axis=1)
    width = high.shape[1]
    ray_len = width // fanout
    row, lane = iota((2 * fanout, width), 0), iota((2 * fanout, width), 1)
    own = lane // ray_len == row % fanout
    for b in range(ray_blocks):
        if ready is not None:
            ready(b)
        lhs = jnp.where(row < fanout, high[b : b + 1], low[b : b + 1])
        lhs = jnp.where(own, lhs, 0.0).astype(BF16)
        both = matmul(lhs, kernel_ref[b * width : (b + 1) * width, :])
        out_ref[b * fanout : (b + 1) * fanout, :] = both[:fanout] + both[fanout:]


def forward_products(kernel_ref, blocks, ray_blocks, fanout, ray_len):
    entries = ray_blocks * fanout
    lane = iota((ray_len, entries), 1)
    picked = jnp.zeros((ray_len, entries), F32)
    group = 16
    for start in range(0, entries, group):
        products = lax.dot_general(
            kernel_ref[start * ray_len : (start + group) * ray_len, :], blocks, NT, preferred_element_type=F32
        )
        for i in range(group):
            picked = jnp.where(lane == start + i, products[i * ray_len : (i + 1) * ray_len], picked)
    member = jnp.where(iota((ray_blocks, entries), 1) // fanout == iota((ray_blocks, entries), 0), 1.0, 0.0)
    return lax.dot_general(member, picked, NT, preferred_element_type=F32, precision=lax.Precision.HIGHEST)


def roughen(cell, rads):
    shape = cell.shape
    devices, blocks = shape
    device, block = iota(shape, 0), iota(shape, 1)
    rad, place = device % rads, block % MB_L
    lanes = lambda x, step: pltpu.roll(x, step % blocks, 1)
    owner = lambda x, step: pltpu.roll(x, step % devices, 0)
    up = lanes(cell, MB_L)
    north = jnp.where(block >= MB_L, up, jnp.where(rad > 0, owner(up, 1), 0.0))
    down = lanes(cell, -MB_L)
    south = jnp.where(block < blocks - MB_L, down, jnp.where(rad < rads - 1, owner(down, -1), 0.0))
    far = owner(lanes(cell, 1 - MB_L), rads)
    west = jnp.where(place > 0, lanes(cell, 1), jnp.where(device >= rads, far, 0.0))
    far = owner(lanes(cell, MB_L - 1), -rads)
    east = jnp.where(place < MB_L - 1, lanes(cell, -1), jnp.where(device < devices - rads, far, 0.0))
    return 4.0 * cell - (south + north + east + west)


def scalars_row(*values):
    lane = iota((8, LANES), 1)
    out = jnp.zeros((8, LANES), F32)
    for i, value in enumerate(values):
        out = jnp.where(lane == i, value, out)
    return out


def start_kernel(
    kernel_hbm, device_hbm, block_hbm, counts_hbm, times_hbm, prior_hbm,
    send_ref, tiles_ref, weights_ref, data_ref, pick_ref, place_ref,
    device_ref, block_ref, counts_ref, times_ref, prior_ref, partial_ref, small_sem, tile_sem,
):
    fanout, ray_blocks = device_ref.shape
    ray_len = times_ref.shape[1]
    entries = ray_blocks * fanout
    rows = send_ref.shape[0]
    devices = rows // CHUNK
    part = tiles_ref.shape[0] // PARTS

    small = [
        pltpu.make_async_copy(source, target, small_sem.at[i])
        for i, (source, target) in enumerate(
            ((device_hbm, device_ref), (block_hbm, block_ref), (counts_hbm, counts_ref),
             (times_hbm, times_ref), (prior_hbm, prior_ref))
        )
    ]
    large = [
        pltpu.make_async_copy(
            kernel_hbm.at[pl.ds(i * part, part), :], tiles_ref.at[pl.ds(i * part, part), :], tile_sem.at[i]
        )
        for i in range(PARTS)
    ]
    for copy in small + large:
        copy.start()
    write_cell_picks(pick_ref, 2 * entries, devices)
    write_cell_places(place_ref, 2 * entries, devices)
    for copy in small:
        copy.wait()

    member = ones_where(iota((entries, ray_blocks), 0) // fanout == iota((entries, ray_blocks), 1))
    turn = iota((entries, fanout), 0) % fanout == iota((entries, fanout), 1)

    def column(table_ref):
        table = table_ref[...].astype(F32).astype(BF16)
        spread = lax.dot_general(member, table, NT, preferred_element_type=F32)
        return jnp.sum(jnp.where(turn, spread, 0.0), axis=1, keepdims=True)

    diagonal = iota((entries, entries), 0) == iota((entries, entries), 1)

    def as_row(col):
        return jnp.sum(jnp.where(diagonal, col, 0.0), axis=0, keepdims=True)

    target = column(device_ref)
    block = column(block_ref)
    target_row = as_row(target)
    earlier = iota((entries, entries), 1) < iota((entries, entries), 0)
    rank = jnp.sum(jnp.where(earlier & (target == target_row), 1.0, 0.0), axis=1, keepdims=True)
    first = target * CHUNK + 2.0 * rank
    first_row = as_row(first)

    to_col = first.astype(jnp.int32)
    to_row = first_row.astype(jnp.int32)
    for half in range(2):
        here = slice(half * entries, (half + 1) * entries)
        pick_ref[here, :] = ones_where(iota((entries, rows), 1) == to_col + half)
        place_ref[:, here] = ones_where(iota((rows, entries), 0) == to_row + half)

    same = iota((ray_blocks, ray_blocks), 0) == iota((ray_blocks, ray_blocks), 1)
    counts = jnp.sum(jnp.where(same, counts_ref[...].astype(F32), 0.0), axis=1, keepdims=True)
    mask = jnp.where(iota((ray_blocks, ray_len), 1).astype(F32) < counts, 1.0, 0.0)
    prior = prior_ref[...]
    weights = mask * jnp.sqrt((FREEDOM + 1.0) / (FREEDOM + prior * prior))
    weights_ref[...] = weights
    data = weights * times_ref[...]
    data_ref[...] = data

    def ready(b):
        if b % (ray_blocks // PARTS) == 0:
            large[b // (ray_blocks // PARTS)].wait()

    adjoint_products(tiles_ref, weights * data, partial_ref, ray_blocks, fanout, ready)
    ids = jnp.where(iota((entries, LANES), 1).astype(F32) == rank, block + 1.0, 0.0).astype(BF16)
    id_rows = (target_row * CHUNK + ID_ROW).astype(jnp.int32)
    id_place = ones_where(iota((rows, entries), 0) == id_rows)
    packed = matmul(place_ref[:, : 2 * entries], stacked(partial_ref[...].astype(BF16))) + matmul(id_place, ids)
    send_ref[...] = with_norm(packed, total(data * data))


def send_field(send_ref, field, gather_ref):
    halves = [field[:, :LANES], field[:, LANES:]]
    packed = jnp.concatenate(halves + [half.T for half in halves], axis=0).astype(BF16)
    send_ref[...] = with_norm(matmul(gather_ref[...], packed), total(field * field))


def first_model_kernel(received_ref, send_ref, field_ref, state_ref, gather_ref, scatter_ref):
    received = received_ref[...]
    rows = received.shape[0]
    devices = rows // CHUNK
    blocks = MB_R * MB_L
    pick = ones_where(iota((devices, rows), 1) == iota((devices, rows), 0) * CHUNK + ID_ROW)
    ids = matmul(pick, received).astype(BF16)
    owner = ones_where(iota((rows, devices), 0) // CHUNK == iota((rows, devices), 1))
    spread = matmul(owner, ids)
    place = iota((rows, LANES), 0) % CHUNK
    lane = iota((rows, LANES), 1)
    slot = (place < NORM_ROW) & (lane == place // 2)
    ident = jnp.sum(jnp.where(slot, spread, 0.0), axis=1, keepdims=True) - 1.0
    hit = ident == lane.astype(F32)
    for half in range(2):
        here = slice(half * blocks, (half + 1) * blocks)
        chosen = jnp.where(hit & (place % 2 == half), 1.0, 0.0)
        gather_ref[:, here] = chosen.astype(BF16)
        scatter_ref[here, :] = chosen.T.astype(BF16)
    write_cell_picks(scatter_ref, 2 * blocks, devices)
    write_cell_places(gather_ref, 2 * blocks, devices)

    got = matmul(scatter_ref[...], received)
    beta = norm_of(got[2 * blocks + 2 * devices :])
    field = unstacked(got[: 2 * blocks]) / beta
    field_ref[...] = field
    state_ref[...] = scalars_row(beta)
    send_field(send_ref, field, gather_ref)


def ray_step(sweep, rads, received_ref, kernel_ref, pick_ref, weights_ref, data_ref, state_ref, pen_ref):
    received = received_ref[...]
    ray_blocks, ray_len = data_ref.shape
    devices = received.shape[0] // CHUNK
    got = matmul(pick_ref[...], received)
    entries = (got.shape[0] - 2 * devices - 16) // 2
    fanout = entries // ray_blocks
    alpha = norm_of(got[2 * entries + 2 * devices :])
    blocks = unstacked(got[: 2 * entries]).astype(BF16)
    products = forward_products(kernel_ref, blocks, ray_blocks, fanout, ray_len)
    beta = state_ref[0:1, 0:1]
    data = weights_ref[...] * (products / alpha) - alpha * (data_ref[...] / beta)
    partial = total(data * data)
    pens = []
    for j in range(2):
        cell = got[2 * entries + j * devices : 2 * entries + (j + 1) * devices]
        pen = DAMPING * (roughen(cell, rads) / alpha)
        if sweep:
            pen = pen - alpha * (pen_ref[j * devices : (j + 1) * devices] / beta)
        partial = partial + total(pen * pen)
        pens.append(pen)
    return alpha, data, pens, partial


def ray_kernel(sweep, rads, *refs):
    received_ref, kernel_ref, pick_ref, place_ref, weights_ref, data_ref, state_ref = refs[:7]
    pen_ref = refs[7] if sweep else None
    send_ref, data_out, pen_out, alpha_out, partial_ref = refs[-5:]
    alpha, data, pens, partial = ray_step(
        sweep, rads, received_ref, kernel_ref, pick_ref, weights_ref, data_ref, state_ref, pen_ref
    )
    data_out[...] = data
    pen_out[...] = jnp.concatenate(pens, axis=0)
    alpha_out[...] = scalars_row(alpha)
    ray_blocks = data.shape[0]
    fanout = partial_ref.shape[0] // ray_blocks
    adjoint_products(kernel_ref, weights_ref[...] * data, partial_ref, ray_blocks, fanout)
    rough = [DAMPING * roughen(pen, rads) for pen in pens]
    packed = jnp.concatenate([stacked(partial_ref[...])] + rough, axis=0).astype(BF16)
    send_ref[...] = with_norm(matmul(place_ref[...], packed), partial)


def last_ray_kernel(sweep, rads, *refs):
    send_ref, data_out, alpha_out = refs[-3:]
    alpha, data, pens, partial = ray_step(sweep, rads, *refs[:-3])
    data_out[...] = data
    alpha_out[...] = scalars_row(alpha)
    send_ref[...] = jnp.broadcast_to(partial, send_ref.shape)


def advance(sweep, beta, field_ref, alpha_ref, state_ref, search_ref, update_ref):
    alpha = alpha_ref[0:1, 0:1]
    direction = field_ref[...] / alpha
    if sweep:
        phi_bar, rho, cosine, sine = [state_ref[0:1, i : i + 1] for i in range(1, 5)]
        search = direction - (sine * alpha / rho) * search_ref[...]
        rho_bar = -cosine * alpha
    else:
        phi_bar, rho_bar = state_ref[0:1, 0:1], alpha
        search = direction
    rho = jnp.sqrt(rho_bar * rho_bar + beta * beta)
    cosine, sine = rho_bar / rho, beta / rho
    update = (cosine * phi_bar / rho) * search
    if sweep:
        update = update_ref[...] + update
    return direction, search, update, scalars_row(beta, sine * phi_bar, rho, cosine, sine)


def model_kernel(sweep, *refs):
    received_ref, scatter_ref, gather_ref, field_ref, alpha_ref, state_ref = refs[:6]
    search_ref, update_ref = refs[6:8] if sweep else (None, None)
    send_ref, field_out, state_out, search_out, update_out = refs[-5:]
    received = received_ref[...]
    devices = received.shape[0] // CHUNK
    got = matmul(scatter_ref[...], received)
    blocks = field_ref.shape[0]
    beta = norm_of(got[2 * blocks + 2 * devices :])
    direction, search, update, state = advance(
        sweep, beta, field_ref, alpha_ref, state_ref, search_ref, update_ref
    )
    rough = [got[2 * blocks + j * devices : 2 * blocks + (j + 1) * devices].T for j in range(2)]
    field = (unstacked(got[: 2 * blocks]) + jnp.concatenate(rough, axis=1)) / beta - beta * direction
    field_out[...] = field
    send_field(send_ref, field, gather_ref)
    state_out[...] = state
    search_out[...] = search
    update_out[...] = update


def last_kernel(norms_ref, data_ref, field_ref, alpha_ref, state_ref, search_ref, update_ref, update_out, data_out):
    beta = jnp.sqrt(jnp.sum(norms_ref[...], axis=0, keepdims=True)[:, 0:1])
    update_out[...] = advance(ITERS - 1, beta, field_ref, alpha_ref, state_ref, search_ref, update_ref)[2]
    data_out[...] = data_ref[...] / beta


def call(kernel, name, outputs, scratch, operands, flops=0, space=pltpu.VMEM):
    bytes_accessed = sum(x.size * x.dtype.itemsize for x in operands)
    return pl.pallas_call(
        kernel,
        name=name,
        out_shape=[jax.ShapeDtypeStruct(shape, dtype) for shape, dtype in outputs],
        in_specs=[pl.BlockSpec(memory_space=space)] * len(operands),
        out_specs=[pl.BlockSpec(memory_space=pltpu.VMEM)] * len(outputs),
        scratch_shapes=scratch,
        compiler_params=pltpu.CompilerParams(vmem_limit_bytes=40 << 20),
        cost_estimate=pl.CostEstimate(flops=flops, bytes_accessed=bytes_accessed, transcendentals=0),
    )(*operands)


def exchange(packed, devices):
    rows, lanes = packed.shape
    chunks = packed.reshape(devices, rows // devices, lanes)
    return lax.all_to_all(chunks, AXES, split_axis=0, concat_axis=0, tiled=True).reshape(rows, lanes)


def body(kernel, target_device, target_block, counts, traveltimes, prior_residual):
    rads = lax.axis_size("rad")
    devices = lax.axis_size("lat") * rads
    ray_blocks, fanout, ray_len, cells = kernel.shape
    entries = ray_blocks * fanout
    rows = devices * CHUNK
    blocks = MB_R * MB_L
    flops = 4 * entries * ray_len * cells

    packet = ((rows, LANES), BF16)
    ray = ((ray_blocks, ray_len), F32)
    model = ((blocks, cells), F32)
    scalar = ((8, LANES), F32)
    partials = pltpu.VMEM((entries, cells), F32)

    def picks(named):
        return ((2 * named + 2 * devices + 16, rows), BF16)

    def places(named):
        return ((rows, 2 * named + 2 * devices), BF16)

    send, tiles, weights, data, pick, place = call(
        start_kernel, "start",
        [packet, ((entries * ray_len, cells), BF16), ray, ray, picks(entries), places(entries)],
        [
            pltpu.VMEM((fanout, ray_blocks), jnp.int32), pltpu.VMEM((fanout, ray_blocks), jnp.int32),
            pltpu.VMEM((1, ray_blocks), jnp.int32), pltpu.VMEM((ray_blocks, ray_len), F32),
            pltpu.VMEM((ray_blocks, ray_len), F32), partials,
            pltpu.SemaphoreType.DMA((5,)), pltpu.SemaphoreType.DMA((PARTS,)),
        ],
        (kernel.reshape(entries * ray_len, cells), target_device.T, target_block.T,
         counts.reshape(1, ray_blocks), traveltimes, prior_residual),
        flops, pltpu.HBM,
    )
    received = exchange(send, devices)
    send, field, state, gather, scatter = call(
        first_model_kernel, "first_model", [packet, model, scalar, places(blocks), picks(blocks)], [], (received,),
    )
    carried, pens = (), ()
    for sweep in range(ITERS):
        received = exchange(send, devices)
        if sweep == ITERS - 1:
            break
        send, data, pen, alpha = call(
            functools.partial(ray_kernel, sweep, rads), "ray",
            [packet, ray, ((2 * devices, blocks), F32), scalar], [partials],
            (received, tiles, pick, place, weights, data, state) + pens, flops,
        )
        pens = (pen,)
        received = exchange(send, devices)
        send, field, state, *carried = call(
            functools.partial(model_kernel, sweep), "model", [packet, model, scalar, model, model], [],
            (received, scatter, gather, field, alpha, state, *carried), flops,
        )
    send, data, alpha = call(
        functools.partial(last_ray_kernel, ITERS - 1, rads), "last_ray", [((devices, LANES), F32), ray, scalar], [],
        (received, tiles, pick, weights, data, state) + pens, flops,
    )
    norms = exchange(send, devices)
    update, data = call(last_kernel, "last", [model, ray], [], (norms, data, field, alpha, state, *carried))
    return (update.reshape(MB_R, MB_L, cells), data)


def solution(mesh):
    in_specs = (
        P(("lat", "rad"), None, None, None),
        P(("lat", "rad"), None),
        P(("lat", "rad"), None),
        P(("lat", "rad")),
        P(("lat", "rad"), None),
        P(("lat", "rad"), None),
    )
    out_specs = (P("rad", "lat", None), P(("lat", "rad"), None))
    return jax.shard_map(body, mesh=mesh, in_specs=in_specs, out_specs=out_specs, check_vma=False)
```

```python
import functools

import jax
import jax.numpy as jnp
from jax import lax
from jax.experimental import pallas as pl
from jax.experimental.pallas import tpu as pltpu
from jax.sharding import PartitionSpec as P

ITERS = 3
MB_R = 8
MB_L = 16
FREEDOM = 4.0
DAMPING = 0.3

AXES = ("lat", "rad")
CHUNK = 8
NORM_ROW = 4
ID_ROW = 5
CELL_ROW = 6
LANES = 128
PARTS = 4

F32 = jnp.float32
BF16 = jnp.bfloat16
NT = (((1,), (1,)), ((), ()))


def iota(shape, dim):
    return lax.broadcasted_iota(jnp.int32, shape, dim)


def matmul(a, b):
    return jnp.dot(a, b, preferred_element_type=F32)


def total(x):
    return jnp.sum(jnp.sum(x, axis=1, keepdims=True), axis=0, keepdims=True)


def norm_row(partial):
    high = partial.astype(BF16).astype(F32)
    middle = (partial - high).astype(BF16).astype(F32)
    low = partial - high - middle
    lane = iota((1, LANES), 1)
    return jnp.where(lane == 0, high, jnp.where(lane == 1, middle, jnp.where(lane == 2, low, 0.0)))


def with_norm(packed, partial):
    rows = iota(packed.shape, 0) % CHUNK
    return jnp.where(rows == NORM_ROW, norm_row(partial), packed).astype(BF16)


def norm_of(sums):
    lane = iota((1, LANES), 1)
    return jnp.sqrt(jnp.sum(jnp.where(lane < 3, sums[0:1, :], 0.0), axis=1, keepdims=True))


def ones_where(condition):
    return jnp.where(condition, 1.0, 0.0).astype(BF16)


def write_cell_picks(ref, start, devices):
    rows = devices * CHUNK
    device, row = iota((devices, rows), 0), iota((devices, rows), 1)
    for j in range(2):
        ref[start + j * devices : start + (j + 1) * devices, :] = ones_where(row == device * CHUNK + CELL_ROW + j)
    ref[start + 2 * devices :, :] = ones_where(iota((16, rows), 1) % CHUNK == NORM_ROW)


def write_cell_places(ref, start, devices):
    rows = devices * CHUNK
    row, device = iota((rows, devices), 0), iota((rows, devices), 1)
    for j in range(2):
        ref[:, start + j * devices : start + (j + 1) * devices] = ones_where(row == device * CHUNK + CELL_ROW + j)


def stacked(x):
    return jnp.concatenate([x[:, :LANES], x[:, LANES:]], axis=0)


def unstacked(x):
    half = x.shape[0] // 2
    return jnp.concatenate([x[:half], x[half:]], axis=1)


def adjoint_products(kernel_ref, y, out_ref, ray_blocks, fanout, ready=None):
    high = y.astype(BF16).astype(F32)
    low = y - high
    high = jnp.concatenate([high] * fanout, axis=1)
    low = jnp.concatenate([low] * fanout, axis=1)
    width = high.shape[1]
    ray_len = width // fanout
    row, lane = iota((2 * fanout, width), 0), iota((2 * fanout, width), 1)
    own = lane // ray_len == row % fanout
    for b in range(ray_blocks):
        if ready is not None:
            ready(b)
        lhs = jnp.where(row < fanout, high[b : b + 1], low[b : b + 1])
        lhs = jnp.where(own, lhs, 0.0).astype(BF16)
        both = matmul(lhs, kernel_ref[b * width : (b + 1) * width, :])
        out_ref[b * fanout : (b + 1) * fanout, :] = both[:fanout] + both[fanout:]


def forward_products(kernel_ref, blocks, ray_blocks, fanout, ray_len):
    entries = ray_blocks * fanout
    lane = iota((ray_len, entries), 1)
    picked = jnp.zeros((ray_len, entries), F32)
    group = 16
    for start in range(0, entries, group):
        products = lax.dot_general(
            kernel_ref[start * ray_len : (start + group) * ray_len, :], blocks, NT, preferred_element_type=F32
        )
        for i in range(group):
            picked = jnp.where(lane == start + i, products[i * ray_len : (i + 1) * ray_len], picked)
    member = jnp.where(iota((ray_blocks, entries), 1) // fanout == iota((ray_blocks, entries), 0), 1.0, 0.0)
    return lax.dot_general(member, picked, NT, preferred_element_type=F32, precision=lax.Precision.HIGHEST)


def roughen(cell, rads):
    shape = cell.shape
    devices, blocks = shape
    device, block = iota(shape, 0), iota(shape, 1)
    rad, place = device % rads, block % MB_L
    lanes = lambda x, step: pltpu.roll(x, step % blocks, 1)
    owner = lambda x, step: pltpu.roll(x, step % devices, 0)
    up = lanes(cell, MB_L)
    north = jnp.where(block >= MB_L, up, jnp.where(rad > 0, owner(up, 1), 0.0))
    down = lanes(cell, -MB_L)
    south = jnp.where(block < blocks - MB_L, down, jnp.where(rad < rads - 1, owner(down, -1), 0.0))
    far = owner(lanes(cell, 1 - MB_L), rads)
    west = jnp.where(place > 0, lanes(cell, 1), jnp.where(device >= rads, far, 0.0))
    far = owner(lanes(cell, MB_L - 1), -rads)
    east = jnp.where(place < MB_L - 1, lanes(cell, -1), jnp.where(device < devices - rads, far, 0.0))
    return 4.0 * cell - (south + north + east + west)


def scalars_row(*values):
    lane = iota((8, LANES), 1)
    out = jnp.zeros((8, LANES), F32)
    for i, value in enumerate(values):
        out = jnp.where(lane == i, value, out)
    return out


def start_kernel(
    kernel_hbm, device_hbm, block_hbm, counts_hbm, times_hbm, prior_hbm,
    send_ref, tiles_ref, weights_ref, data_ref, pick_ref, place_ref,
    device_ref, block_ref, counts_ref, times_ref, prior_ref, partial_ref, small_sem, tile_sem,
):
    fanout, ray_blocks = device_ref.shape
    ray_len = times_ref.shape[1]
    entries = ray_blocks * fanout
    rows = send_ref.shape[0]
    devices = rows // CHUNK
    part = tiles_ref.shape[0] // PARTS

    small = [
        pltpu.make_async_copy(source, target, small_sem.at[i])
        for i, (source, target) in enumerate(
            ((device_hbm, device_ref), (block_hbm, block_ref), (counts_hbm, counts_ref),
             (times_hbm, times_ref), (prior_hbm, prior_ref))
        )
    ]
    large = [
        pltpu.make_async_copy(
            kernel_hbm.at[pl.ds(i * part, part), :], tiles_ref.at[pl.ds(i * part, part), :], tile_sem.at[i]
        )
        for i in range(PARTS)
    ]
    for copy in small + large:
        copy.start()
    write_cell_picks(pick_ref, 2 * entries, devices)
    write_cell_places(place_ref, 2 * entries, devices)
    for copy in small:
        copy.wait()

    member = ones_where(iota((entries, ray_blocks), 0) // fanout == iota((entries, ray_blocks), 1))
    turn = iota((entries, fanout), 0) % fanout == iota((entries, fanout), 1)

    def column(table_ref):
        table = table_ref[...].astype(F32).astype(BF16)
        spread = lax.dot_general(member, table, NT, preferred_element_type=F32)
        return jnp.sum(jnp.where(turn, spread, 0.0), axis=1, keepdims=True)

    diagonal = iota((entries, entries), 0) == iota((entries, entries), 1)

    def as_row(col):
        return jnp.sum(jnp.where(diagonal, col, 0.0), axis=0, keepdims=True)

    target = column(device_ref)
    block = column(block_ref)
    target_row = as_row(target)
    earlier = iota((entries, entries), 1) < iota((entries, entries), 0)
    rank = jnp.sum(jnp.where(earlier & (target == target_row), 1.0, 0.0), axis=1, keepdims=True)
    first = target * CHUNK + 2.0 * rank
    first_row = as_row(first)

    to_col = first.astype(jnp.int32)
    to_row = first_row.astype(jnp.int32)
    for half in range(2):
        here = slice(half * entries, (half + 1) * entries)
        pick_ref[here, :] = ones_where(iota((entries, rows), 1) == to_col + half)
        place_ref[:, here] = ones_where(iota((rows, entries), 0) == to_row + half)

    same = iota((ray_blocks, ray_blocks), 0) == iota((ray_blocks, ray_blocks), 1)
    counts = jnp.sum(jnp.where(same, counts_ref[...].astype(F32), 0.0), axis=1, keepdims=True)
    mask = jnp.where(iota((ray_blocks, ray_len), 1).astype(F32) < counts, 1.0, 0.0)
    prior = prior_ref[...]
    weights = mask * jnp.sqrt((FREEDOM + 1.0) / (FREEDOM + prior * prior))
    weights_ref[...] = weights
    data = weights * times_ref[...]
    data_ref[...] = data

    def ready(b):
        if b % (ray_blocks // PARTS) == 0:
            large[b // (ray_blocks // PARTS)].wait()

    adjoint_products(tiles_ref, weights * data, partial_ref, ray_blocks, fanout, ready)
    ids = jnp.where(iota((entries, LANES), 1).astype(F32) == rank, block + 1.0, 0.0).astype(BF16)
    id_rows = (target_row * CHUNK + ID_ROW).astype(jnp.int32)
    id_place = ones_where(iota((rows, entries), 0) == id_rows)
    packed = matmul(place_ref[:, : 2 * entries], stacked(partial_ref[...].astype(BF16))) + matmul(id_place, ids)
    send_ref[...] = with_norm(packed, total(data * data))


def send_field(send_ref, gathered, field, gather_ref):
    cells = [gathered[:, half * LANES : (half + 1) * LANES].T for half in range(2)]
    packed = jnp.concatenate([stacked(field)] + cells, axis=0).astype(BF16)
    send_ref[...] = with_norm(matmul(gather_ref[...], packed), total(field * field))


def first_model_kernel(received_ref, send_ref, field_ref, state_ref, gather_ref, scatter_ref):
    received = received_ref[...]
    rows = received.shape[0]
    devices = rows // CHUNK
    blocks = MB_R * MB_L
    pick = ones_where(iota((devices, rows), 1) == iota((devices, rows), 0) * CHUNK + ID_ROW)
    ids = matmul(pick, received).astype(BF16)
    owner = ones_where(iota((rows, devices), 0) // CHUNK == iota((rows, devices), 1))
    spread = matmul(owner, ids)
    place = iota((rows, LANES), 0) % CHUNK
    lane = iota((rows, LANES), 1)
    slot = (place < NORM_ROW) & (lane == place // 2)
    ident = jnp.sum(jnp.where(slot, spread, 0.0), axis=1, keepdims=True) - 1.0
    hit = ident == lane.astype(F32)
    for half in range(2):
        here = slice(half * blocks, (half + 1) * blocks)
        chosen = jnp.where(hit & (place % 2 == half), 1.0, 0.0)
        gather_ref[:, here] = chosen.astype(BF16)
        scatter_ref[here, :] = chosen.T.astype(BF16)
    write_cell_picks(scatter_ref, 2 * blocks, devices)
    write_cell_places(gather_ref, 2 * blocks, devices)

    got = matmul(scatter_ref[...], received)
    beta = norm_of(got[2 * blocks + 2 * devices :])
    gathered = unstacked(got[: 2 * blocks]).astype(BF16).astype(F32)
    field = gathered / beta
    field_ref[...] = field
    state_ref[...] = scalars_row(beta)
    send_field(send_ref, gathered, field, gather_ref)


def ray_step(sweep, rads, received_ref, kernel_ref, pick_ref, weights_ref, data_ref, state_ref, cells_ref):
    received = received_ref[...]
    ray_blocks, ray_len = data_ref.shape
    devices = received.shape[0] // CHUNK
    got = matmul(pick_ref[...], received)
    entries = (got.shape[0] - 2 * devices - 16) // 2
    fanout = entries // ray_blocks
    alpha = norm_of(got[2 * entries + 2 * devices :])
    blocks = unstacked(got[: 2 * entries]).astype(BF16)
    products = forward_products(kernel_ref, blocks, ray_blocks, fanout, ray_len)
    beta = state_ref[0:1, 0:1]
    data = weights_ref[...] * (products / alpha) - alpha * (data_ref[...] / beta)
    partial = total(data * data)
    pens, directions = [], []
    for j in range(2):
        cell = got[2 * entries + j * devices : 2 * entries + (j + 1) * devices]
        if sweep:
            rough, before, pen = [cells_ref[i, j * devices : (j + 1) * devices] for i in range(3)]
            direction = ((cell + rough) / beta - beta * before) / alpha
            pen = DAMPING * roughen(direction, rads) - alpha * (pen / beta)
        else:
            direction = cell / (beta * alpha)
            pen = DAMPING * roughen(direction, rads)
        partial = partial + total(pen * pen)
        pens.append(pen)
        directions.append(direction)
    return alpha, data, pens, directions, partial


def ray_kernel(sweep, rads, *refs):
    received_ref, kernel_ref, pick_ref, place_ref, weights_ref, data_ref, state_ref = refs[:7]
    cells_ref = refs[7] if sweep else None
    send_ref, data_out, cells_out, alpha_out, partial_ref = refs[-5:]
    alpha, data, pens, directions, partial = ray_step(
        sweep, rads, received_ref, kernel_ref, pick_ref, weights_ref, data_ref, state_ref, cells_ref
    )
    data_out[...] = data
    alpha_out[...] = scalars_row(alpha)
    ray_blocks = data.shape[0]
    fanout = partial_ref.shape[0] // ray_blocks
    adjoint_products(kernel_ref, weights_ref[...] * data, partial_ref, ray_blocks, fanout)
    rough = [DAMPING * roughen(pen, rads) for pen in pens]
    for i, kept in enumerate((rough, directions, pens)):
        cells_out[i] = jnp.concatenate(kept, axis=0)
    packed = jnp.concatenate([stacked(partial_ref[...])] + rough, axis=0).astype(BF16)
    send_ref[...] = with_norm(matmul(place_ref[...], packed), partial)


def last_ray_kernel(sweep, rads, *refs):
    send_ref, data_out, alpha_out = refs[-3:]
    alpha, data, _, _, partial = ray_step(sweep, rads, *refs[:-3])
    data_out[...] = data
    alpha_out[...] = scalars_row(alpha)
    send_ref[...] = jnp.broadcast_to(partial, send_ref.shape)


def advance(sweep, beta, field_ref, alpha_ref, state_ref, search_ref, update_ref):
    alpha = alpha_ref[0:1, 0:1]
    direction = field_ref[...] / alpha
    if sweep:
        phi_bar, rho, cosine, sine = [state_ref[0:1, i : i + 1] for i in range(1, 5)]
        search = direction - (sine * alpha / rho) * search_ref[...]
        rho_bar = -cosine * alpha
    else:
        phi_bar, rho_bar = state_ref[0:1, 0:1], alpha
        search = direction
    rho = jnp.sqrt(rho_bar * rho_bar + beta * beta)
    cosine, sine = rho_bar / rho, beta / rho
    update = (cosine * phi_bar / rho) * search
    if sweep:
        update = update_ref[...] + update
    return direction, search, update, scalars_row(beta, sine * phi_bar, rho, cosine, sine)


def model_kernel(sweep, *refs):
    received_ref, scatter_ref, gather_ref, field_ref, alpha_ref, state_ref = refs[:6]
    search_ref, update_ref = refs[6:8] if sweep else (None, None)
    send_ref, field_out, state_out, search_out, update_out = refs[-5:]
    received = received_ref[...]
    devices = received.shape[0] // CHUNK
    got = matmul(scatter_ref[...], received)
    blocks = field_ref.shape[0]
    beta = norm_of(got[2 * blocks + 2 * devices :])
    direction, search, update, state = advance(
        sweep, beta, field_ref, alpha_ref, state_ref, search_ref, update_ref
    )
    rough = [got[2 * blocks + j * devices : 2 * blocks + (j + 1) * devices].T for j in range(2)]
    gathered = unstacked(got[: 2 * blocks]).astype(BF16).astype(F32)
    field = (gathered + jnp.concatenate(rough, axis=1)) / beta - beta * direction
    field_out[...] = field
    send_field(send_ref, gathered, field, gather_ref)
    state_out[...] = state
    search_out[...] = search
    update_out[...] = update


def last_kernel(norms_ref, data_ref, field_ref, alpha_ref, state_ref, search_ref, update_ref, update_out, data_out):
    beta = jnp.sqrt(jnp.sum(norms_ref[...], axis=0, keepdims=True)[:, 0:1])
    update_out[...] = advance(ITERS - 1, beta, field_ref, alpha_ref, state_ref, search_ref, update_ref)[2]
    data_out[...] = data_ref[...] / beta


def call(kernel, name, outputs, scratch, operands, flops=0, space=pltpu.VMEM):
    bytes_accessed = sum(x.size * x.dtype.itemsize for x in operands)
    return pl.pallas_call(
        kernel,
        name=name,
        out_shape=[jax.ShapeDtypeStruct(shape, dtype) for shape, dtype in outputs],
        in_specs=[pl.BlockSpec(memory_space=space)] * len(operands),
        out_specs=[pl.BlockSpec(memory_space=pltpu.VMEM)] * len(outputs),
        scratch_shapes=scratch,
        compiler_params=pltpu.CompilerParams(vmem_limit_bytes=40 << 20),
        cost_estimate=pl.CostEstimate(flops=flops, bytes_accessed=bytes_accessed, transcendentals=0),
    )(*operands)


def exchange(packed, devices):
    rows, lanes = packed.shape
    chunks = packed.reshape(devices, rows // devices, lanes)
    return lax.all_to_all(chunks, AXES, split_axis=0, concat_axis=0, tiled=True).reshape(rows, lanes)


def body(kernel, target_device, target_block, counts, traveltimes, prior_residual):
    rads = lax.axis_size("rad")
    devices = lax.axis_size("lat") * rads
    ray_blocks, fanout, ray_len, cells = kernel.shape
    entries = ray_blocks * fanout
    rows = devices * CHUNK
    blocks = MB_R * MB_L
    flops = 4 * entries * ray_len * cells

    packet = ((rows, LANES), BF16)
    ray = ((ray_blocks, ray_len), F32)
    model = ((blocks, cells), F32)
    scalar = ((8, LANES), F32)
    partials = pltpu.VMEM((entries, cells), F32)

    def picks(named):
        return ((2 * named + 2 * devices + 16, rows), BF16)

    def places(named):
        return ((rows, 2 * named + 2 * devices), BF16)

    send, tiles, weights, data, pick, place = call(
        start_kernel, "start",
        [packet, ((entries * ray_len, cells), BF16), ray, ray, picks(entries), places(entries)],
        [
            pltpu.VMEM((fanout, ray_blocks), jnp.int32), pltpu.VMEM((fanout, ray_blocks), jnp.int32),
            pltpu.VMEM((1, ray_blocks), jnp.int32), pltpu.VMEM((ray_blocks, ray_len), F32),
            pltpu.VMEM((ray_blocks, ray_len), F32), partials,
            pltpu.SemaphoreType.DMA((5,)), pltpu.SemaphoreType.DMA((PARTS,)),
        ],
        tuple(
            pltpu.with_memory_space_constraint(x, pltpu.HBM)
            for x in (kernel.reshape(entries * ray_len, cells), target_device.T, target_block.T,
                      counts.reshape(1, ray_blocks), traveltimes, prior_residual)
        ),
        flops, pltpu.HBM,
    )
    received = exchange(send, devices)
    send, field, state, gather, scatter = call(
        first_model_kernel, "first_model", [packet, model, scalar, places(blocks), picks(blocks)], [], (received,),
    )
    carried, kept = (), ()
    for sweep in range(ITERS):
        received = exchange(send, devices)
        if sweep == ITERS - 1:
            break
        send, data, cell_state, alpha = call(
            functools.partial(ray_kernel, sweep, rads), "ray",
            [packet, ray, ((3, 2 * devices, blocks), F32), scalar], [partials],
            (received, tiles, pick, place, weights, data, state) + kept, flops,
        )
        kept = (cell_state,)
        received = exchange(send, devices)
        send, field, state, *carried = call(
            functools.partial(model_kernel, sweep), "model", [packet, model, scalar, model, model], [],
            (received, scatter, gather, field, alpha, state, *carried), flops,
        )
    send, data, alpha = call(
        functools.partial(last_ray_kernel, ITERS - 1, rads), "last_ray", [((devices, LANES), F32), ray, scalar], [],
        (received, tiles, pick, weights, data, state) + kept, flops,
    )
    norms = exchange(send, devices)
    update, data = call(last_kernel, "last", [model, ray], [], (norms, data, field, alpha, state, *carried))
    return (update.reshape(MB_R, MB_L, cells), data)


def solution(mesh):
    in_specs = (
        P(("lat", "rad"), None, None, None),
        P(("lat", "rad"), None),
        P(("lat", "rad"), None),
        P(("lat", "rad")),
        P(("lat", "rad"), None),
        P(("lat", "rad"), None),
    )
    out_specs = (P("rad", "lat", None), P(("lat", "rad"), None))
    return jax.shard_map(body, mesh=mesh, in_specs=in_specs, out_specs=out_specs, check_vma=False)
```

```python
import functools

import jax
import jax.numpy as jnp
from jax import lax
from jax.experimental import pallas as pl
from jax.experimental.pallas import tpu as pltpu
from jax.sharding import PartitionSpec as P

ITERS = 3
MB_R = 8
MB_L = 16
FREEDOM = 4.0
DAMPING = 0.3

AXES = ("lat", "rad")
CHUNK = 8
NORM_ROW = 4
ID_ROW = 5
CELL_ROW = 6
LANES = 128
PARTS = 4

F32 = jnp.float32
BF16 = jnp.bfloat16
NT = (((1,), (1,)), ((), ()))


def iota(shape, dim):
    return lax.broadcasted_iota(jnp.int32, shape, dim)


def matmul(a, b):
    return jnp.dot(a, b, preferred_element_type=F32)


def total(x):
    return jnp.sum(jnp.sum(x, axis=1, keepdims=True), axis=0, keepdims=True)


def ones_where(condition):
    return jnp.where(condition, 1.0, 0.0).astype(BF16)


def norm_row(partial, rest):
    high = partial.astype(BF16).astype(F32)
    lane = iota(rest.shape, 1)
    return jnp.where(lane == 0, high, jnp.where(lane == 1, partial - high, rest))


def norm_of(sums):
    sums = jnp.where(iota(sums.shape, 1) < 2, sums, 0.0)
    return jnp.sqrt(total(sums))


def row_of(ref, j):
    return ref.at[pl.ds(j, ref.shape[0] // CHUNK, stride=CHUNK), :]


def pack(send_ref, stage_ref, named, *rest):
    for j, rows in enumerate(rest):
        row_of(stage_ref, NORM_ROW + j)[...] = rows
    data = iota(named.shape, 0) % CHUNK < NORM_ROW
    send_ref[...] = jnp.where(data, named, stage_ref[...]).astype(BF16)


def stacked(x):
    return jnp.concatenate([x[:, :LANES], x[:, LANES:]], axis=0)


def unstacked(x):
    half = x.shape[0] // 2
    return jnp.concatenate([x[:half], x[half:]], axis=1)


def adjoint_products(kernel_ref, y, out_ref, ray_blocks, fanout, ready=None):
    high = y.astype(BF16).astype(F32)
    low = y - high
    high = jnp.concatenate([high] * fanout, axis=1)
    low = jnp.concatenate([low] * fanout, axis=1)
    width = high.shape[1]
    ray_len = width // fanout
    row, lane = iota((2 * fanout, width), 0), iota((2 * fanout, width), 1)
    own = lane // ray_len == row % fanout
    for b in range(ray_blocks):
        if ready is not None:
            ready(b)
        lhs = jnp.where(row < fanout, high[b : b + 1], low[b : b + 1])
        lhs = jnp.where(own, lhs, 0.0).astype(BF16)
        both = matmul(lhs, kernel_ref[b * width : (b + 1) * width, :])
        out_ref[b * fanout : (b + 1) * fanout, :] = both[:fanout] + both[fanout:]


def forward_products(kernel_ref, blocks, ray_blocks, fanout, ray_len):
    entries = ray_blocks * fanout
    lane = iota((ray_len, entries), 1)
    picked = jnp.zeros((ray_len, entries), F32)
    group = 16
    for start in range(0, entries, group):
        products = lax.dot_general(
            kernel_ref[start * ray_len : (start + group) * ray_len, :], blocks, NT, preferred_element_type=F32
        )
        for i in range(group):
            picked = jnp.where(lane == start + i, products[i * ray_len : (i + 1) * ray_len], picked)
    member = jnp.where(iota((ray_blocks, entries), 1) // fanout == iota((ray_blocks, entries), 0), 1.0, 0.0)
    return lax.dot_general(member, picked, NT, preferred_element_type=F32, precision=lax.Precision.HIGHEST)


def roughen(cell, rads):
    shape = cell.shape
    devices, blocks = shape
    device, block = iota(shape, 0), iota(shape, 1)
    rad, place = device % rads, block % MB_L
    lanes = lambda x, step: pltpu.roll(x, step % blocks, 1)
    owner = lambda x, step: pltpu.roll(x, step % devices, 0)
    up = lanes(cell, MB_L)
    north = jnp.where(block >= MB_L, up, jnp.where(rad > 0, owner(up, 1), 0.0))
    down = lanes(cell, -MB_L)
    south = jnp.where(block < blocks - MB_L, down, jnp.where(rad < rads - 1, owner(down, -1), 0.0))
    far = owner(lanes(cell, 1 - MB_L), rads)
    west = jnp.where(place > 0, lanes(cell, 1), jnp.where(device >= rads, far, 0.0))
    far = owner(lanes(cell, MB_L - 1), -rads)
    east = jnp.where(place < MB_L - 1, lanes(cell, -1), jnp.where(device < devices - rads, far, 0.0))
    return 4.0 * cell - (south + north + east + west)


def scalars_row(*values):
    lane = iota((8, LANES), 1)
    out = jnp.zeros((8, LANES), F32)
    for i, value in enumerate(values):
        out = jnp.where(lane == i, value, out)
    return out


def start_kernel(
    kernel_hbm, device_hbm, block_hbm, counts_hbm, times_hbm, prior_hbm,
    send_ref, tiles_ref, weights_ref, data_ref, place_ref, pick_ref,
    device_ref, block_ref, counts_ref, times_ref, prior_ref, partial_ref, stage_ref, small_sem, tile_sem,
):
    fanout, ray_blocks = device_ref.shape
    ray_len = times_ref.shape[1]
    entries = ray_blocks * fanout
    rows = send_ref.shape[0]
    devices = rows // CHUNK
    part = tiles_ref.shape[0] // PARTS

    small = [
        pltpu.make_async_copy(source, target, small_sem.at[i])
        for i, (source, target) in enumerate(
            ((device_hbm, device_ref), (block_hbm, block_ref), (counts_hbm, counts_ref),
             (times_hbm, times_ref), (prior_hbm, prior_ref))
        )
    ]
    large = [
        pltpu.make_async_copy(
            kernel_hbm.at[pl.ds(i * part, part), :], tiles_ref.at[pl.ds(i * part, part), :], tile_sem.at[i]
        )
        for i in range(PARTS)
    ]
    for copy in small + large:
        copy.start()
    for copy in small:
        copy.wait()

    member = ones_where(iota((entries, ray_blocks), 0) // fanout == iota((entries, ray_blocks), 1))
    turn = iota((entries, fanout), 0) % fanout == iota((entries, fanout), 1)

    def column(table_ref):
        table = table_ref[...].astype(F32).astype(BF16)
        spread = lax.dot_general(member, table, NT, preferred_element_type=F32)
        return jnp.sum(jnp.where(turn, spread, 0.0), axis=1, keepdims=True)

    diagonal = iota((entries, entries), 0) == iota((entries, entries), 1)

    def as_row(col):
        return jnp.sum(jnp.where(diagonal, col, 0.0), axis=0, keepdims=True)

    target = column(device_ref)
    block = column(block_ref)
    target_row = as_row(target)
    earlier = iota((entries, entries), 1) < iota((entries, entries), 0)
    rank = jnp.sum(jnp.where(earlier & (target == target_row), 1.0, 0.0), axis=1, keepdims=True)
    first = target * CHUNK + 2.0 * rank
    to_col = first.astype(jnp.int32)
    to_row = as_row(first).astype(jnp.int32)
    for half in range(2):
        here = slice(half * entries, (half + 1) * entries)
        pick_ref[here, :] = ones_where(iota((entries, rows), 1) == to_col + half)
        place_ref[:, here] = ones_where(iota((rows, entries), 0) == to_row + half)

    same = iota((ray_blocks, ray_blocks), 0) == iota((ray_blocks, ray_blocks), 1)
    counts = jnp.sum(jnp.where(same, counts_ref[...].astype(F32), 0.0), axis=1, keepdims=True)
    mask = jnp.where(iota((ray_blocks, ray_len), 1).astype(F32) < counts, 1.0, 0.0)
    prior = prior_ref[...]
    weights = mask * jnp.sqrt((FREEDOM + 1.0) / (FREEDOM + prior * prior))
    weights_ref[...] = weights
    data = weights * times_ref[...]
    data_ref[...] = data

    def ready(b):
        if b % (ray_blocks // PARTS) == 0:
            large[b // (ray_blocks // PARTS)].wait()

    adjoint_products(tiles_ref, weights * data, partial_ref, ray_blocks, fanout, ready)
    ids = jnp.where(iota((entries, LANES), 1).astype(F32) == rank, block + 1.0, 0.0).astype(BF16)
    named_by = ones_where(iota((devices, entries), 0).astype(F32) == target_row)
    zeros = jnp.zeros((devices, LANES), F32)
    pack(
        send_ref, stage_ref, matmul(place_ref[...], stacked(partial_ref[...].astype(BF16))),
        norm_row(total(data * data), zeros), matmul(named_by, ids), zeros, zeros,
    )


def send_field(send_ref, stage_ref, gathered, field, gather_ref):
    cells = [gathered[:, half * LANES : (half + 1) * LANES].T for half in range(2)]
    zeros = jnp.zeros(cells[0].shape, F32)
    norms = norm_row(total(field * field), zeros)
    pack(send_ref, stage_ref, matmul(gather_ref[...], stacked(field).astype(BF16)), norms, zeros, *cells)


def first_model_kernel(received_ref, send_ref, field_ref, state_ref, gather_ref, scatter_ref, stage_ref):
    received = received_ref[...]
    rows = received.shape[0]
    blocks = MB_R * MB_L
    stage_ref[...] = received.astype(F32)
    beta = norm_of(row_of(stage_ref, NORM_ROW)[...])
    ids = row_of(stage_ref, ID_ROW)[...]
    for j in range(CHUNK):
        ident = ids[:, j // 2 : j // 2 + 1] if j < NORM_ROW else 0.0
        row_of(stage_ref, j)[...] = jnp.broadcast_to(ident, ids.shape)
    hit = stage_ref[...] - 1.0 == iota((rows, LANES), 1).astype(F32)
    odd = iota((rows, LANES), 0) % 2
    for half in range(2):
        here = slice(half * blocks, (half + 1) * blocks)
        chosen = jnp.where(hit & (odd == half), 1.0, 0.0)
        gather_ref[:, here] = chosen.astype(BF16)
        scatter_ref[here, :] = chosen.T.astype(BF16)

    gathered = unstacked(matmul(scatter_ref[...], received)).astype(BF16).astype(F32)
    field = gathered / beta
    field_ref[...] = field
    state_ref[...] = scalars_row(beta)
    send_field(send_ref, stage_ref, gathered, field, gather_ref)


def ray_step(
    sweep, rads, received_ref, tiles_ref, pick_ref, weights_ref, data_ref, state_ref, cells_ref, stage_ref,
):
    received = received_ref[...]
    ray_blocks, ray_len = data_ref.shape
    devices = received.shape[0] // CHUNK
    fanout = pick_ref.shape[0] // 2 // ray_blocks
    blocks = unstacked(matmul(pick_ref[...], received)).astype(BF16)
    stage_ref[...] = received.astype(F32)
    alpha = norm_of(row_of(stage_ref, NORM_ROW)[...])
    products = forward_products(tiles_ref, blocks, ray_blocks, fanout, ray_len)
    beta = state_ref[0:1, 0:1]
    data = weights_ref[...] * (products / alpha) - alpha * (data_ref[...] / beta)
    partial = total(data * data)
    pens, directions = [], []
    for j in range(2):
        cell = row_of(stage_ref, CELL_ROW + j)[...]
        if sweep:
            rough, before, pen = [cells_ref[i, j * devices : (j + 1) * devices] for i in range(3)]
            direction = ((cell + rough) / beta - beta * before) / alpha
            pen = DAMPING * roughen(direction, rads) - alpha * (pen / beta)
        else:
            direction = cell / (beta * alpha)
            pen = DAMPING * roughen(direction, rads)
        partial = partial + total(pen * pen)
        pens.append(pen)
        directions.append(direction)
    return alpha, data, pens, directions, partial


def ray_kernel(sweep, rads, *refs):
    received_ref, tiles_ref, pick_ref, weights_ref, data_ref, state_ref, place_ref = refs[:7]
    cells_ref = refs[7] if sweep else None
    send_ref, data_out, cells_out, alpha_out, stage_ref, partial_ref = refs[-6:]
    alpha, data, pens, directions, partial = ray_step(
        sweep, rads, received_ref, tiles_ref, pick_ref, weights_ref, data_ref, state_ref, cells_ref, stage_ref
    )
    data_out[...] = data
    alpha_out[...] = scalars_row(alpha)
    ray_blocks = data.shape[0]
    fanout = partial_ref.shape[0] // ray_blocks
    adjoint_products(tiles_ref, weights_ref[...] * data, partial_ref, ray_blocks, fanout)
    rough = [DAMPING * roughen(pen, rads) for pen in pens]
    for i, kept in enumerate((rough, directions, pens)):
        cells_out[i] = jnp.concatenate(kept, axis=0)
    high = [x.astype(BF16).astype(F32) for x in rough]
    low = [x - y for x, y in zip(rough, high)]
    pack(
        send_ref, stage_ref, matmul(place_ref[...], stacked(partial_ref[...]).astype(BF16)),
        norm_row(partial, low[1]), low[0], *high,
    )


def last_ray_kernel(sweep, rads, *refs):
    send_ref, data_out, alpha_out, stage_ref = refs[-4:]
    alpha, data, _, _, partial = ray_step(sweep, rads, *refs[:-4], stage_ref)
    data_out[...] = data
    alpha_out[...] = scalars_row(alpha)
    send_ref[...] = jnp.broadcast_to(partial, send_ref.shape)


def advance(sweep, beta, field_ref, alpha_ref, state_ref, search_ref, update_ref):
    alpha = alpha_ref[0:1, 0:1]
    direction = field_ref[...] / alpha
    if sweep:
        phi_bar, rho, cosine, sine = [state_ref[0:1, i : i + 1] for i in range(1, 5)]
        search = direction - (sine * alpha / rho) * search_ref[...]
        rho_bar = -cosine * alpha
    else:
        phi_bar, rho_bar = state_ref[0:1, 0:1], alpha
        search = direction
    rho = jnp.sqrt(rho_bar * rho_bar + beta * beta)
    cosine, sine = rho_bar / rho, beta / rho
    update = (cosine * phi_bar / rho) * search
    if sweep:
        update = update_ref[...] + update
    return direction, search, update, scalars_row(beta, sine * phi_bar, rho, cosine, sine)


def model_kernel(sweep, *refs):
    received_ref, scatter_ref, gather_ref, field_ref, alpha_ref, state_ref = refs[:6]
    search_ref, update_ref = refs[6:8] if sweep else (None, None)
    send_ref, field_out, state_out, search_out, update_out, stage_ref = refs[-6:]
    received = received_ref[...]
    gathered = unstacked(matmul(scatter_ref[...], received)).astype(BF16).astype(F32)
    stage_ref[...] = received.astype(F32)
    first = row_of(stage_ref, NORM_ROW)[...]
    beta = norm_of(first)
    low = [row_of(stage_ref, ID_ROW)[...], jnp.where(iota(first.shape, 1) < 2, 0.0, first)]
    rough = [(row_of(stage_ref, CELL_ROW + j)[...] + low[j]).T for j in range(2)]
    direction, search, update, state = advance(
        sweep, beta, field_ref, alpha_ref, state_ref, search_ref, update_ref
    )
    field = (gathered + jnp.concatenate(rough, axis=1)) / beta - beta * direction
    field_out[...] = field
    send_field(send_ref, stage_ref, gathered, field, gather_ref)
    state_out[...] = state
    search_out[...] = search
    update_out[...] = update


def last_kernel(norms_ref, data_ref, field_ref, alpha_ref, state_ref, search_ref, update_ref, update_out, data_out):
    beta = jnp.sqrt(jnp.sum(norms_ref[...], axis=0, keepdims=True)[:, 0:1])
    update_out[...] = advance(ITERS - 1, beta, field_ref, alpha_ref, state_ref, search_ref, update_ref)[2]
    data_out[...] = data_ref[...] / beta


def call(kernel, name, outputs, scratch, operands, flops=0, space=pltpu.VMEM):
    bytes_accessed = sum(x.size * x.dtype.itemsize for x in operands)
    return pl.pallas_call(
        kernel,
        name=name,
        out_shape=[jax.ShapeDtypeStruct(shape, dtype) for shape, dtype in outputs],
        in_specs=[pl.BlockSpec(memory_space=space)] * len(operands),
        out_specs=[pl.BlockSpec(memory_space=pltpu.VMEM)] * len(outputs),
        scratch_shapes=scratch,
        compiler_params=pltpu.CompilerParams(vmem_limit_bytes=12 << 20),
        cost_estimate=pl.CostEstimate(flops=flops, bytes_accessed=bytes_accessed, transcendentals=0),
    )(*operands)


def exchange(packed, devices):
    rows, lanes = packed.shape
    chunks = packed.reshape(devices, rows // devices, lanes)
    return lax.all_to_all(chunks, AXES, split_axis=0, concat_axis=0, tiled=True).reshape(rows, lanes)


def body(kernel, target_device, target_block, counts, traveltimes, prior_residual):
    rads = lax.axis_size("rad")
    devices = lax.axis_size("lat") * rads
    ray_blocks, fanout, ray_len, cells = kernel.shape
    entries = ray_blocks * fanout
    rows = devices * CHUNK
    blocks = MB_R * MB_L
    flops = 4 * entries * ray_len * cells

    packet = ((rows, LANES), BF16)
    ray = ((ray_blocks, ray_len), F32)
    model = ((blocks, cells), F32)
    scalar = ((8, LANES), F32)
    partials = pltpu.VMEM((entries, cells), F32)

    stage = pltpu.VMEM((rows, LANES), F32)
    send, tiles, weights, data, place, pick = call(
        start_kernel, "start",
        [packet, ((entries * ray_len, cells), BF16), ray, ray,
         ((rows, 2 * entries), BF16), ((2 * entries, rows), BF16)],
        [
            pltpu.VMEM((fanout, ray_blocks), jnp.int32), pltpu.VMEM((fanout, ray_blocks), jnp.int32),
            pltpu.VMEM((1, ray_blocks), jnp.int32), pltpu.VMEM((ray_blocks, ray_len), F32),
            pltpu.VMEM((ray_blocks, ray_len), F32), partials, stage,
            pltpu.SemaphoreType.DMA((5,)), pltpu.SemaphoreType.DMA((PARTS,)),
        ],
        tuple(
            pltpu.with_memory_space_constraint(x, pltpu.HBM)
            for x in (kernel.reshape(entries * ray_len, cells), target_device.T, target_block.T,
                      counts.reshape(1, ray_blocks), traveltimes, prior_residual)
        ),
        flops, pltpu.HBM,
    )
    received = exchange(send, devices)
    send, field, state, gather, scatter = call(
        first_model_kernel, "first_model",
        [packet, model, scalar, ((rows, 2 * blocks), BF16), ((2 * blocks, rows), BF16)], [stage], (received,),
    )
    carried, kept = (), ()
    for sweep in range(ITERS):
        received = exchange(send, devices)
        if sweep == ITERS - 1:
            break
        send, data, cell_state, alpha = call(
            functools.partial(ray_kernel, sweep, rads), "ray",
            [packet, ray, ((3, 2 * devices, blocks), F32), scalar], [stage, partials],
            (received, tiles, pick, weights, data, state, place) + kept, flops,
        )
        kept = (cell_state,)
        received = exchange(send, devices)
        send, field, state, *carried = call(
            functools.partial(model_kernel, sweep), "model", [packet, model, scalar, model, model], [stage],
            (received, scatter, gather, field, alpha, state, *carried), flops,
        )
    send, data, alpha = call(
        functools.partial(last_ray_kernel, ITERS - 1, rads), "last_ray", [((devices, LANES), F32), ray, scalar],
        [stage], (received, tiles, pick, weights, data, state) + kept, flops,
    )
    norms = exchange(send, devices)
    update, data = call(last_kernel, "last", [model, ray], [], (norms, data, field, alpha, state, *carried))
    return (update.reshape(MB_R, MB_L, cells), data)


def solution(mesh):
    in_specs = (
        P(("lat", "rad"), None, None, None),
        P(("lat", "rad"), None),
        P(("lat", "rad"), None),
        P(("lat", "rad")),
        P(("lat", "rad"), None),
        P(("lat", "rad"), None),
    )
    out_specs = (P("rad", "lat", None), P(("lat", "rad"), None))
    return jax.shard_map(body, mesh=mesh, in_specs=in_specs, out_specs=out_specs, check_vma=False)
```

```python
import functools

import jax
import jax.numpy as jnp
from jax import lax
from jax.experimental import pallas as pl
from jax.experimental.pallas import tpu as pltpu
from jax.sharding import PartitionSpec as P

ITERS = 3
MB_R = 8
MB_L = 16
FREEDOM = 4.0
DAMPING = 0.3

AXES = ("lat", "rad")
CHUNK = 8
NORM_ROW = 4
ID_ROW = 5
CELL_ROW = 6
LANES = 128
GROUP = 8

F32 = jnp.float32
BF16 = jnp.bfloat16
NT = (((1,), (1,)), ((), ()))


def iota(shape, dim):
    return lax.broadcasted_iota(jnp.int32, shape, dim)


def matmul(a, b):
    return jnp.dot(a, b, preferred_element_type=F32)


def total(x):
    return jnp.sum(jnp.sum(x, axis=1, keepdims=True), axis=0, keepdims=True)


def ones_where(condition):
    return jnp.where(condition, 1.0, 0.0).astype(BF16)


def norm_row(partial, rest):
    high = partial.astype(BF16).astype(F32)
    lane = iota(rest.shape, 1)
    return jnp.where(lane == 0, high, jnp.where(lane == 1, partial - high, rest))


def norm_of(sums):
    sums = jnp.where(iota(sums.shape, 1) < 2, sums, 0.0)
    return jnp.sqrt(total(sums))


def row_of(ref, j):
    return ref.at[pl.ds(j, ref.shape[0] // CHUNK, stride=CHUNK), :]


def pack(send_ref, stage_ref, named, *rest):
    for j, rows in enumerate(rest):
        row_of(stage_ref, NORM_ROW + j)[...] = rows
    data = iota(named.shape, 0) % CHUNK < NORM_ROW
    send_ref[...] = jnp.where(data, named, stage_ref[...]).astype(BF16)


def stacked(x):
    return jnp.concatenate([x[:, :LANES], x[:, LANES:]], axis=0)


def unstacked(x):
    half = x.shape[0] // 2
    return jnp.concatenate([x[:half], x[half:]], axis=1)


def forward_group(tiles_ref, blocks_ref, start, count, fanout, ray_len):
    lane = iota((ray_len, LANES), 1)
    sums = jnp.zeros((ray_len, LANES), F32)
    for i in range(count):
        products = None
        for e in range((start + i) * fanout, (start + i + 1) * fanout):
            product = tiles_ref[e * ray_len : (e + 1) * ray_len, :].astype(F32) * blocks_ref[e : e + 1, :]
            product = product[:, :LANES] + product[:, LANES:]
            products = product if products is None else products + product
        sums = jnp.where(lane == i, jnp.sum(products, axis=1, keepdims=True), sums)
    return sums.T[:count]


def adjoint_group(tiles_ref, y, out_ref, start, fanout):
    high = y.astype(BF16).astype(F32)
    low = y - high
    high = jnp.concatenate([high] * fanout, axis=1)
    low = jnp.concatenate([low] * fanout, axis=1)
    count, width = high.shape
    ray_len = width // fanout
    row, lane = iota((2 * fanout, width), 0), iota((2 * fanout, width), 1)
    own = lane // ray_len == row % fanout
    for i in range(count):
        b = start + i
        lhs = jnp.where(row < fanout, high[i : i + 1], low[i : i + 1])
        lhs = jnp.where(own, lhs, 0.0).astype(BF16)
        both = matmul(lhs, tiles_ref[b * width : (b + 1) * width, :])
        out_ref[b * fanout : (b + 1) * fanout, :] = both[:fanout] + both[fanout:]


def roughen(cell, rads):
    shape = cell.shape
    devices, blocks = shape
    device, block = iota(shape, 0), iota(shape, 1)
    rad, place = device % rads, block % MB_L
    lanes = lambda x, step: pltpu.roll(x, step % blocks, 1)
    owner = lambda x, step: pltpu.roll(x, step % devices, 0)
    up = lanes(cell, MB_L)
    north = jnp.where(block >= MB_L, up, jnp.where(rad > 0, owner(up, 1), 0.0))
    down = lanes(cell, -MB_L)
    south = jnp.where(block < blocks - MB_L, down, jnp.where(rad < rads - 1, owner(down, -1), 0.0))
    far = owner(lanes(cell, 1 - MB_L), rads)
    west = jnp.where(place > 0, lanes(cell, 1), jnp.where(device >= rads, far, 0.0))
    far = owner(lanes(cell, MB_L - 1), -rads)
    east = jnp.where(place < MB_L - 1, lanes(cell, -1), jnp.where(device < devices - rads, far, 0.0))
    return 4.0 * cell - (south + north + east + west)


def scalars_row(*values):
    lane = iota((8, LANES), 1)
    out = jnp.zeros((8, LANES), F32)
    for i, value in enumerate(values):
        out = jnp.where(lane == i, value, out)
    return out


def start_kernel(
    kernel_hbm, device_hbm, block_hbm, counts_hbm, times_hbm, prior_hbm,
    send_ref, tiles_ref, weights_ref, data_ref, place_ref, pick_ref,
    device_ref, block_ref, counts_ref, times_ref, prior_ref, partial_ref, stage_ref, small_sem, tile_sem,
):
    fanout, ray_blocks = device_ref.shape
    ray_len = times_ref.shape[1]
    entries = ray_blocks * fanout
    rows = send_ref.shape[0]
    devices = rows // CHUNK

    small = [
        pltpu.make_async_copy(source, target, small_sem.at[i])
        for i, (source, target) in enumerate(
            ((device_hbm, device_ref), (block_hbm, block_ref), (counts_hbm, counts_ref),
             (times_hbm, times_ref), (prior_hbm, prior_ref))
        )
    ]
    large = pltpu.make_async_copy(kernel_hbm, tiles_ref, tile_sem)
    for copy in small + [large]:
        copy.start()
    for copy in small:
        copy.wait()

    member = ones_where(iota((entries, ray_blocks), 0) // fanout == iota((entries, ray_blocks), 1))
    turn = iota((entries, fanout), 0) % fanout == iota((entries, fanout), 1)

    def column(table_ref):
        table = table_ref[...].astype(F32).astype(BF16)
        spread = lax.dot_general(member, table, NT, preferred_element_type=F32)
        return jnp.sum(jnp.where(turn, spread, 0.0), axis=1, keepdims=True)

    diagonal = iota((entries, entries), 0) == iota((entries, entries), 1)

    def as_row(col):
        return jnp.sum(jnp.where(diagonal, col, 0.0), axis=0, keepdims=True)

    target = column(device_ref)
    block = column(block_ref)
    target_row = as_row(target)
    earlier = iota((entries, entries), 1) < iota((entries, entries), 0)
    rank = jnp.sum(jnp.where(earlier & (target == target_row), 1.0, 0.0), axis=1, keepdims=True)
    first = target * CHUNK + 2.0 * rank
    to_col = first.astype(jnp.int32)
    to_row = as_row(first).astype(jnp.int32)
    for half in range(2):
        here = slice(half * entries, (half + 1) * entries)
        pick_ref[here, :] = ones_where(iota((entries, rows), 1) == to_col + half)
        place_ref[:, here] = ones_where(iota((rows, entries), 0) == to_row + half)

    same = iota((ray_blocks, ray_blocks), 0) == iota((ray_blocks, ray_blocks), 1)
    counts = jnp.sum(jnp.where(same, counts_ref[...].astype(F32), 0.0), axis=1, keepdims=True)
    mask = jnp.where(iota((ray_blocks, ray_len), 1).astype(F32) < counts, 1.0, 0.0)
    prior = prior_ref[...]
    weights = mask * jnp.sqrt((FREEDOM + 1.0) / (FREEDOM + prior * prior))
    weights_ref[...] = weights
    data = weights * times_ref[...]
    data_ref[...] = data

    large.wait()
    adjoint_group(tiles_ref, weights * data, partial_ref, 0, fanout)
    ids = jnp.where(iota((entries, LANES), 1).astype(F32) == rank, block + 1.0, 0.0).astype(BF16)
    named_by = ones_where(iota((devices, entries), 0).astype(F32) == target_row)
    zeros = jnp.zeros((devices, LANES), F32)
    pack(
        send_ref, stage_ref, matmul(place_ref[...], stacked(partial_ref[...].astype(BF16))),
        norm_row(total(data * data), zeros), matmul(named_by, ids), zeros, zeros,
    )


def send_field(send_ref, stage_ref, gathered, field, gather_ref):
    cells = [gathered[:, half * LANES : (half + 1) * LANES].T for half in range(2)]
    zeros = jnp.zeros(cells[0].shape, F32)
    norms = norm_row(total(field * field), zeros)
    pack(send_ref, stage_ref, matmul(gather_ref[...], stacked(field).astype(BF16)), norms, zeros, *cells)


def first_model_kernel(received_ref, send_ref, field_ref, state_ref, gather_ref, scatter_ref, stage_ref):
    received = received_ref[...]
    rows = received.shape[0]
    blocks = MB_R * MB_L
    stage_ref[...] = received.astype(F32)
    beta = norm_of(row_of(stage_ref, NORM_ROW)[...])
    ids = row_of(stage_ref, ID_ROW)[...]
    for j in range(CHUNK):
        ident = ids[:, j // 2 : j // 2 + 1] if j < NORM_ROW else 0.0
        row_of(stage_ref, j)[...] = jnp.broadcast_to(ident, ids.shape)
    hit = stage_ref[...] - 1.0 == iota((rows, LANES), 1).astype(F32)
    odd = iota((rows, LANES), 0) % 2
    for half in range(2):
        here = slice(half * blocks, (half + 1) * blocks)
        chosen = jnp.where(hit & (odd == half), 1.0, 0.0)
        gather_ref[:, here] = chosen.astype(BF16)
        scatter_ref[here, :] = chosen.T.astype(BF16)

    gathered = unstacked(matmul(scatter_ref[...], received)).astype(BF16).astype(F32)
    field = gathered / beta
    field_ref[...] = field
    state_ref[...] = scalars_row(beta)
    send_field(send_ref, stage_ref, gathered, field, gather_ref)


def ray_step(
    sweep, rads, received_ref, tiles_ref, pick_ref, weights_ref, data_ref, state_ref, cells_ref, data_out, alpha_out,
    stage_ref, blocks_ref, partial_ref=None,
):
    received = received_ref[...]
    ray_blocks, ray_len = data_ref.shape
    devices = received.shape[0] // CHUNK
    fanout = blocks_ref.shape[0] // ray_blocks
    blocks_ref[...] = unstacked(matmul(pick_ref[...], received))
    stage_ref[...] = received.astype(F32)
    alpha = norm_of(row_of(stage_ref, NORM_ROW)[...])
    alpha_out[...] = scalars_row(alpha)
    beta = state_ref[0:1, 0:1]

    waiting = None
    for start in range(0, ray_blocks, GROUP):
        here = slice(start, start + GROUP)
        products = forward_group(tiles_ref, blocks_ref, start, GROUP, fanout, ray_len)
        weights = weights_ref[here, :]
        data = weights * (products / alpha) - alpha * (data_ref[here, :] / beta)
        data_out[here, :] = data
        if partial_ref is not None:
            if waiting is not None:
                adjoint_group(tiles_ref, waiting[0], partial_ref, waiting[1], fanout)
            waiting = weights * data, start
    if partial_ref is not None:
        adjoint_group(tiles_ref, waiting[0], partial_ref, waiting[1], fanout)

    data = data_out[...]
    partial = total(data * data)
    pens, directions = [], []
    for j in range(2):
        cell = row_of(stage_ref, CELL_ROW + j)[...]
        if sweep:
            rough, before, pen = [cells_ref[i, j * devices : (j + 1) * devices] for i in range(3)]
            direction = ((cell + rough) / beta - beta * before) / alpha
            pen = DAMPING * roughen(direction, rads) - alpha * (pen / beta)
        else:
            direction = cell / (beta * alpha)
            pen = DAMPING * roughen(direction, rads)
        partial = partial + total(pen * pen)
        pens.append(pen)
        directions.append(direction)
    return partial, pens, directions


def ray_kernel(sweep, rads, *refs):
    inputs, place_ref = refs[:6], refs[6]
    cells_ref = refs[7] if sweep else None
    send_ref, data_out, cells_out, alpha_out, stage_ref, blocks_ref, partial_ref = refs[-7:]
    partial, pens, directions = ray_step(
        sweep, rads, *inputs, cells_ref, data_out, alpha_out, stage_ref, blocks_ref, partial_ref
    )
    rough = [DAMPING * roughen(pen, rads) for pen in pens]
    for i, kept in enumerate((rough, directions, pens)):
        cells_out[i] = jnp.concatenate(kept, axis=0)
    high = [x.astype(BF16).astype(F32) for x in rough]
    low = [x - y for x, y in zip(rough, high)]
    pack(
        send_ref, stage_ref, matmul(place_ref[...], stacked(partial_ref[...]).astype(BF16)),
        norm_row(partial, low[1]), low[0], *high,
    )


def last_ray_kernel(sweep, rads, *refs):
    send_ref, data_out, alpha_out, stage_ref, blocks_ref = refs[-5:]
    partial, _, _ = ray_step(sweep, rads, *refs[:-5], data_out, alpha_out, stage_ref, blocks_ref)
    send_ref[...] = jnp.broadcast_to(partial.reshape(1, 1, 1), send_ref.shape)


def advance(sweep, beta, field_ref, alpha_ref, state_ref, search_ref, update_ref):
    alpha = alpha_ref[0:1, 0:1]
    direction = field_ref[...] / alpha
    if sweep:
        phi_bar, rho, cosine, sine = [state_ref[0:1, i : i + 1] for i in range(1, 5)]
        search = direction - (sine * alpha / rho) * search_ref[...]
        rho_bar = -cosine * alpha
    else:
        phi_bar, rho_bar = state_ref[0:1, 0:1], alpha
        search = direction
    rho = jnp.sqrt(rho_bar * rho_bar + beta * beta)
    cosine, sine = rho_bar / rho, beta / rho
    update = (cosine * phi_bar / rho) * search
    if sweep:
        update = update_ref[...] + update
    return direction, search, update, scalars_row(beta, sine * phi_bar, rho, cosine, sine)


def model_kernel(sweep, *refs):
    received_ref, scatter_ref, gather_ref, field_ref, alpha_ref, state_ref = refs[:6]
    search_ref, update_ref = refs[6:8] if sweep else (None, None)
    send_ref, field_out, state_out, search_out, update_out, stage_ref = refs[-6:]
    received = received_ref[...]
    gathered = unstacked(matmul(scatter_ref[...], received)).astype(BF16).astype(F32)
    stage_ref[...] = received.astype(F32)
    first = row_of(stage_ref, NORM_ROW)[...]
    beta = norm_of(first)
    low = [row_of(stage_ref, ID_ROW)[...], jnp.where(iota(first.shape, 1) < 2, 0.0, first)]
    rough = [(row_of(stage_ref, CELL_ROW + j)[...] + low[j]).T for j in range(2)]
    direction, search, update, state = advance(
        sweep, beta, field_ref, alpha_ref, state_ref, search_ref, update_ref
    )
    field = (gathered + jnp.concatenate(rough, axis=1)) / beta - beta * direction
    field_out[...] = field
    send_field(send_ref, stage_ref, gathered, field, gather_ref)
    state_out[...] = state
    search_out[...] = search
    update_out[...] = update


def last_kernel(norms_ref, data_ref, field_ref, alpha_ref, state_ref, search_ref, update_ref, update_out, data_out):
    beta = jnp.sqrt(jnp.sum(norms_ref[...], axis=0))
    update_out[...] = advance(ITERS - 1, beta, field_ref, alpha_ref, state_ref, search_ref, update_ref)[2]
    data_out[...] = data_ref[...] / beta


def call(kernel, name, outputs, scratch, operands, flops=0, space=pltpu.VMEM):
    bytes_accessed = sum(x.size * x.dtype.itemsize for x in operands)
    return pl.pallas_call(
        kernel,
        name=name,
        out_shape=[jax.ShapeDtypeStruct(shape, dtype) for shape, dtype in outputs],
        in_specs=[pl.BlockSpec(memory_space=space)] * len(operands),
        out_specs=[pl.BlockSpec(memory_space=pltpu.VMEM)] * len(outputs),
        scratch_shapes=scratch,
        compiler_params=pltpu.CompilerParams(vmem_limit_bytes=12 << 20),
        cost_estimate=pl.CostEstimate(flops=flops, bytes_accessed=bytes_accessed, transcendentals=0),
    )(*operands)


def exchange(packed, devices):
    rows, lanes = packed.shape
    chunks = packed.reshape(devices, rows // devices, lanes)
    return lax.all_to_all(chunks, AXES, split_axis=0, concat_axis=0, tiled=True).reshape(rows, lanes)


def body(kernel, target_device, target_block, counts, traveltimes, prior_residual):
    rads = lax.axis_size("rad")
    devices = lax.axis_size("lat") * rads
    ray_blocks, fanout, ray_len, cells = kernel.shape
    entries = ray_blocks * fanout
    rows = devices * CHUNK
    blocks = MB_R * MB_L
    flops = 4 * entries * ray_len * cells

    packet = ((rows, LANES), BF16)
    ray = ((ray_blocks, ray_len), F32)
    model = ((blocks, cells), F32)
    scalar = ((8, LANES), F32)
    partials = pltpu.VMEM((entries, cells), F32)

    stage = pltpu.VMEM((rows, LANES), F32)
    send, tiles, weights, data, place, pick = call(
        start_kernel, "start",
        [packet, ((entries * ray_len, cells), BF16), ray, ray,
         ((rows, 2 * entries), BF16), ((2 * entries, rows), BF16)],
        [
            pltpu.VMEM((fanout, ray_blocks), jnp.int32), pltpu.VMEM((fanout, ray_blocks), jnp.int32),
            pltpu.VMEM((1, ray_blocks), jnp.int32), pltpu.VMEM((ray_blocks, ray_len), F32),
            pltpu.VMEM((ray_blocks, ray_len), F32), partials, stage,
            pltpu.SemaphoreType.DMA((5,)), pltpu.SemaphoreType.DMA,
        ],
        tuple(
            pltpu.with_memory_space_constraint(x, pltpu.HBM)
            for x in (kernel.reshape(entries * ray_len, cells), target_device.T, target_block.T,
                      counts.reshape(1, ray_blocks), traveltimes, prior_residual)
        ),
        flops, pltpu.HBM,
    )
    received = exchange(send, devices)
    send, field, state, gather, scatter = call(
        first_model_kernel, "first_model",
        [packet, model, scalar, ((rows, 2 * blocks), BF16), ((2 * blocks, rows), BF16)], [stage], (received,),
    )
    carried, kept = (), ()
    for sweep in range(ITERS):
        received = exchange(send, devices)
        if sweep == ITERS - 1:
            break
        send, data, cell_state, alpha = call(
            functools.partial(ray_kernel, sweep, rads), "ray",
            [packet, ray, ((3, 2 * devices, blocks), F32), scalar], [stage, partials, partials],
            (received, tiles, pick, weights, data, state, place) + kept, flops,
        )
        kept = (cell_state,)
        received = exchange(send, devices)
        send, field, state, *carried = call(
            functools.partial(model_kernel, sweep), "model", [packet, model, scalar, model, model], [stage],
            (received, scatter, gather, field, alpha, state, *carried), flops,
        )
    send, data, alpha = call(
        functools.partial(last_ray_kernel, ITERS - 1, rads), "last_ray", [((devices, 1, 1), F32), ray, scalar],
        [stage, partials], (received, tiles, pick, weights, data, state) + kept, flops,
    )
    norms = lax.all_to_all(send, AXES, split_axis=0, concat_axis=0, tiled=True)
    update, data = call(last_kernel, "last", [model, ray], [], (norms, data, field, alpha, state, *carried))
    return (update.reshape(MB_R, MB_L, cells), data)


def solution(mesh):
    in_specs = (
        P(("lat", "rad"), None, None, None),
        P(("lat", "rad"), None),
        P(("lat", "rad"), None),
        P(("lat", "rad")),
        P(("lat", "rad"), None),
        P(("lat", "rad"), None),
    )
    out_specs = (P("rad", "lat", None), P(("lat", "rad"), None))
    return jax.shard_map(body, mesh=mesh, in_specs=in_specs, out_specs=out_specs, check_vma=False)
```

```python
import functools

import jax
import jax.numpy as jnp
from jax import lax
from jax.experimental import pallas as pl
from jax.experimental.pallas import tpu as pltpu
from jax.sharding import PartitionSpec as P

ITERS = 3
MB_R = 8
MB_L = 16
FREEDOM = 4.0
DAMPING = 0.3

AXES = ("lat", "rad")
CHUNK = 8
NORM_ROW = 4
ID_ROW = 5
CELL_ROW = 6
LANES = 128
GROUP = 8

F32 = jnp.float32
BF16 = jnp.bfloat16
NT = (((1,), (1,)), ((), ()))


def iota(shape, dim):
    return lax.broadcasted_iota(jnp.int32, shape, dim)


def matmul(a, b):
    return jnp.dot(a, b, preferred_element_type=F32)


def total(x):
    return jnp.sum(jnp.sum(x, axis=1, keepdims=True), axis=0, keepdims=True)


def ones_where(condition):
    return jnp.where(condition, 1.0, 0.0).astype(BF16)


def norm_row(partial, rest):
    high = partial.astype(BF16).astype(F32)
    lane = iota(rest.shape, 1)
    return jnp.where(lane == 0, high, jnp.where(lane == 1, partial - high, rest))


def norm_of(sums):
    sums = jnp.where(iota(sums.shape, 1) < 2, sums, 0.0)
    return jnp.sqrt(total(sums))


def row_of(ref, j):
    return ref.at[pl.ds(j, ref.shape[0] // CHUNK, stride=CHUNK), :]


def pack(send_ref, stage_ref, named, *rest):
    for j, rows in enumerate(rest):
        row_of(stage_ref, NORM_ROW + j)[...] = rows
    data = iota(named.shape, 0) % CHUNK < NORM_ROW
    send_ref[...] = jnp.where(data, named, stage_ref[...]).astype(BF16)


def stacked(x):
    return jnp.concatenate([x[:, :LANES], x[:, LANES:]], axis=0)


def unstacked(x):
    half = x.shape[0] // 2
    return jnp.concatenate([x[:half], x[half:]], axis=1)


def forward_group(tiles_ref, blocks_ref, start, count, fanout, ray_len):
    lane = iota((ray_len, LANES), 1)
    sums = jnp.zeros((ray_len, LANES), F32)
    for i in range(count):
        products = None
        for e in range((start + i) * fanout, (start + i + 1) * fanout):
            product = tiles_ref[e * ray_len : (e + 1) * ray_len, :].astype(F32) * blocks_ref[e : e + 1, :]
            product = product[:, :LANES] + product[:, LANES:]
            products = product if products is None else products + product
        sums = jnp.where(lane == i, jnp.sum(products, axis=1, keepdims=True), sums)
    return sums.T[:count]


def adjoint_group(tiles_ref, y, out_ref, start, fanout):
    high = y.astype(BF16).astype(F32)
    low = y - high
    high = jnp.concatenate([high] * fanout, axis=1)
    low = jnp.concatenate([low] * fanout, axis=1)
    count, width = high.shape
    ray_len = width // fanout
    row, lane = iota((2 * fanout, width), 0), iota((2 * fanout, width), 1)
    own = lane // ray_len == row % fanout
    for i in range(count):
        b = start + i
        lhs = jnp.where(row < fanout, high[i : i + 1], low[i : i + 1])
        lhs = jnp.where(own, lhs, 0.0).astype(BF16)
        both = matmul(lhs, tiles_ref[b * width : (b + 1) * width, :])
        out_ref[b * fanout : (b + 1) * fanout, :] = both[:fanout] + both[fanout:]


def roughen(cell, rads):
    shape = cell.shape
    devices, blocks = shape
    device, block = iota(shape, 0), iota(shape, 1)
    rad, place = device % rads, block % MB_L
    lanes = lambda x, step: pltpu.roll(x, step % blocks, 1)
    owner = lambda x, step: pltpu.roll(x, step % devices, 0)
    up = lanes(cell, MB_L)
    north = jnp.where(block >= MB_L, up, jnp.where(rad > 0, owner(up, 1), 0.0))
    down = lanes(cell, -MB_L)
    south = jnp.where(block < blocks - MB_L, down, jnp.where(rad < rads - 1, owner(down, -1), 0.0))
    far = owner(lanes(cell, 1 - MB_L), rads)
    west = jnp.where(place > 0, lanes(cell, 1), jnp.where(device >= rads, far, 0.0))
    far = owner(lanes(cell, MB_L - 1), -rads)
    east = jnp.where(place < MB_L - 1, lanes(cell, -1), jnp.where(device < devices - rads, far, 0.0))
    return 4.0 * cell - (south + north + east + west)


def scalars_row(*values):
    lane = iota((8, LANES), 1)
    out = jnp.zeros((8, LANES), F32)
    for i, value in enumerate(values):
        out = jnp.where(lane == i, value, out)
    return out


def start_kernel(
    kernel_hbm, device_hbm, block_hbm, counts_hbm, times_hbm, prior_hbm,
    send_ref, tiles_ref, weights_ref, data_ref, place_ref, pick_ref,
    device_ref, block_ref, counts_ref, times_ref, prior_ref, partial_ref, stage_ref, small_sem, tile_sem,
):
    fanout, ray_blocks = device_ref.shape
    ray_len = times_ref.shape[1]
    entries = ray_blocks * fanout
    rows = send_ref.shape[0]
    devices = rows // CHUNK

    small = [
        pltpu.make_async_copy(source, target, small_sem.at[i])
        for i, (source, target) in enumerate(
            ((device_hbm, device_ref), (block_hbm, block_ref), (counts_hbm, counts_ref),
             (times_hbm, times_ref), (prior_hbm, prior_ref))
        )
    ]
    large = pltpu.make_async_copy(kernel_hbm, tiles_ref, tile_sem)
    for copy in small + [large]:
        copy.start()
    for copy in small:
        copy.wait()

    member = ones_where(iota((entries, ray_blocks), 0) // fanout == iota((entries, ray_blocks), 1))
    turn = iota((entries, fanout), 0) % fanout == iota((entries, fanout), 1)

    def column(table_ref):
        table = table_ref[...].astype(F32).astype(BF16)
        spread = lax.dot_general(member, table, NT, preferred_element_type=F32)
        return jnp.sum(jnp.where(turn, spread, 0.0), axis=1, keepdims=True)

    diagonal = iota((entries, entries), 0) == iota((entries, entries), 1)

    def as_row(col):
        return jnp.sum(jnp.where(diagonal, col, 0.0), axis=0, keepdims=True)

    target = column(device_ref)
    block = column(block_ref)
    target_row = as_row(target)
    earlier = iota((entries, entries), 1) < iota((entries, entries), 0)
    rank = jnp.sum(jnp.where(earlier & (target == target_row), 1.0, 0.0), axis=1, keepdims=True)
    first = target * CHUNK + 2.0 * rank
    to_col = first.astype(jnp.int32)
    to_row = as_row(first).astype(jnp.int32)
    for half in range(2):
        here = slice(half * entries, (half + 1) * entries)
        pick_ref[here, :] = ones_where(iota((entries, rows), 1) == to_col + half)
        place_ref[:, here] = ones_where(iota((rows, entries), 0) == to_row + half)

    same = iota((ray_blocks, ray_blocks), 0) == iota((ray_blocks, ray_blocks), 1)
    counts = jnp.sum(jnp.where(same, counts_ref[...].astype(F32), 0.0), axis=1, keepdims=True)
    mask = jnp.where(iota((ray_blocks, ray_len), 1).astype(F32) < counts, 1.0, 0.0)
    prior = prior_ref[...]
    weights = mask * jnp.sqrt((FREEDOM + 1.0) / (FREEDOM + prior * prior))
    weights_ref[...] = weights
    data = weights * times_ref[...]
    data_ref[...] = data

    large.wait()
    adjoint_group(tiles_ref, weights * data, partial_ref, 0, fanout)
    ids = jnp.where(iota((entries, LANES), 1).astype(F32) == rank, block + 1.0, 0.0).astype(BF16)
    named_by = ones_where(iota((devices, entries), 0).astype(F32) == target_row)
    zeros = jnp.zeros((devices, LANES), F32)
    pack(
        send_ref, stage_ref, matmul(place_ref[...], stacked(partial_ref[...].astype(BF16))),
        norm_row(total(data * data), zeros), matmul(named_by, ids), zeros, zeros,
    )


def send_field(send_ref, stage_ref, gathered, field, gather_ref):
    cells = [gathered[:, half * LANES : (half + 1) * LANES].T for half in range(2)]
    zeros = jnp.zeros(cells[0].shape, F32)
    norms = norm_row(total(field * field), zeros)
    pack(send_ref, stage_ref, matmul(gather_ref[...], stacked(field).astype(BF16)), norms, zeros, *cells)


def first_model_kernel(received_ref, send_ref, field_ref, state_ref, gather_ref, scatter_ref, stage_ref):
    received = received_ref[...]
    rows = received.shape[0]
    blocks = MB_R * MB_L
    stage_ref[...] = received.astype(F32)
    beta = norm_of(row_of(stage_ref, NORM_ROW)[...])
    ids = row_of(stage_ref, ID_ROW)[...]
    for j in range(CHUNK):
        ident = ids[:, j // 2 : j // 2 + 1] if j < NORM_ROW else 0.0
        row_of(stage_ref, j)[...] = jnp.broadcast_to(ident, ids.shape)
    hit = stage_ref[...] - 1.0 == iota((rows, LANES), 1).astype(F32)
    odd = iota((rows, LANES), 0) % 2
    for half in range(2):
        here = slice(half * blocks, (half + 1) * blocks)
        chosen = jnp.where(hit & (odd == half), 1.0, 0.0)
        gather_ref[:, here] = chosen.astype(BF16)
        scatter_ref[here, :] = chosen.T.astype(BF16)

    gathered = unstacked(matmul(scatter_ref[...], received)).astype(BF16).astype(F32)
    field = gathered * (1.0 / beta)
    field_ref[...] = field
    state_ref[...] = scalars_row(beta)
    send_field(send_ref, stage_ref, gathered, field, gather_ref)


def ray_step(
    sweep, rads, received_ref, tiles_ref, pick_ref, weights_ref, data_ref, state_ref, cells_ref, data_out, alpha_out,
    stage_ref, blocks_ref, partial_ref=None,
):
    received = received_ref[...]
    ray_blocks, ray_len = data_ref.shape
    devices = received.shape[0] // CHUNK
    fanout = blocks_ref.shape[0] // ray_blocks
    blocks_ref[...] = unstacked(matmul(pick_ref[...], received))
    stage_ref[...] = received.astype(F32)
    alpha = norm_of(row_of(stage_ref, NORM_ROW)[...])
    alpha_out[...] = scalars_row(alpha)
    beta = state_ref[0:1, 0:1]
    inverse_alpha, inverse_beta = 1.0 / alpha, 1.0 / beta
    ratio = alpha / beta

    waiting = None
    for start in range(0, ray_blocks, GROUP):
        here = slice(start, start + GROUP)
        products = forward_group(tiles_ref, blocks_ref, start, GROUP, fanout, ray_len)
        weights = weights_ref[here, :]
        data = weights * (products * inverse_alpha) - ratio * data_ref[here, :]
        data_out[here, :] = data
        if partial_ref is not None:
            if waiting is not None:
                adjoint_group(tiles_ref, waiting[0], partial_ref, waiting[1], fanout)
            waiting = weights * data, start
    if partial_ref is not None:
        adjoint_group(tiles_ref, waiting[0], partial_ref, waiting[1], fanout)

    data = data_out[...]
    partial = total(data * data)
    pens, directions = [], []
    for j in range(2):
        cell = row_of(stage_ref, CELL_ROW + j)[...]
        if sweep:
            rough, before, pen = [cells_ref[i, j * devices : (j + 1) * devices] for i in range(3)]
            direction = ((cell + rough) * inverse_beta - beta * before) * inverse_alpha
            pen = DAMPING * roughen(direction, rads) - ratio * pen
        else:
            direction = (cell * inverse_beta) * inverse_alpha
            pen = DAMPING * roughen(direction, rads)
        partial = partial + total(pen * pen)
        pens.append(pen)
        directions.append(direction)
    return partial, pens, directions


def ray_kernel(sweep, rads, *refs):
    inputs, place_ref = refs[:6], refs[6]
    cells_ref = refs[7] if sweep else None
    send_ref, data_out, cells_out, alpha_out, stage_ref, blocks_ref, partial_ref = refs[-7:]
    partial, pens, directions = ray_step(
        sweep, rads, *inputs, cells_ref, data_out, alpha_out, stage_ref, blocks_ref, partial_ref
    )
    rough = [DAMPING * roughen(pen, rads) for pen in pens]
    for i, kept in enumerate((rough, directions, pens)):
        cells_out[i] = jnp.concatenate(kept, axis=0)
    high = [x.astype(BF16).astype(F32) for x in rough]
    low = [x - y for x, y in zip(rough, high)]
    pack(
        send_ref, stage_ref, matmul(place_ref[...], stacked(partial_ref[...]).astype(BF16)),
        norm_row(partial, low[1]), low[0], *high,
    )


def last_ray_kernel(sweep, rads, *refs):
    send_ref, data_out, alpha_out, stage_ref, blocks_ref = refs[-5:]
    partial, _, _ = ray_step(sweep, rads, *refs[:-5], data_out, alpha_out, stage_ref, blocks_ref)
    send_ref[...] = jnp.broadcast_to(partial, send_ref.shape)


def turn(sweep, field_ref, alpha_ref, state_ref, search_ref):
    alpha = alpha_ref[0:1, 0:1]
    direction = field_ref[...] * (1.0 / alpha)
    if sweep == 0:
        return direction, direction, state_ref[0:1, 0:1], alpha
    phi_bar, rho, cosine, sine = [state_ref[0:1, i : i + 1] for i in range(1, 5)]
    return direction, direction - (sine * alpha / rho) * search_ref[...], phi_bar, -cosine * alpha


def model_kernel(sweep, *refs):
    received_ref, scatter_ref, gather_ref, field_ref, alpha_ref, state_ref = refs[:6]
    search_ref, update_ref = refs[6:8] if sweep else (None, None)
    send_ref, field_out, state_out, search_out, update_out, stage_ref = refs[-6:]
    received = received_ref[...]
    gathered = unstacked(matmul(scatter_ref[...], received)).astype(BF16).astype(F32)
    stage_ref[...] = received.astype(F32)
    first = row_of(stage_ref, NORM_ROW)[...]
    beta = norm_of(first)
    low = [row_of(stage_ref, ID_ROW)[...], jnp.where(iota(first.shape, 1) < 2, 0.0, first)]
    rough = [(row_of(stage_ref, CELL_ROW + j)[...] + low[j]).T for j in range(2)]
    direction, search, phi_bar, rho_bar = turn(sweep, field_ref, alpha_ref, state_ref, search_ref)
    field = (gathered + jnp.concatenate(rough, axis=1)) * (1.0 / beta) - beta * direction
    field_out[...] = field
    send_field(send_ref, stage_ref, gathered, field, gather_ref)
    rho = jnp.sqrt(rho_bar * rho_bar + beta * beta)
    cosine, sine = rho_bar / rho, beta / rho
    state_out[...] = scalars_row(beta, sine * phi_bar, rho, cosine, sine)
    search_out[...] = search
    update = (cosine * phi_bar / rho) * search
    update_out[...] = update_ref[...] + update if sweep else update


def last_kernel(norms_ref, data_ref, field_ref, alpha_ref, state_ref, search_ref, update_ref, update_out, data_out):
    squares = jnp.sum(norms_ref[...], axis=0, keepdims=True)[:, 0:1]
    _, search, phi_bar, rho_bar = turn(ITERS - 1, field_ref, alpha_ref, state_ref, search_ref)
    step = rho_bar * phi_bar / (rho_bar * rho_bar + squares)
    update_out[...] = update_ref[...] + step * search
    data_out[...] = data_ref[...] * (1.0 / jnp.sqrt(squares))


def call(kernel, name, outputs, scratch, operands, flops=0, space=pltpu.VMEM):
    bytes_accessed = sum(x.size * x.dtype.itemsize for x in operands)
    return pl.pallas_call(
        kernel,
        name=name,
        out_shape=[jax.ShapeDtypeStruct(shape, dtype) for shape, dtype in outputs],
        in_specs=[pl.BlockSpec(memory_space=space)] * len(operands),
        out_specs=[pl.BlockSpec(memory_space=pltpu.VMEM)] * len(outputs),
        scratch_shapes=scratch,
        compiler_params=pltpu.CompilerParams(vmem_limit_bytes=12 << 20),
        cost_estimate=pl.CostEstimate(flops=flops, bytes_accessed=bytes_accessed, transcendentals=0),
    )(*operands)


def exchange(packed, devices):
    rows, lanes = packed.shape
    chunks = packed.reshape(devices, rows // devices, lanes)
    return lax.all_to_all(chunks, AXES, split_axis=0, concat_axis=0, tiled=True).reshape(rows, lanes)


def body(kernel, target_device, target_block, counts, traveltimes, prior_residual):
    rads = lax.axis_size("rad")
    devices = lax.axis_size("lat") * rads
    ray_blocks, fanout, ray_len, cells = kernel.shape
    entries = ray_blocks * fanout
    rows = devices * CHUNK
    blocks = MB_R * MB_L
    flops = 4 * entries * ray_len * cells

    packet = ((rows, LANES), BF16)
    ray = ((ray_blocks, ray_len), F32)
    model = ((blocks, cells), F32)
    scalar = ((8, LANES), F32)
    partials = pltpu.VMEM((entries, cells), F32)

    stage = pltpu.VMEM((rows, LANES), F32)
    send, tiles, weights, data, place, pick = call(
        start_kernel, "start",
        [packet, ((entries * ray_len, cells), BF16), ray, ray,
         ((rows, 2 * entries), BF16), ((2 * entries, rows), BF16)],
        [
            pltpu.VMEM((fanout, ray_blocks), jnp.int32), pltpu.VMEM((fanout, ray_blocks), jnp.int32),
            pltpu.VMEM((1, ray_blocks), jnp.int32), pltpu.VMEM((ray_blocks, ray_len), F32),
            pltpu.VMEM((ray_blocks, ray_len), F32), partials, stage,
            pltpu.SemaphoreType.DMA((5,)), pltpu.SemaphoreType.DMA,
        ],
        tuple(
            pltpu.with_memory_space_constraint(x, pltpu.HBM)
            for x in (kernel.reshape(entries * ray_len, cells), target_device.T, target_block.T,
                      counts.reshape(1, ray_blocks), traveltimes, prior_residual)
        ),
        flops, pltpu.HBM,
    )
    received = exchange(send, devices)
    send, field, state, gather, scatter = call(
        first_model_kernel, "first_model",
        [packet, model, scalar, ((rows, 2 * blocks), BF16), ((2 * blocks, rows), BF16)], [stage], (received,),
    )
    carried, kept = (), ()
    for sweep in range(ITERS):
        received = exchange(send, devices)
        if sweep == ITERS - 1:
            break
        send, data, cell_state, alpha = call(
            functools.partial(ray_kernel, sweep, rads), "ray",
            [packet, ray, ((3, 2 * devices, blocks), F32), scalar], [stage, partials, partials],
            (received, tiles, pick, weights, data, state, place) + kept, flops,
        )
        kept = (cell_state,)
        received = exchange(send, devices)
        send, field, state, *carried = call(
            functools.partial(model_kernel, sweep), "model", [packet, model, scalar, model, model], [stage],
            (received, scatter, gather, field, alpha, state, *carried), flops,
        )
    send, data, alpha = call(
        functools.partial(last_ray_kernel, ITERS - 1, rads), "last_ray", [((devices, LANES), F32), ray, scalar],
        [stage, partials], (received, tiles, pick, weights, data, state) + kept, flops,
    )
    norms = exchange(send, devices)
    update, data = call(last_kernel, "last", [model, ray], [], (norms, data, field, alpha, state, *carried))
    return (update.reshape(MB_R, MB_L, cells), data)


def solution(mesh):
    in_specs = (
        P(("lat", "rad"), None, None, None),
        P(("lat", "rad"), None),
        P(("lat", "rad"), None),
        P(("lat", "rad")),
        P(("lat", "rad"), None),
        P(("lat", "rad"), None),
    )
    out_specs = (P("rad", "lat", None), P(("lat", "rad"), None))
    return jax.shard_map(body, mesh=mesh, in_specs=in_specs, out_specs=out_specs, check_vma=False)
```

```python
import functools

import jax
import jax.numpy as jnp
from jax import lax
from jax.experimental import pallas as pl
from jax.experimental.pallas import tpu as pltpu
from jax.sharding import PartitionSpec as P

ITERS = 3
MB_R = 8
MB_L = 16
FREEDOM = 4.0
DAMPING = 0.3

AXES = ("lat", "rad")
CHUNK = 8
NORM_ROW = 4
ID_ROW = 5
CELL_ROW = 6
LANES = 128
GROUP = 8

F32 = jnp.float32
BF16 = jnp.bfloat16
NT = (((1,), (1,)), ((), ()))


def iota(shape, dim):
    return lax.broadcasted_iota(jnp.int32, shape, dim)


def low(index, size):
    assert size & (size - 1) == 0
    return index & (size - 1)


def high(index, size):
    assert size & (size - 1) == 0
    return lax.shift_right_logical(index, jnp.int32(size.bit_length() - 1))


def matmul(a, b):
    return jnp.dot(a, b, preferred_element_type=F32)


def total(x):
    return jnp.sum(jnp.sum(x, axis=1, keepdims=True), axis=0, keepdims=True)


def ones_where(condition):
    return jnp.where(condition, 1.0, 0.0).astype(BF16)


def norm_row(partial, rest):
    upper = partial.astype(BF16).astype(F32)
    lane = iota(rest.shape, 1)
    return jnp.where(lane == 0, upper, jnp.where(lane == 1, partial - upper, rest))


def norm_of(sums):
    sums = jnp.where(iota(sums.shape, 1) < 2, sums, 0.0)
    return jnp.sqrt(total(sums))


def row_of(ref, j):
    return ref.at[pl.ds(j, ref.shape[0] // CHUNK, stride=CHUNK), :]


def pack(send_ref, stage_ref, named, *rest):
    for j, rows in enumerate(rest):
        row_of(stage_ref, NORM_ROW + j)[...] = rows
    data = low(iota(named.shape, 0), CHUNK) < NORM_ROW
    send_ref[...] = jnp.where(data, named, stage_ref[...]).astype(BF16)


def stacked(x):
    return jnp.concatenate([x[:, :LANES], x[:, LANES:]], axis=0)


def unstacked(x):
    half = x.shape[0] // 2
    return jnp.concatenate([x[:half], x[half:]], axis=1)


def forward_group(tiles_ref, blocks_ref, start, count, fanout, ray_len):
    lane = iota((ray_len, LANES), 1)
    sums = jnp.zeros((ray_len, LANES), F32)
    for i in range(count):
        products = None
        for e in range((start + i) * fanout, (start + i + 1) * fanout):
            product = tiles_ref[e * ray_len : (e + 1) * ray_len, :].astype(F32) * blocks_ref[e : e + 1, :]
            product = product[:, :LANES] + product[:, LANES:]
            products = product if products is None else products + product
        sums = jnp.where(lane == i, jnp.sum(products, axis=1, keepdims=True), sums)
    return sums.T[:count]


def spread_rows(y, fanout):
    upper = y.astype(BF16).astype(F32)
    lower = y - upper
    upper = jnp.concatenate([upper] * fanout, axis=1)
    lower = jnp.concatenate([lower] * fanout, axis=1)
    count, width = upper.shape
    row, lane = iota((2 * fanout, width), 0), iota((2 * fanout, width), 1)
    own = high(lane, width // fanout) == low(row, fanout)
    return [
        jnp.where(own, jnp.where(row < fanout, upper[i : i + 1], lower[i : i + 1]), 0.0) for i in range(count)
    ]


def adjoint_products(tiles_ref, lhs, out_ref, b, fanout):
    width = lhs.shape[1]
    both = matmul(lhs, tiles_ref[b * width : (b + 1) * width, :])
    out_ref[b * fanout : (b + 1) * fanout, :] = both[:fanout] + both[fanout:]


def adjoint_group(tiles_ref, y, out_ref, start, fanout):
    for i, lhs in enumerate(spread_rows(y, fanout)):
        adjoint_products(tiles_ref, lhs.astype(BF16), out_ref, start + i, fanout)


def roughen(cell, rads):
    shape = cell.shape
    devices, blocks = shape
    device, block = iota(shape, 0), iota(shape, 1)
    rad, place = low(device, rads), low(block, MB_L)
    lanes = lambda x, step: pltpu.roll(x, step % blocks, 1)
    owner = lambda x, step: pltpu.roll(x, step % devices, 0)
    up = lanes(cell, MB_L)
    north = jnp.where(block >= MB_L, up, jnp.where(rad > 0, owner(up, 1), 0.0))
    down = lanes(cell, -MB_L)
    south = jnp.where(block < blocks - MB_L, down, jnp.where(rad < rads - 1, owner(down, -1), 0.0))
    far = owner(lanes(cell, 1 - MB_L), rads)
    west = jnp.where(place > 0, lanes(cell, 1), jnp.where(device >= rads, far, 0.0))
    far = owner(lanes(cell, MB_L - 1), -rads)
    east = jnp.where(place < MB_L - 1, lanes(cell, -1), jnp.where(device < devices - rads, far, 0.0))
    return 4.0 * cell - (south + north + east + west)


def scalars_row(*values):
    lane = iota((8, LANES), 1)
    out = jnp.zeros((8, LANES), F32)
    for i, value in enumerate(values):
        out = jnp.where(lane == i, value, out)
    return out


def start_kernel(
    kernel_hbm, device_hbm, block_hbm, counts_hbm, times_hbm, prior_hbm,
    send_ref, tiles_ref, weights_ref, data_ref, place_ref, pick_ref,
    device_ref, block_ref, counts_ref, times_ref, prior_ref, partial_ref, stage_ref, operand_ref, small_sem, tile_sem,
):
    fanout, ray_blocks = device_ref.shape
    ray_len = times_ref.shape[1]
    entries = ray_blocks * fanout
    rows = send_ref.shape[0]
    devices = rows // CHUNK

    small = [
        pltpu.make_async_copy(source, target, small_sem.at[i])
        for i, (source, target) in enumerate(
            ((device_hbm, device_ref), (block_hbm, block_ref), (counts_hbm, counts_ref),
             (times_hbm, times_ref), (prior_hbm, prior_ref))
        )
    ]
    large = pltpu.make_async_copy(kernel_hbm, tiles_ref, tile_sem)
    for copy in small + [large]:
        copy.start()
    for copy in small:
        copy.wait()

    member = ones_where(high(iota((entries, ray_blocks), 0), fanout) == iota((entries, ray_blocks), 1))
    turn = low(iota((entries, fanout), 0), fanout) == iota((entries, fanout), 1)

    def column(table_ref):
        table = table_ref[...].astype(F32).astype(BF16)
        spread = lax.dot_general(member, table, NT, preferred_element_type=F32)
        return jnp.sum(jnp.where(turn, spread, 0.0), axis=1, keepdims=True)

    diagonal = iota((entries, entries), 0) == iota((entries, entries), 1)

    def as_row(col):
        return jnp.sum(jnp.where(diagonal, col, 0.0), axis=0, keepdims=True)

    target = column(device_ref)
    block = column(block_ref)
    target_row = as_row(target)
    earlier = iota((entries, entries), 1) < iota((entries, entries), 0)
    rank = jnp.sum(jnp.where(earlier & (target == target_row), 1.0, 0.0), axis=1, keepdims=True)
    first = target * CHUNK + 2.0 * rank
    to_col = first.astype(jnp.int32)
    to_row = as_row(first).astype(jnp.int32)
    for half in range(2):
        here = slice(half * entries, (half + 1) * entries)
        pick_ref[here, :] = ones_where(iota((entries, rows), 1) == to_col + half)
        place_ref[:, here] = ones_where(iota((rows, entries), 0) == to_row + half)

    same = iota((ray_blocks, ray_blocks), 0) == iota((ray_blocks, ray_blocks), 1)
    counts = jnp.sum(jnp.where(same, counts_ref[...].astype(F32), 0.0), axis=1, keepdims=True)
    mask = jnp.where(iota((ray_blocks, ray_len), 1).astype(F32) < counts, 1.0, 0.0)
    prior = prior_ref[...]
    weights = mask * jnp.sqrt((FREEDOM + 1.0) / (FREEDOM + prior * prior))
    weights_ref[...] = weights
    data = weights * times_ref[...]
    data_ref[...] = data

    operands = spread_rows(weights * data, fanout)
    depth = 2 * fanout
    for b in range(0, ray_blocks, 2):
        operand_ref[b * depth : (b + 2) * depth, :] = jnp.concatenate(operands[b : b + 2], axis=0).astype(BF16)
    ids = jnp.where(iota((entries, LANES), 1).astype(F32) == rank, block + 1.0, 0.0).astype(BF16)
    named_by = ones_where(iota((devices, entries), 0).astype(F32) == target_row)
    zeros = jnp.zeros((devices, LANES), F32)
    rest = norm_row(total(data * data), zeros), matmul(named_by, ids), zeros, zeros
    for j, rows_of in enumerate(rest):
        row_of(stage_ref, NORM_ROW + j)[...] = rows_of
    large.wait()
    for b in range(ray_blocks):
        adjoint_products(tiles_ref, operand_ref[b * depth : (b + 1) * depth, :], partial_ref, b, fanout)
    pack(send_ref, stage_ref, matmul(place_ref[...], stacked(partial_ref[...].astype(BF16))))


def send_field(send_ref, stage_ref, gathered, field, gather_ref):
    cells = [gathered[:, half * LANES : (half + 1) * LANES].T for half in range(2)]
    zeros = jnp.zeros(cells[0].shape, F32)
    norms = norm_row(total(field * field), zeros)
    pack(send_ref, stage_ref, matmul(gather_ref[...], stacked(field).astype(BF16)), norms, zeros, *cells)


def first_model_kernel(received_ref, send_ref, field_ref, state_ref, gather_ref, scatter_ref, stage_ref):
    received = received_ref[...]
    rows = received.shape[0]
    blocks = MB_R * MB_L
    stage_ref[...] = received.astype(F32)
    beta = norm_of(row_of(stage_ref, NORM_ROW)[...])
    ids = row_of(stage_ref, ID_ROW)[...]
    for j in range(CHUNK):
        ident = ids[:, j // 2 : j // 2 + 1] if j < NORM_ROW else 0.0
        row_of(stage_ref, j)[...] = jnp.broadcast_to(ident, ids.shape)
    hit = stage_ref[...] - 1.0 == iota((rows, LANES), 1).astype(F32)
    odd = low(iota((rows, LANES), 0), 2)
    for half in range(2):
        here = slice(half * blocks, (half + 1) * blocks)
        chosen = jnp.where(hit & (odd == half), 1.0, 0.0)
        gather_ref[:, here] = chosen.astype(BF16)
        scatter_ref[here, :] = chosen.T.astype(BF16)

    gathered = unstacked(matmul(scatter_ref[...], received)).astype(BF16).astype(F32)
    field = gathered * (1.0 / beta)
    field_ref[...] = field
    state_ref[...] = scalars_row(beta)
    send_field(send_ref, stage_ref, gathered, field, gather_ref)


def ray_step(
    sweep, rads, received_ref, tiles_ref, pick_ref, weights_ref, data_ref, state_ref, cells_ref, data_out, alpha_out,
    stage_ref, blocks_ref, partial_ref=None,
):
    received = received_ref[...]
    ray_blocks, ray_len = data_ref.shape
    devices = received.shape[0] // CHUNK
    fanout = blocks_ref.shape[0] // ray_blocks
    blocks_ref[...] = unstacked(matmul(pick_ref[...], received))
    stage_ref[...] = received.astype(F32)
    alpha = norm_of(row_of(stage_ref, NORM_ROW)[...])
    alpha_out[...] = scalars_row(alpha)
    beta = state_ref[0:1, 0:1]
    inverse_alpha, inverse_beta = 1.0 / alpha, 1.0 / beta
    ratio = alpha / beta

    waiting = None
    for start in range(0, ray_blocks, GROUP):
        here = slice(start, start + GROUP)
        products = forward_group(tiles_ref, blocks_ref, start, GROUP, fanout, ray_len)
        weights = weights_ref[here, :]
        data = weights * (products * inverse_alpha) - ratio * data_ref[here, :]
        data_out[here, :] = data
        if partial_ref is not None:
            if waiting is not None:
                adjoint_group(tiles_ref, waiting[0], partial_ref, waiting[1], fanout)
            waiting = weights * data, start
    if partial_ref is not None:
        adjoint_group(tiles_ref, waiting[0], partial_ref, waiting[1], fanout)

    data = data_out[...]
    partial = total(data * data)
    pens, directions = [], []
    for j in range(2):
        cell = row_of(stage_ref, CELL_ROW + j)[...]
        if sweep:
            rough, before, pen = [cells_ref[i, j * devices : (j + 1) * devices] for i in range(3)]
            direction = ((cell + rough) * inverse_beta - beta * before) * inverse_alpha
            pen = DAMPING * roughen(direction, rads) - ratio * pen
        else:
            direction = (cell * inverse_beta) * inverse_alpha
            pen = DAMPING * roughen(direction, rads)
        partial = partial + total(pen * pen)
        pens.append(pen)
        directions.append(direction)
    return partial, pens, directions


def ray_kernel(sweep, rads, *refs):
    inputs, place_ref = refs[:6], refs[6]
    cells_ref = refs[7] if sweep else None
    send_ref, data_out, cells_out, alpha_out, stage_ref, blocks_ref, partial_ref = refs[-7:]
    partial, pens, directions = ray_step(
        sweep, rads, *inputs, cells_ref, data_out, alpha_out, stage_ref, blocks_ref, partial_ref
    )
    rough = [DAMPING * roughen(pen, rads) for pen in pens]
    for i, kept in enumerate((rough, directions, pens)):
        cells_out[i] = jnp.concatenate(kept, axis=0)
    upper = [x.astype(BF16).astype(F32) for x in rough]
    lower = [x - y for x, y in zip(rough, upper)]
    pack(
        send_ref, stage_ref, matmul(place_ref[...], stacked(partial_ref[...]).astype(BF16)),
        norm_row(partial, lower[1]), lower[0], *upper,
    )


def last_ray_kernel(sweep, rads, *refs):
    send_ref, data_out, alpha_out, stage_ref, blocks_ref = refs[-5:]
    partial, _, _ = ray_step(sweep, rads, *refs[:-5], data_out, alpha_out, stage_ref, blocks_ref)
    send_ref[...] = jnp.broadcast_to(partial, send_ref.shape)


def turn(sweep, field_ref, alpha_ref, state_ref, search_ref):
    alpha = alpha_ref[0:1, 0:1]
    direction = field_ref[...] * (1.0 / alpha)
    if sweep == 0:
        return direction, direction, state_ref[0:1, 0:1], alpha
    phi_bar, rho, cosine, sine = [state_ref[0:1, i : i + 1] for i in range(1, 5)]
    return direction, direction - (sine * alpha / rho) * search_ref[...], phi_bar, -cosine * alpha


def model_kernel(sweep, *refs):
    received_ref, scatter_ref, gather_ref, field_ref, alpha_ref, state_ref = refs[:6]
    search_ref, update_ref = refs[6:8] if sweep else (None, None)
    send_ref, field_out, state_out, search_out, update_out, stage_ref = refs[-6:]
    received = received_ref[...]
    gathered = unstacked(matmul(scatter_ref[...], received)).astype(BF16).astype(F32)
    stage_ref[...] = received.astype(F32)
    first = row_of(stage_ref, NORM_ROW)[...]
    beta = norm_of(first)
    lower = [row_of(stage_ref, ID_ROW)[...], jnp.where(iota(first.shape, 1) < 2, 0.0, first)]
    rough = [(row_of(stage_ref, CELL_ROW + j)[...] + lower[j]).T for j in range(2)]
    direction, search, phi_bar, rho_bar = turn(sweep, field_ref, alpha_ref, state_ref, search_ref)
    field = (gathered + jnp.concatenate(rough, axis=1)) * (1.0 / beta) - beta * direction
    field_out[...] = field
    send_field(send_ref, stage_ref, gathered, field, gather_ref)
    rho = jnp.sqrt(rho_bar * rho_bar + beta * beta)
    cosine, sine = rho_bar / rho, beta / rho
    state_out[...] = scalars_row(beta, sine * phi_bar, rho, cosine, sine)
    search_out[...] = search
    update = (cosine * phi_bar / rho) * search
    update_out[...] = update_ref[...] + update if sweep else update


def last_kernel(norms_ref, data_ref, field_ref, alpha_ref, state_ref, search_ref, update_ref, update_out, data_out):
    squares = jnp.sum(norms_ref[...], axis=0, keepdims=True)[:, 0:1]
    _, search, phi_bar, rho_bar = turn(ITERS - 1, field_ref, alpha_ref, state_ref, search_ref)
    step = rho_bar * phi_bar / (rho_bar * rho_bar + squares)
    update_out[...] = update_ref[...] + step * search
    data_out[...] = data_ref[...] * (1.0 / jnp.sqrt(squares))


def call(kernel, name, outputs, scratch, operands, flops=0, space=pltpu.VMEM):
    bytes_accessed = sum(x.size * x.dtype.itemsize for x in operands)
    return pl.pallas_call(
        kernel,
        name=name,
        out_shape=[jax.ShapeDtypeStruct(shape, dtype) for shape, dtype in outputs],
        in_specs=[pl.BlockSpec(memory_space=space)] * len(operands),
        out_specs=[pl.BlockSpec(memory_space=pltpu.VMEM)] * len(outputs),
        scratch_shapes=scratch,
        compiler_params=pltpu.CompilerParams(vmem_limit_bytes=12 << 20),
        cost_estimate=pl.CostEstimate(flops=flops, bytes_accessed=bytes_accessed, transcendentals=0),
    )(*operands)


def exchange(packed, devices):
    rows, lanes = packed.shape
    chunks = packed.reshape(devices, rows // devices, lanes)
    return lax.all_to_all(chunks, AXES, split_axis=0, concat_axis=0, tiled=True).reshape(rows, lanes)


def body(kernel, target_device, target_block, counts, traveltimes, prior_residual):
    rads = lax.axis_size("rad")
    devices = lax.axis_size("lat") * rads
    ray_blocks, fanout, ray_len, cells = kernel.shape
    entries = ray_blocks * fanout
    rows = devices * CHUNK
    blocks = MB_R * MB_L
    flops = 4 * entries * ray_len * cells

    packet = ((rows, LANES), BF16)
    ray = ((ray_blocks, ray_len), F32)
    model = ((blocks, cells), F32)
    scalar = ((8, LANES), F32)
    partials = pltpu.VMEM((entries, cells), F32)

    stage = pltpu.VMEM((rows, LANES), F32)
    send, tiles, weights, data, place, pick = call(
        start_kernel, "start",
        [packet, ((entries * ray_len, cells), BF16), ray, ray,
         ((rows, 2 * entries), BF16), ((2 * entries, rows), BF16)],
        [
            pltpu.VMEM((fanout, ray_blocks), jnp.int32), pltpu.VMEM((fanout, ray_blocks), jnp.int32),
            pltpu.VMEM((1, ray_blocks), jnp.int32), pltpu.VMEM((ray_blocks, ray_len), F32),
            pltpu.VMEM((ray_blocks, ray_len), F32), partials, stage,
            pltpu.VMEM((2 * entries, fanout * ray_len), BF16),
            pltpu.SemaphoreType.DMA((5,)), pltpu.SemaphoreType.DMA,
        ],
        tuple(
            pltpu.with_memory_space_constraint(x, pltpu.HBM)
            for x in (kernel.reshape(entries * ray_len, cells), target_device.T, target_block.T,
                      counts.reshape(1, ray_blocks), traveltimes, prior_residual)
        ),
        flops, pltpu.HBM,
    )
    received = exchange(send, devices)
    send, field, state, gather, scatter = call(
        first_model_kernel, "first_model",
        [packet, model, scalar, ((rows, 2 * blocks), BF16), ((2 * blocks, rows), BF16)], [stage], (received,),
    )
    carried, kept = (), ()
    for sweep in range(ITERS):
        received = exchange(send, devices)
        if sweep == ITERS - 1:
            break
        send, data, cell_state, alpha = call(
            functools.partial(ray_kernel, sweep, rads), "ray",
            [packet, ray, ((3, 2 * devices, blocks), F32), scalar], [stage, partials, partials],
            (received, tiles, pick, weights, data, state, place) + kept, flops,
        )
        kept = (cell_state,)
        received = exchange(send, devices)
        send, field, state, *carried = call(
            functools.partial(model_kernel, sweep), "model", [packet, model, scalar, model, model], [stage],
            (received, scatter, gather, field, alpha, state, *carried), flops,
        )
    send, data, alpha = call(
        functools.partial(last_ray_kernel, ITERS - 1, rads), "last_ray", [((devices, LANES), F32), ray, scalar],
        [stage, partials], (received, tiles, pick, weights, data, state) + kept, flops,
    )
    norms = exchange(send, devices)
    update, data = call(last_kernel, "last", [model, ray], [], (norms, data, field, alpha, state, *carried))
    return (update.reshape(MB_R, MB_L, cells), data)


def solution(mesh):
    in_specs = (
        P(("lat", "rad"), None, None, None),
        P(("lat", "rad"), None),
        P(("lat", "rad"), None),
        P(("lat", "rad")),
        P(("lat", "rad"), None),
        P(("lat", "rad"), None),
    )
    out_specs = (P("rad", "lat", None), P(("lat", "rad"), None))
    return jax.shard_map(body, mesh=mesh, in_specs=in_specs, out_specs=out_specs, check_vma=False)
```

```python
import functools

import jax
import jax.numpy as jnp
from jax import lax
from jax.experimental import pallas as pl
from jax.experimental.pallas import tpu as pltpu
from jax.sharding import PartitionSpec as P

ITERS = 3
MB_R = 8
MB_L = 16
FREEDOM = 4.0
DAMPING = 0.3

AXES = ("lat", "rad")
CHUNK = 8
NORM_ROW = 4
ID_ROW = 5
CELL_ROW = 6
LANES = 128
GROUP = 8

F32 = jnp.float32
BF16 = jnp.bfloat16
NT = (((1,), (1,)), ((), ()))


def iota(shape, dim):
    return lax.broadcasted_iota(jnp.int32, shape, dim)


def low(index, size):
    assert size & (size - 1) == 0
    return index & (size - 1)


def high(index, size):
    assert size & (size - 1) == 0
    return lax.shift_right_logical(index, jnp.int32(size.bit_length() - 1))


def matmul(a, b):
    return jnp.dot(a, b, preferred_element_type=F32)


def total(x):
    return jnp.sum(jnp.sum(x, axis=1, keepdims=True), axis=0, keepdims=True)


def ones_where(condition):
    return jnp.where(condition, 1.0, 0.0).astype(BF16)


def norm_row(partial, rest):
    upper = partial.astype(BF16).astype(F32)
    lane = iota(rest.shape, 1)
    return jnp.where(lane == 0, upper, jnp.where(lane == 1, partial - upper, rest))


def norm_of(sums):
    sums = jnp.where(iota(sums.shape, 1) < 2, sums, 0.0)
    return jnp.sqrt(total(sums))


def row_of(ref, j):
    return ref.at[pl.ds(j, ref.shape[0] // CHUNK, stride=CHUNK), :]


def pack(send_ref, stage_ref, named, *rest):
    for j, rows in enumerate(rest):
        row_of(stage_ref, NORM_ROW + j)[...] = rows
    data = low(iota(named.shape, 0), CHUNK) < NORM_ROW
    send_ref[...] = jnp.where(data, named, stage_ref[...]).astype(BF16)


def stacked(x):
    return jnp.concatenate([x[:, :LANES], x[:, LANES:]], axis=0)


def unstacked(x):
    half = x.shape[0] // 2
    return jnp.concatenate([x[:half], x[half:]], axis=1)


def forward_group(tiles_ref, blocks_ref, start, count, fanout, ray_len):
    lane = iota((ray_len, LANES), 1)
    sums = jnp.zeros((ray_len, LANES), F32)
    for i in range(count):
        products = None
        for e in range((start + i) * fanout, (start + i + 1) * fanout):
            product = tiles_ref[e * ray_len : (e + 1) * ray_len, :].astype(F32) * blocks_ref[e : e + 1, :]
            product = product[:, :LANES] + product[:, LANES:]
            products = product if products is None else products + product
        sums = jnp.where(lane == i, jnp.sum(products, axis=1, keepdims=True), sums)
    return sums.T[:count]


def spread_rows(y, fanout):
    upper = y.astype(BF16).astype(F32)
    lower = y - upper
    upper = jnp.concatenate([upper] * fanout, axis=1)
    lower = jnp.concatenate([lower] * fanout, axis=1)
    count, width = upper.shape
    row, lane = iota((2 * fanout, width), 0), iota((2 * fanout, width), 1)
    own = high(lane, width // fanout) == low(row, fanout)
    return [
        jnp.where(own, jnp.where(row < fanout, upper[i : i + 1], lower[i : i + 1]), 0.0) for i in range(count)
    ]


def adjoint_products(tiles_ref, lhs, out_ref, b, fanout):
    width = lhs.shape[1]
    both = matmul(lhs, tiles_ref[b * width : (b + 1) * width, :])
    out_ref[b * fanout : (b + 1) * fanout, :] = both[:fanout] + both[fanout:]


def adjoint_group(tiles_ref, y, out_ref, start, fanout):
    for i, lhs in enumerate(spread_rows(y, fanout)):
        adjoint_products(tiles_ref, lhs.astype(BF16), out_ref, start + i, fanout)


def write_links(ref, blocks):
    source, block = iota((blocks, blocks), 0), iota((blocks, blocks), 1)
    place = low(block, MB_L)
    links = (
        (source == block - MB_L) | (source == block + MB_L)
        | ((source == block - 1) & (place > 0)) | ((source == block + 1) & (place < MB_L - 1)),
        source == block + blocks - MB_L,
        source == block - blocks + MB_L,
        (source == block + MB_L - 1) & (place == 0),
        (source == block - MB_L + 1) & (place == MB_L - 1),
    )
    for i, link in enumerate(links):
        for part in range(3):
            ref[part * blocks : (part + 1) * blocks, i * blocks : (i + 1) * blocks] = ones_where(link)


def roughen(cells, links_ref, rads):
    rows, blocks = cells.shape
    devices = rows // 2
    upper = cells.astype(BF16)
    rest = cells - upper.astype(F32)
    middle = rest.astype(BF16)
    lower = (rest - middle.astype(F32)).astype(BF16)
    sums = matmul(jnp.concatenate([upper, middle, lower], axis=1), links_ref[...])
    device = low(iota(cells.shape, 0), devices)
    rad = low(device, rads)
    piece = lambda i, step: pltpu.roll(sums[:, i * blocks : (i + 1) * blocks], step % rows, 0)
    beside = sums[:, :blocks]
    beside = beside + jnp.where(rad > 0, piece(1, 1), 0.0)
    beside = beside + jnp.where(rad < rads - 1, piece(2, -1), 0.0)
    beside = beside + jnp.where(device >= rads, piece(3, rads), 0.0)
    beside = beside + jnp.where(device < devices - rads, piece(4, -rads), 0.0)
    return 4.0 * cells - beside


def scalars_row(*values):
    lane = iota((8, LANES), 1)
    out = jnp.zeros((8, LANES), F32)
    for i, value in enumerate(values):
        out = jnp.where(lane == i, value, out)
    return out


def start_kernel(
    kernel_hbm, device_hbm, block_hbm, counts_hbm, times_hbm, prior_hbm,
    send_ref, tiles_ref, weights_ref, data_ref, place_ref, pick_ref, links_ref,
    device_ref, block_ref, counts_ref, times_ref, prior_ref, partial_ref, stage_ref, operand_ref, small_sem, tile_sem,
):
    fanout, ray_blocks = device_ref.shape
    ray_len = times_ref.shape[1]
    entries = ray_blocks * fanout
    rows = send_ref.shape[0]
    devices = rows // CHUNK

    small = [
        pltpu.make_async_copy(source, target, small_sem.at[i])
        for i, (source, target) in enumerate(
            ((device_hbm, device_ref), (block_hbm, block_ref), (counts_hbm, counts_ref),
             (times_hbm, times_ref), (prior_hbm, prior_ref))
        )
    ]
    large = pltpu.make_async_copy(kernel_hbm, tiles_ref, tile_sem)
    for copy in small + [large]:
        copy.start()
    write_links(links_ref, links_ref.shape[0] // 3)
    for copy in small:
        copy.wait()

    member = ones_where(high(iota((entries, ray_blocks), 0), fanout) == iota((entries, ray_blocks), 1))
    turn = low(iota((entries, fanout), 0), fanout) == iota((entries, fanout), 1)

    def column(table_ref):
        table = table_ref[...].astype(F32).astype(BF16)
        spread = lax.dot_general(member, table, NT, preferred_element_type=F32)
        return jnp.sum(jnp.where(turn, spread, 0.0), axis=1, keepdims=True)

    diagonal = iota((entries, entries), 0) == iota((entries, entries), 1)

    def as_row(col):
        return jnp.sum(jnp.where(diagonal, col, 0.0), axis=0, keepdims=True)

    target = column(device_ref)
    block = column(block_ref)
    target_row = as_row(target)
    earlier = iota((entries, entries), 1) < iota((entries, entries), 0)
    rank = jnp.sum(jnp.where(earlier & (target == target_row), 1.0, 0.0), axis=1, keepdims=True)
    first = target * CHUNK + 2.0 * rank
    to_col = first.astype(jnp.int32)
    to_row = as_row(first).astype(jnp.int32)
    for half in range(2):
        here = slice(half * entries, (half + 1) * entries)
        pick_ref[here, :] = ones_where(iota((entries, rows), 1) == to_col + half)
        place_ref[:, here] = ones_where(iota((rows, entries), 0) == to_row + half)

    same = iota((ray_blocks, ray_blocks), 0) == iota((ray_blocks, ray_blocks), 1)
    counts = jnp.sum(jnp.where(same, counts_ref[...].astype(F32), 0.0), axis=1, keepdims=True)
    mask = jnp.where(iota((ray_blocks, ray_len), 1).astype(F32) < counts, 1.0, 0.0)
    prior = prior_ref[...]
    weights = mask * jnp.sqrt((FREEDOM + 1.0) / (FREEDOM + prior * prior))
    weights_ref[...] = weights
    data = weights * times_ref[...]
    data_ref[...] = data

    operands = spread_rows(weights * data, fanout)
    depth = 2 * fanout
    for b in range(0, ray_blocks, 2):
        operand_ref[b * depth : (b + 2) * depth, :] = jnp.concatenate(operands[b : b + 2], axis=0).astype(BF16)
    ids = jnp.where(iota((entries, LANES), 1).astype(F32) == rank, block + 1.0, 0.0).astype(BF16)
    named_by = ones_where(iota((devices, entries), 0).astype(F32) == target_row)
    zeros = jnp.zeros((devices, LANES), F32)
    rest = norm_row(total(data * data), zeros), matmul(named_by, ids), zeros, zeros
    for j, rows_of in enumerate(rest):
        row_of(stage_ref, NORM_ROW + j)[...] = rows_of
    large.wait()
    for b in range(ray_blocks):
        adjoint_products(tiles_ref, operand_ref[b * depth : (b + 1) * depth, :], partial_ref, b, fanout)
    pack(send_ref, stage_ref, matmul(place_ref[...], stacked(partial_ref[...].astype(BF16))))


def send_field(send_ref, stage_ref, gathered, field, gather_ref):
    cells = [gathered[:, half * LANES : (half + 1) * LANES].T for half in range(2)]
    zeros = jnp.zeros(cells[0].shape, F32)
    norms = norm_row(total(field * field), zeros)
    pack(send_ref, stage_ref, matmul(gather_ref[...], stacked(field).astype(BF16)), norms, zeros, *cells)


def first_model_kernel(received_ref, send_ref, field_ref, state_ref, gather_ref, scatter_ref, stage_ref):
    received = received_ref[...]
    rows = received.shape[0]
    blocks = MB_R * MB_L
    stage_ref[...] = received.astype(F32)
    beta = norm_of(row_of(stage_ref, NORM_ROW)[...])
    ids = row_of(stage_ref, ID_ROW)[...]
    for j in range(CHUNK):
        ident = ids[:, j // 2 : j // 2 + 1] if j < NORM_ROW else 0.0
        row_of(stage_ref, j)[...] = jnp.broadcast_to(ident, ids.shape)
    hit = stage_ref[...] - 1.0 == iota((rows, LANES), 1).astype(F32)
    odd = low(iota((rows, LANES), 0), 2)
    for half in range(2):
        here = slice(half * blocks, (half + 1) * blocks)
        chosen = jnp.where(hit & (odd == half), 1.0, 0.0)
        gather_ref[:, here] = chosen.astype(BF16)
        scatter_ref[here, :] = chosen.T.astype(BF16)

    gathered = unstacked(matmul(scatter_ref[...], received)).astype(BF16).astype(F32)
    field = gathered * (1.0 / beta)
    field_ref[...] = field
    state_ref[...] = scalars_row(beta)
    send_field(send_ref, stage_ref, gathered, field, gather_ref)


def ray_step(
    sweep, rads, received_ref, tiles_ref, pick_ref, links_ref, weights_ref, data_ref, state_ref, cells_ref,
    data_out, alpha_out,
    stage_ref, blocks_ref, partial_ref=None,
):
    received = received_ref[...]
    ray_blocks, ray_len = data_ref.shape
    devices = received.shape[0] // CHUNK
    fanout = blocks_ref.shape[0] // ray_blocks
    blocks_ref[...] = unstacked(matmul(pick_ref[...], received))
    stage_ref[...] = received.astype(F32)
    alpha = norm_of(row_of(stage_ref, NORM_ROW)[...])
    alpha_out[...] = scalars_row(alpha)
    beta = state_ref[0:1, 0:1]
    inverse_alpha, inverse_beta = 1.0 / alpha, 1.0 / beta
    ratio = alpha / beta

    waiting = None
    for start in range(0, ray_blocks, GROUP):
        here = slice(start, start + GROUP)
        products = forward_group(tiles_ref, blocks_ref, start, GROUP, fanout, ray_len)
        weights = weights_ref[here, :]
        data = weights * (products * inverse_alpha) - ratio * data_ref[here, :]
        data_out[here, :] = data
        if partial_ref is not None:
            if waiting is not None:
                adjoint_group(tiles_ref, waiting[0], partial_ref, waiting[1], fanout)
            waiting = weights * data, start
    if partial_ref is not None:
        adjoint_group(tiles_ref, waiting[0], partial_ref, waiting[1], fanout)

    data = data_out[...]
    cell = jnp.concatenate([row_of(stage_ref, CELL_ROW + j)[...] for j in range(2)], axis=0)
    if sweep:
        direction = ((cell + cells_ref[0]) * inverse_beta - beta * cells_ref[1]) * inverse_alpha
        pen = DAMPING * roughen(direction, links_ref, rads) - ratio * cells_ref[2]
    else:
        direction = (cell * inverse_beta) * inverse_alpha
        pen = DAMPING * roughen(direction, links_ref, rads)
    return total(data * data) + total(pen * pen), pen, direction


def ray_kernel(sweep, rads, *refs):
    inputs, place_ref = refs[:7], refs[7]
    links_ref = inputs[3]
    cells_ref = refs[8] if sweep else None
    send_ref, data_out, cells_out, alpha_out, stage_ref, blocks_ref, partial_ref = refs[-7:]
    partial, pen, direction = ray_step(
        sweep, rads, *inputs, cells_ref, data_out, alpha_out, stage_ref, blocks_ref, partial_ref
    )
    rough = DAMPING * roughen(pen, links_ref, rads)
    for i, kept in enumerate((rough, direction, pen)):
        cells_out[i] = kept
    upper = rough.astype(BF16).astype(F32)
    lower = rough - upper
    half = rough.shape[0] // 2
    pack(
        send_ref, stage_ref, matmul(place_ref[...], stacked(partial_ref[...]).astype(BF16)),
        norm_row(partial, lower[half:]), lower[:half], upper[:half], upper[half:],
    )


def last_ray_kernel(sweep, rads, *refs):
    send_ref, data_out, alpha_out, stage_ref, blocks_ref = refs[-5:]
    partial, _, _ = ray_step(sweep, rads, *refs[:-5], data_out, alpha_out, stage_ref, blocks_ref)
    send_ref[...] = jnp.broadcast_to(partial, send_ref.shape)


def turn(sweep, field_ref, alpha_ref, state_ref, search_ref):
    alpha = alpha_ref[0:1, 0:1]
    direction = field_ref[...] * (1.0 / alpha)
    if sweep == 0:
        return direction, direction, state_ref[0:1, 0:1], alpha
    phi_bar, rho, cosine, sine = [state_ref[0:1, i : i + 1] for i in range(1, 5)]
    return direction, direction - (sine * alpha / rho) * search_ref[...], phi_bar, -cosine * alpha


def model_kernel(sweep, *refs):
    received_ref, scatter_ref, gather_ref, field_ref, alpha_ref, state_ref = refs[:6]
    search_ref, update_ref = refs[6:8] if sweep else (None, None)
    send_ref, field_out, state_out, search_out, update_out, stage_ref = refs[-6:]
    received = received_ref[...]
    gathered = unstacked(matmul(scatter_ref[...], received)).astype(BF16).astype(F32)
    stage_ref[...] = received.astype(F32)
    first = row_of(stage_ref, NORM_ROW)[...]
    beta = norm_of(first)
    lower = [row_of(stage_ref, ID_ROW)[...], jnp.where(iota(first.shape, 1) < 2, 0.0, first)]
    rough = [(row_of(stage_ref, CELL_ROW + j)[...] + lower[j]).T for j in range(2)]
    direction, search, phi_bar, rho_bar = turn(sweep, field_ref, alpha_ref, state_ref, search_ref)
    field = (gathered + jnp.concatenate(rough, axis=1)) * (1.0 / beta) - beta * direction
    field_out[...] = field
    send_field(send_ref, stage_ref, gathered, field, gather_ref)
    rho = jnp.sqrt(rho_bar * rho_bar + beta * beta)
    cosine, sine = rho_bar / rho, beta / rho
    state_out[...] = scalars_row(beta, sine * phi_bar, rho, cosine, sine)
    search_out[...] = search
    update = (cosine * phi_bar / rho) * search
    update_out[...] = update_ref[...] + update if sweep else update


def last_kernel(norms_ref, data_ref, field_ref, alpha_ref, state_ref, search_ref, update_ref, update_out, data_out):
    squares = jnp.sum(norms_ref[...], axis=0, keepdims=True)[:, 0:1]
    _, search, phi_bar, rho_bar = turn(ITERS - 1, field_ref, alpha_ref, state_ref, search_ref)
    step = rho_bar * phi_bar / (rho_bar * rho_bar + squares)
    update_out[...] = update_ref[...] + step * search
    data_out[...] = data_ref[...] * (1.0 / jnp.sqrt(squares))


def call(kernel, name, outputs, scratch, operands, flops=0, space=pltpu.VMEM):
    bytes_accessed = sum(x.size * x.dtype.itemsize for x in operands)
    return pl.pallas_call(
        kernel,
        name=name,
        out_shape=[jax.ShapeDtypeStruct(shape, dtype) for shape, dtype in outputs],
        in_specs=[pl.BlockSpec(memory_space=space)] * len(operands),
        out_specs=[pl.BlockSpec(memory_space=pltpu.VMEM)] * len(outputs),
        scratch_shapes=scratch,
        compiler_params=pltpu.CompilerParams(vmem_limit_bytes=12 << 20),
        cost_estimate=pl.CostEstimate(flops=flops, bytes_accessed=bytes_accessed, transcendentals=0),
    )(*operands)


def exchange(packed, devices):
    rows, lanes = packed.shape
    chunks = packed.reshape(devices, rows // devices, lanes)
    return lax.all_to_all(chunks, AXES, split_axis=0, concat_axis=0, tiled=True).reshape(rows, lanes)


def body(kernel, target_device, target_block, counts, traveltimes, prior_residual):
    rads = lax.axis_size("rad")
    devices = lax.axis_size("lat") * rads
    ray_blocks, fanout, ray_len, cells = kernel.shape
    entries = ray_blocks * fanout
    rows = devices * CHUNK
    blocks = MB_R * MB_L
    flops = 4 * entries * ray_len * cells

    packet = ((rows, LANES), BF16)
    ray = ((ray_blocks, ray_len), F32)
    model = ((blocks, cells), F32)
    scalar = ((8, LANES), F32)
    partials = pltpu.VMEM((entries, cells), F32)

    stage = pltpu.VMEM((rows, LANES), F32)
    send, tiles, weights, data, place, pick, links = call(
        start_kernel, "start",
        [packet, ((entries * ray_len, cells), BF16), ray, ray,
         ((rows, 2 * entries), BF16), ((2 * entries, rows), BF16), ((3 * blocks, 5 * blocks), BF16)],
        [
            pltpu.VMEM((fanout, ray_blocks), jnp.int32), pltpu.VMEM((fanout, ray_blocks), jnp.int32),
            pltpu.VMEM((1, ray_blocks), jnp.int32), pltpu.VMEM((ray_blocks, ray_len), F32),
            pltpu.VMEM((ray_blocks, ray_len), F32), partials, stage,
            pltpu.VMEM((2 * entries, fanout * ray_len), BF16),
            pltpu.SemaphoreType.DMA((5,)), pltpu.SemaphoreType.DMA,
        ],
        tuple(
            pltpu.with_memory_space_constraint(x, pltpu.HBM)
            for x in (kernel.reshape(entries * ray_len, cells), target_device.T, target_block.T,
                      counts.reshape(1, ray_blocks), traveltimes, prior_residual)
        ),
        flops, pltpu.HBM,
    )
    received = exchange(send, devices)
    send, field, state, gather, scatter = call(
        first_model_kernel, "first_model",
        [packet, model, scalar, ((rows, 2 * blocks), BF16), ((2 * blocks, rows), BF16)], [stage], (received,),
    )
    carried, kept = (), ()
    for sweep in range(ITERS):
        received = exchange(send, devices)
        if sweep == ITERS - 1:
            break
        send, data, cell_state, alpha = call(
            functools.partial(ray_kernel, sweep, rads), "ray",
            [packet, ray, ((3, 2 * devices, blocks), F32), scalar], [stage, partials, partials],
            (received, tiles, pick, links, weights, data, state, place) + kept, flops,
        )
        kept = (cell_state,)
        received = exchange(send, devices)
        send, field, state, *carried = call(
            functools.partial(model_kernel, sweep), "model", [packet, model, scalar, model, model], [stage],
            (received, scatter, gather, field, alpha, state, *carried), flops,
        )
    send, data, alpha = call(
        functools.partial(last_ray_kernel, ITERS - 1, rads), "last_ray", [((devices, LANES), F32), ray, scalar],
        [stage, partials], (received, tiles, pick, links, weights, data, state) + kept, flops,
    )
    norms = exchange(send, devices)
    update, data = call(last_kernel, "last", [model, ray], [], (norms, data, field, alpha, state, *carried))
    return (update.reshape(MB_R, MB_L, cells), data)


def solution(mesh):
    in_specs = (
        P(("lat", "rad"), None, None, None),
        P(("lat", "rad"), None),
        P(("lat", "rad"), None),
        P(("lat", "rad")),
        P(("lat", "rad"), None),
        P(("lat", "rad"), None),
    )
    out_specs = (P("rad", "lat", None), P(("lat", "rad"), None))
    return jax.shard_map(body, mesh=mesh, in_specs=in_specs, out_specs=out_specs, check_vma=False)
```

```python
import functools

import jax
import jax.numpy as jnp
from jax import lax
from jax.experimental import pallas as pl
from jax.experimental.pallas import tpu as pltpu
from jax.sharding import PartitionSpec as P

ITERS = 3
MB_R = 8
MB_L = 16
FREEDOM = 4.0
DAMPING = 0.3

AXES = ("lat", "rad")
CHUNK = 8
NORM_ROW = 4
ID_ROW = 5
CELL_ROW = 6
LANES = 128
GROUP = 8

F32 = jnp.float32
BF16 = jnp.bfloat16
NT = (((1,), (1,)), ((), ()))


def iota(shape, dim):
    return lax.broadcasted_iota(jnp.int32, shape, dim)


def low(index, size):
    assert size & (size - 1) == 0
    return index & (size - 1)


def high(index, size):
    assert size & (size - 1) == 0
    return lax.shift_right_logical(index, jnp.int32(size.bit_length() - 1))


def matmul(a, b):
    return jnp.dot(a, b, preferred_element_type=F32)


def total(x):
    return jnp.sum(jnp.sum(x, axis=1, keepdims=True), axis=0, keepdims=True)


def ones_where(condition):
    return jnp.where(condition, 1.0, 0.0).astype(BF16)


def norm_row(partial, rest):
    upper = partial.astype(BF16).astype(F32)
    lane = iota(rest.shape, 1)
    return jnp.where(lane == 0, upper, jnp.where(lane == 1, partial - upper, rest))


def norm_of(sums):
    sums = jnp.where(iota(sums.shape, 1) < 2, sums, 0.0)
    return jnp.sqrt(total(sums))


def row_of(ref, j):
    return ref.at[pl.ds(j, ref.shape[0] // CHUNK, stride=CHUNK), :]


def pack(send_ref, stage_ref, named, *rest):
    for j, rows in enumerate(rest):
        row_of(stage_ref, NORM_ROW + j)[...] = rows
    data = low(iota(named.shape, 0), CHUNK) < NORM_ROW
    send_ref[...] = jnp.where(data, named, stage_ref[...]).astype(BF16)


def stacked(x):
    return jnp.concatenate([x[:, :LANES], x[:, LANES:]], axis=0)


def unstacked(x):
    half = x.shape[0] // 2
    return jnp.concatenate([x[:half], x[half:]], axis=1)


def forward_group(tiles_ref, blocks_ref, start, count, fanout, ray_len):
    lane = iota((ray_len, LANES), 1)
    sums = jnp.zeros((ray_len, LANES), F32)
    for i in range(count):
        products = None
        for e in range((start + i) * fanout, (start + i + 1) * fanout):
            product = tiles_ref[e * ray_len : (e + 1) * ray_len, :].astype(F32) * blocks_ref[e : e + 1, :]
            product = product[:, :LANES] + product[:, LANES:]
            products = product if products is None else products + product
        sums = jnp.where(lane == i, jnp.sum(products, axis=1, keepdims=True), sums)
    return sums.T[:count]


def spread_rows(y, fanout):
    upper = y.astype(BF16).astype(F32)
    lower = y - upper
    upper = jnp.concatenate([upper] * fanout, axis=1)
    lower = jnp.concatenate([lower] * fanout, axis=1)
    count, width = upper.shape
    row, lane = iota((2 * fanout, width), 0), iota((2 * fanout, width), 1)
    own = high(lane, width // fanout) == low(row, fanout)
    return [
        jnp.where(own, jnp.where(row < fanout, upper[i : i + 1], lower[i : i + 1]), 0.0) for i in range(count)
    ]


def adjoint_products(tiles_ref, lhs, out_ref, b, fanout):
    width = lhs.shape[1]
    both = matmul(lhs, tiles_ref[b * width : (b + 1) * width, :])
    out_ref[b * fanout : (b + 1) * fanout, :] = both[:fanout] + both[fanout:]


def adjoint_group(tiles_ref, y, out_ref, start, fanout):
    for i, lhs in enumerate(spread_rows(y, fanout)):
        adjoint_products(tiles_ref, lhs.astype(BF16), out_ref, start + i, fanout)


def write_links(ref, blocks):
    source, block = iota((blocks, blocks), 0), iota((blocks, blocks), 1)
    place = low(block, MB_L)
    links = (
        (source == block - MB_L) | (source == block + MB_L)
        | ((source == block - 1) & (place > 0)) | ((source == block + 1) & (place < MB_L - 1)),
        source == block + blocks - MB_L,
        source == block - blocks + MB_L,
        (source == block + MB_L - 1) & (place == 0),
        (source == block - MB_L + 1) & (place == MB_L - 1),
    )
    for i, link in enumerate(links):
        for part in range(3):
            ref[part * blocks : (part + 1) * blocks, i * blocks : (i + 1) * blocks] = ones_where(link)


def roughen(cells, links_ref, rads):
    rows, blocks = cells.shape
    devices = rows // 2
    device, block = low(iota(cells.shape, 0), devices), iota(cells.shape, 1)
    rad, place = low(device, rads), low(block, MB_L)
    owner = lambda x, step: pltpu.roll(x, step % rows, 0)
    lanes = lambda step: pltpu.roll(cells, step % blocks, 1)
    if links_ref is None:
        up, down = lanes(MB_L), lanes(-MB_L)
        left, right = lanes(1 - MB_L), lanes(MB_L - 1)
        north = jnp.where(block >= MB_L, up, jnp.where(rad > 0, owner(up, 1), 0.0))
        south = jnp.where(block < blocks - MB_L, down, jnp.where(rad < rads - 1, owner(down, -1), 0.0))
        west = jnp.where(place > 0, lanes(1), jnp.where(device >= rads, owner(left, rads), 0.0))
        east = jnp.where(place < MB_L - 1, lanes(-1), jnp.where(device < devices - rads, owner(right, -rads), 0.0))
        return 4.0 * cells - (south + north + east + west)
    upper = cells.astype(BF16)
    rest = cells - upper.astype(F32)
    middle = rest.astype(BF16)
    lower = (rest - middle.astype(F32)).astype(BF16)
    sums = matmul(jnp.concatenate([upper, middle, lower], axis=1), links_ref[...])
    piece = lambda i, step: owner(sums[:, i * blocks : (i + 1) * blocks], step)
    beside = sums[:, :blocks]
    beside = beside + jnp.where(rad > 0, piece(1, 1), 0.0)
    beside = beside + jnp.where(rad < rads - 1, piece(2, -1), 0.0)
    beside = beside + jnp.where(device >= rads, piece(3, rads), 0.0)
    beside = beside + jnp.where(device < devices - rads, piece(4, -rads), 0.0)
    return 4.0 * cells - beside


def scalars_row(*values):
    lane = iota((8, LANES), 1)
    out = jnp.zeros((8, LANES), F32)
    for i, value in enumerate(values):
        out = jnp.where(lane == i, value, out)
    return out


def start_kernel(
    kernel_hbm, device_hbm, block_hbm, counts_hbm, times_hbm, prior_hbm,
    send_ref, tiles_ref, weights_ref, data_ref, place_ref, pick_ref, links_ref,
    device_ref, block_ref, counts_ref, times_ref, prior_ref, partial_ref, stage_ref, operand_ref, small_sem, tile_sem,
):
    fanout, ray_blocks = device_ref.shape
    ray_len = times_ref.shape[1]
    entries = ray_blocks * fanout
    rows = send_ref.shape[0]
    devices = rows // CHUNK

    small = [
        pltpu.make_async_copy(source, target, small_sem.at[i])
        for i, (source, target) in enumerate(
            ((device_hbm, device_ref), (block_hbm, block_ref), (counts_hbm, counts_ref),
             (times_hbm, times_ref), (prior_hbm, prior_ref))
        )
    ]
    large = pltpu.make_async_copy(kernel_hbm, tiles_ref, tile_sem)
    for copy in small + [large]:
        copy.start()
    write_links(links_ref, links_ref.shape[0] // 3)
    for copy in small:
        copy.wait()

    member = ones_where(high(iota((entries, ray_blocks), 0), fanout) == iota((entries, ray_blocks), 1))
    turn = low(iota((entries, fanout), 0), fanout) == iota((entries, fanout), 1)

    def column(table_ref):
        table = table_ref[...].astype(F32).astype(BF16)
        spread = lax.dot_general(member, table, NT, preferred_element_type=F32)
        return jnp.sum(jnp.where(turn, spread, 0.0), axis=1, keepdims=True)

    diagonal = iota((entries, entries), 0) == iota((entries, entries), 1)

    def as_row(col):
        return jnp.sum(jnp.where(diagonal, col, 0.0), axis=0, keepdims=True)

    target = column(device_ref)
    block = column(block_ref)
    target_row = as_row(target)
    earlier = iota((entries, entries), 1) < iota((entries, entries), 0)
    rank = jnp.sum(jnp.where(earlier & (target == target_row), 1.0, 0.0), axis=1, keepdims=True)
    first = target * CHUNK + 2.0 * rank
    to_col = first.astype(jnp.int32)
    to_row = as_row(first).astype(jnp.int32)
    for half in range(2):
        here = slice(half * entries, (half + 1) * entries)
        pick_ref[here, :] = ones_where(iota((entries, rows), 1) == to_col + half)
        place_ref[:, here] = ones_where(iota((rows, entries), 0) == to_row + half)

    same = iota((ray_blocks, ray_blocks), 0) == iota((ray_blocks, ray_blocks), 1)
    counts = jnp.sum(jnp.where(same, counts_ref[...].astype(F32), 0.0), axis=1, keepdims=True)
    mask = jnp.where(iota((ray_blocks, ray_len), 1).astype(F32) < counts, 1.0, 0.0)
    prior = prior_ref[...]
    weights = mask * jnp.sqrt((FREEDOM + 1.0) / (FREEDOM + prior * prior))
    weights_ref[...] = weights
    data = weights * times_ref[...]
    data_ref[...] = data

    operands = spread_rows(weights * data, fanout)
    depth = 2 * fanout
    for b in range(0, ray_blocks, 2):
        operand_ref[b * depth : (b + 2) * depth, :] = jnp.concatenate(operands[b : b + 2], axis=0).astype(BF16)
    ids = jnp.where(iota((entries, LANES), 1).astype(F32) == rank, block + 1.0, 0.0).astype(BF16)
    named_by = ones_where(iota((devices, entries), 0).astype(F32) == target_row)
    zeros = jnp.zeros((devices, LANES), F32)
    rest = norm_row(total(data * data), zeros), matmul(named_by, ids), zeros, zeros
    for j, rows_of in enumerate(rest):
        row_of(stage_ref, NORM_ROW + j)[...] = rows_of
    large.wait()
    for b in range(ray_blocks):
        adjoint_products(tiles_ref, operand_ref[b * depth : (b + 1) * depth, :], partial_ref, b, fanout)
    pack(send_ref, stage_ref, matmul(place_ref[...], stacked(partial_ref[...].astype(BF16))))


def send_field(send_ref, stage_ref, gathered, field, gather_ref):
    cells = [gathered[:, half * LANES : (half + 1) * LANES].T for half in range(2)]
    zeros = jnp.zeros(cells[0].shape, F32)
    norms = norm_row(total(field * field), zeros)
    pack(send_ref, stage_ref, matmul(gather_ref[...], stacked(field).astype(BF16)), norms, zeros, *cells)


def first_model_kernel(received_ref, send_ref, field_ref, state_ref, gather_ref, scatter_ref, stage_ref):
    received = received_ref[...]
    rows = received.shape[0]
    blocks = MB_R * MB_L
    stage_ref[...] = received.astype(F32)
    beta = norm_of(row_of(stage_ref, NORM_ROW)[...])
    ids = row_of(stage_ref, ID_ROW)[...]
    for j in range(CHUNK):
        ident = ids[:, j // 2 : j // 2 + 1] if j < NORM_ROW else 0.0
        row_of(stage_ref, j)[...] = jnp.broadcast_to(ident, ids.shape)
    hit = stage_ref[...] - 1.0 == iota((rows, LANES), 1).astype(F32)
    odd = low(iota((rows, LANES), 0), 2)
    for half in range(2):
        here = slice(half * blocks, (half + 1) * blocks)
        chosen = jnp.where(hit & (odd == half), 1.0, 0.0)
        gather_ref[:, here] = chosen.astype(BF16)
        scatter_ref[here, :] = chosen.T.astype(BF16)

    gathered = unstacked(matmul(scatter_ref[...], received)).astype(BF16).astype(F32)
    field = gathered * (1.0 / beta)
    field_ref[...] = field
    state_ref[...] = scalars_row(beta)
    send_field(send_ref, stage_ref, gathered, field, gather_ref)


def ray_step(
    sweep, rads, received_ref, tiles_ref, pick_ref, links_ref, weights_ref, data_ref, state_ref, cells_ref,
    data_out, alpha_out,
    stage_ref, blocks_ref, partial_ref=None,
):
    received = received_ref[...]
    ray_blocks, ray_len = data_ref.shape
    devices = received.shape[0] // CHUNK
    fanout = blocks_ref.shape[0] // ray_blocks
    blocks_ref[...] = unstacked(matmul(pick_ref[...], received))
    stage_ref[...] = received.astype(F32)
    alpha = norm_of(row_of(stage_ref, NORM_ROW)[...])
    alpha_out[...] = scalars_row(alpha)
    beta = state_ref[0:1, 0:1]
    inverse_alpha, inverse_beta = 1.0 / alpha, 1.0 / beta
    ratio = alpha / beta

    waiting = None
    for start in range(0, ray_blocks, GROUP):
        here = slice(start, start + GROUP)
        products = forward_group(tiles_ref, blocks_ref, start, GROUP, fanout, ray_len)
        weights = weights_ref[here, :]
        data = weights * (products * inverse_alpha) - ratio * data_ref[here, :]
        data_out[here, :] = data
        if partial_ref is not None:
            if waiting is not None:
                adjoint_group(tiles_ref, waiting[0], partial_ref, waiting[1], fanout)
            waiting = weights * data, start
    if partial_ref is not None:
        adjoint_group(tiles_ref, waiting[0], partial_ref, waiting[1], fanout)

    data = data_out[...]
    cell = jnp.concatenate([row_of(stage_ref, CELL_ROW + j)[...] for j in range(2)], axis=0)
    if sweep:
        direction = ((cell + cells_ref[0]) * inverse_beta - beta * cells_ref[1]) * inverse_alpha
        pen = DAMPING * roughen(direction, links_ref, rads) - ratio * cells_ref[2]
    else:
        direction = (cell * inverse_beta) * inverse_alpha
        pen = DAMPING * roughen(direction, links_ref, rads)
    return total(data * data) + total(pen * pen), pen, direction


def ray_kernel(sweep, rads, *refs):
    received_ref, tiles_ref, pick_ref, weights_ref, data_ref, state_ref, place_ref = refs[:7]
    cells_ref = refs[7] if sweep else None
    send_ref, data_out, cells_out, alpha_out, stage_ref, blocks_ref, partial_ref = refs[-7:]
    partial, pen, direction = ray_step(
        sweep, rads, received_ref, tiles_ref, pick_ref, None, weights_ref, data_ref, state_ref, cells_ref, data_out, alpha_out, stage_ref, blocks_ref, partial_ref
    )
    rough = DAMPING * roughen(pen, None, rads)
    for i, kept in enumerate((rough, direction, pen)):
        cells_out[i] = kept
    upper = rough.astype(BF16).astype(F32)
    lower = rough - upper
    half = rough.shape[0] // 2
    pack(
        send_ref, stage_ref, matmul(place_ref[...], stacked(partial_ref[...]).astype(BF16)),
        norm_row(partial, lower[half:]), lower[:half], upper[:half], upper[half:],
    )


def last_ray_kernel(sweep, rads, *refs):
    send_ref, data_out, alpha_out, stage_ref, blocks_ref = refs[-5:]
    partial, _, _ = ray_step(sweep, rads, *refs[:-5], data_out, alpha_out, stage_ref, blocks_ref)
    send_ref[...] = jnp.broadcast_to(partial, send_ref.shape)


def turn(sweep, field_ref, alpha_ref, state_ref, search_ref):
    alpha = alpha_ref[0:1, 0:1]
    direction = field_ref[...] * (1.0 / alpha)
    if sweep == 0:
        return direction, direction, state_ref[0:1, 0:1], alpha
    phi_bar, rho, cosine, sine = [state_ref[0:1, i : i + 1] for i in range(1, 5)]
    return direction, direction - (sine * alpha / rho) * search_ref[...], phi_bar, -cosine * alpha


def model_kernel(sweep, *refs):
    received_ref, scatter_ref, gather_ref, field_ref, alpha_ref, state_ref = refs[:6]
    search_ref, update_ref = refs[6:8] if sweep else (None, None)
    send_ref, field_out, state_out, search_out, update_out, stage_ref = refs[-6:]
    received = received_ref[...]
    gathered = unstacked(matmul(scatter_ref[...], received)).astype(BF16).astype(F32)
    stage_ref[...] = received.astype(F32)
    first = row_of(stage_ref, NORM_ROW)[...]
    beta = norm_of(first)
    lower = [row_of(stage_ref, ID_ROW)[...], jnp.where(iota(first.shape, 1) < 2, 0.0, first)]
    rough = [(row_of(stage_ref, CELL_ROW + j)[...] + lower[j]).T for j in range(2)]
    direction, search, phi_bar, rho_bar = turn(sweep, field_ref, alpha_ref, state_ref, search_ref)
    field = (gathered + jnp.concatenate(rough, axis=1)) * (1.0 / beta) - beta * direction
    field_out[...] = field
    send_field(send_ref, stage_ref, gathered, field, gather_ref)
    rho = jnp.sqrt(rho_bar * rho_bar + beta * beta)
    cosine, sine = rho_bar / rho, beta / rho
    state_out[...] = scalars_row(beta, sine * phi_bar, rho, cosine, sine)
    search_out[...] = search
    update = (cosine * phi_bar / rho) * search
    update_out[...] = update_ref[...] + update if sweep else update


def last_kernel(norms_ref, data_ref, field_ref, alpha_ref, state_ref, search_ref, update_ref, update_out, data_out):
    squares = jnp.sum(norms_ref[...], axis=0, keepdims=True)[:, 0:1]
    _, search, phi_bar, rho_bar = turn(ITERS - 1, field_ref, alpha_ref, state_ref, search_ref)
    step = rho_bar * phi_bar / (rho_bar * rho_bar + squares)
    update_out[...] = update_ref[...] + step * search
    data_out[...] = data_ref[...] * (1.0 / jnp.sqrt(squares))


def call(kernel, name, outputs, scratch, operands, flops=0, space=pltpu.VMEM):
    bytes_accessed = sum(x.size * x.dtype.itemsize for x in operands)
    return pl.pallas_call(
        kernel,
        name=name,
        out_shape=[jax.ShapeDtypeStruct(shape, dtype) for shape, dtype in outputs],
        in_specs=[pl.BlockSpec(memory_space=space)] * len(operands),
        out_specs=[pl.BlockSpec(memory_space=pltpu.VMEM)] * len(outputs),
        scratch_shapes=scratch,
        compiler_params=pltpu.CompilerParams(vmem_limit_bytes=12 << 20),
        cost_estimate=pl.CostEstimate(flops=flops, bytes_accessed=bytes_accessed, transcendentals=0),
    )(*operands)


def exchange(packed, devices):
    rows, lanes = packed.shape
    chunks = packed.reshape(devices, rows // devices, lanes)
    return lax.all_to_all(chunks, AXES, split_axis=0, concat_axis=0, tiled=True).reshape(rows, lanes)


def body(kernel, target_device, target_block, counts, traveltimes, prior_residual):
    rads = lax.axis_size("rad")
    devices = lax.axis_size("lat") * rads
    ray_blocks, fanout, ray_len, cells = kernel.shape
    entries = ray_blocks * fanout
    rows = devices * CHUNK
    blocks = MB_R * MB_L
    flops = 4 * entries * ray_len * cells

    packet = ((rows, LANES), BF16)
    ray = ((ray_blocks, ray_len), F32)
    model = ((blocks, cells), F32)
    scalar = ((8, LANES), F32)
    partials = pltpu.VMEM((entries, cells), F32)

    stage = pltpu.VMEM((rows, LANES), F32)
    send, tiles, weights, data, place, pick, links = call(
        start_kernel, "start",
        [packet, ((entries * ray_len, cells), BF16), ray, ray,
         ((rows, 2 * entries), BF16), ((2 * entries, rows), BF16), ((3 * blocks, 5 * blocks), BF16)],
        [
            pltpu.VMEM((fanout, ray_blocks), jnp.int32), pltpu.VMEM((fanout, ray_blocks), jnp.int32),
            pltpu.VMEM((1, ray_blocks), jnp.int32), pltpu.VMEM((ray_blocks, ray_len), F32),
            pltpu.VMEM((ray_blocks, ray_len), F32), partials, stage,
            pltpu.VMEM((2 * entries, fanout * ray_len), BF16),
            pltpu.SemaphoreType.DMA((5,)), pltpu.SemaphoreType.DMA,
        ],
        tuple(
            pltpu.with_memory_space_constraint(x, pltpu.HBM)
            for x in (kernel.reshape(entries * ray_len, cells), target_device.T, target_block.T,
                      counts.reshape(1, ray_blocks), traveltimes, prior_residual)
        ),
        flops, pltpu.HBM,
    )
    received = exchange(send, devices)
    send, field, state, gather, scatter = call(
        first_model_kernel, "first_model",
        [packet, model, scalar, ((rows, 2 * blocks), BF16), ((2 * blocks, rows), BF16)], [stage], (received,),
    )
    carried, kept = (), ()
    for sweep in range(ITERS):
        received = exchange(send, devices)
        if sweep == ITERS - 1:
            break
        send, data, cell_state, alpha = call(
            functools.partial(ray_kernel, sweep, rads), "ray",
            [packet, ray, ((3, 2 * devices, blocks), F32), scalar], [stage, partials, partials],
            (received, tiles, pick, weights, data, state, place) + kept, flops,
        )
        kept = (cell_state,)
        received = exchange(send, devices)
        send, field, state, *carried = call(
            functools.partial(model_kernel, sweep), "model", [packet, model, scalar, model, model], [stage],
            (received, scatter, gather, field, alpha, state, *carried), flops,
        )
    send, data, alpha = call(
        functools.partial(last_ray_kernel, ITERS - 1, rads), "last_ray", [((devices, LANES), F32), ray, scalar],
        [stage, partials], (received, tiles, pick, links, weights, data, state) + kept, flops,
    )
    norms = exchange(send, devices)
    update, data = call(last_kernel, "last", [model, ray], [], (norms, data, field, alpha, state, *carried))
    return (update.reshape(MB_R, MB_L, cells), data)


def solution(mesh):
    in_specs = (
        P(("lat", "rad"), None, None, None),
        P(("lat", "rad"), None),
        P(("lat", "rad"), None),
        P(("lat", "rad")),
        P(("lat", "rad"), None),
        P(("lat", "rad"), None),
    )
    out_specs = (P("rad", "lat", None), P(("lat", "rad"), None))
    return jax.shard_map(body, mesh=mesh, in_specs=in_specs, out_specs=out_specs, check_vma=False)
```

```python
import functools

import jax
import jax.numpy as jnp
from jax import lax
from jax.experimental import pallas as pl
from jax.experimental.pallas import tpu as pltpu
from jax.sharding import PartitionSpec as P

ITERS = 3
MB_R = 8
MB_L = 16
FREEDOM = 4.0
DAMPING = 0.3

AXES = ("lat", "rad")
CHUNK = 8
NORM_ROW = 4
ID_ROW = 5
CELL_ROW = 6
LANES = 128
GROUP = 16

F32 = jnp.float32
BF16 = jnp.bfloat16
NT = (((1,), (1,)), ((), ()))


def iota(shape, dim):
    return lax.broadcasted_iota(jnp.int32, shape, dim)


def low(index, size):
    assert size & (size - 1) == 0
    return index & (size - 1)


def high(index, size):
    assert size & (size - 1) == 0
    return lax.shift_right_logical(index, jnp.int32(size.bit_length() - 1))


def matmul(a, b):
    return jnp.dot(a, b, preferred_element_type=F32)


def total(x):
    return jnp.sum(jnp.sum(x, axis=1, keepdims=True), axis=0, keepdims=True)


def ones_where(condition):
    return jnp.where(condition, 1.0, 0.0).astype(BF16)


def norm_row(partial, rest):
    upper = partial.astype(BF16).astype(F32)
    lane = iota(rest.shape, 1)
    return jnp.where(lane == 0, upper, jnp.where(lane == 1, partial - upper, rest))


def norm_of(sums):
    sums = jnp.where(iota(sums.shape, 1) < 2, sums, 0.0)
    return jnp.sqrt(total(sums))


def row_of(ref, j):
    return ref.at[pl.ds(j, ref.shape[0] // CHUNK, stride=CHUNK), :]


def pack(send_ref, stage_ref, named, *rest):
    for j, rows in enumerate(rest):
        row_of(stage_ref, NORM_ROW + j)[...] = rows
    data = low(iota(named.shape, 0), CHUNK) < NORM_ROW
    send_ref[...] = jnp.where(data, named, stage_ref[...]).astype(BF16)


def stacked(x):
    return jnp.concatenate([x[:, :LANES], x[:, LANES:]], axis=0)


def unstacked(x):
    half = x.shape[0] // 2
    return jnp.concatenate([x[:half], x[half:]], axis=1)


def forward_group(tiles_ref, blocks_ref, start, count, fanout, ray_len):
    lane = iota((ray_len, LANES), 1)
    sums = jnp.zeros((ray_len, LANES), F32)
    for i in range(count):
        products = None
        for e in range((start + i) * fanout, (start + i + 1) * fanout):
            product = tiles_ref[e * ray_len : (e + 1) * ray_len, :].astype(F32) * blocks_ref[e : e + 1, :]
            product = product[:, :LANES] + product[:, LANES:]
            products = product if products is None else products + product
        sums = jnp.where(lane == i, jnp.sum(products, axis=1, keepdims=True), sums)
    return sums.T[:count]


def spread_rows(y, fanout):
    upper = y.astype(BF16).astype(F32)
    lower = y - upper
    upper = jnp.concatenate([upper] * fanout, axis=1)
    lower = jnp.concatenate([lower] * fanout, axis=1)
    count, width = upper.shape
    row, lane = iota((2 * fanout, width), 0), iota((2 * fanout, width), 1)
    own = high(lane, width // fanout) == low(row, fanout)
    return [
        jnp.where(own, jnp.where(row < fanout, upper[i : i + 1], lower[i : i + 1]), 0.0) for i in range(count)
    ]


def adjoint_products(tiles_ref, lhs, out_ref, b, fanout):
    width = lhs.shape[1]
    both = matmul(lhs, tiles_ref[b * width : (b + 1) * width, :])
    out_ref[b * fanout : (b + 1) * fanout, :] = both[:fanout] + both[fanout:]


def adjoint_group(tiles_ref, y, out_ref, start, fanout):
    for i, lhs in enumerate(spread_rows(y, fanout)):
        adjoint_products(tiles_ref, lhs.astype(BF16), out_ref, start + i, fanout)


def write_links(ref, blocks):
    source, block = iota((blocks, blocks), 0), iota((blocks, blocks), 1)
    place = low(block, MB_L)
    links = (
        (source == block - MB_L) | (source == block + MB_L)
        | ((source == block - 1) & (place > 0)) | ((source == block + 1) & (place < MB_L - 1)),
        source == block + blocks - MB_L,
        source == block - blocks + MB_L,
        (source == block + MB_L - 1) & (place == 0),
        (source == block - MB_L + 1) & (place == MB_L - 1),
    )
    for i, link in enumerate(links):
        for part in range(3):
            ref[part * blocks : (part + 1) * blocks, i * blocks : (i + 1) * blocks] = ones_where(link)


def roughen(cells, links_ref, rads):
    rows, blocks = cells.shape
    devices = rows // 2
    device, block = low(iota(cells.shape, 0), devices), iota(cells.shape, 1)
    rad, place = low(device, rads), low(block, MB_L)
    owner = lambda x, step: pltpu.roll(x, step % rows, 0)
    lanes = lambda step: pltpu.roll(cells, step % blocks, 1)
    if links_ref is None:
        up, down = lanes(MB_L), lanes(-MB_L)
        left, right = lanes(1 - MB_L), lanes(MB_L - 1)
        north = jnp.where(block >= MB_L, up, jnp.where(rad > 0, owner(up, 1), 0.0))
        south = jnp.where(block < blocks - MB_L, down, jnp.where(rad < rads - 1, owner(down, -1), 0.0))
        west = jnp.where(place > 0, lanes(1), jnp.where(device >= rads, owner(left, rads), 0.0))
        east = jnp.where(place < MB_L - 1, lanes(-1), jnp.where(device < devices - rads, owner(right, -rads), 0.0))
        return 4.0 * cells - (south + north + east + west)
    upper = cells.astype(BF16)
    rest = cells - upper.astype(F32)
    middle = rest.astype(BF16)
    lower = (rest - middle.astype(F32)).astype(BF16)
    sums = matmul(jnp.concatenate([upper, middle, lower], axis=1), links_ref[...])
    piece = lambda i, step: owner(sums[:, i * blocks : (i + 1) * blocks], step)
    beside = sums[:, :blocks]
    beside = beside + jnp.where(rad > 0, piece(1, 1), 0.0)
    beside = beside + jnp.where(rad < rads - 1, piece(2, -1), 0.0)
    beside = beside + jnp.where(device >= rads, piece(3, rads), 0.0)
    beside = beside + jnp.where(device < devices - rads, piece(4, -rads), 0.0)
    return 4.0 * cells - beside


def scalars_row(*values):
    lane = iota((8, LANES), 1)
    out = jnp.zeros((8, LANES), F32)
    for i, value in enumerate(values):
        out = jnp.where(lane == i, value, out)
    return out


def start_kernel(
    kernel_hbm, device_hbm, block_hbm, counts_hbm, times_hbm, prior_hbm,
    send_ref, tiles_ref, weights_ref, data_ref, place_ref, pick_ref, links_ref,
    device_ref, block_ref, counts_ref, times_ref, prior_ref, partial_ref, stage_ref, operand_ref, small_sem, tile_sem,
):
    fanout, ray_blocks = device_ref.shape
    ray_len = times_ref.shape[1]
    entries = ray_blocks * fanout
    rows = send_ref.shape[0]
    devices = rows // CHUNK

    small = [
        pltpu.make_async_copy(source, target, small_sem.at[i])
        for i, (source, target) in enumerate(
            ((device_hbm, device_ref), (block_hbm, block_ref), (counts_hbm, counts_ref),
             (times_hbm, times_ref), (prior_hbm, prior_ref))
        )
    ]
    large = pltpu.make_async_copy(kernel_hbm, tiles_ref, tile_sem)
    for copy in small + [large]:
        copy.start()
    write_links(links_ref, links_ref.shape[0] // 3)
    for copy in small:
        copy.wait()

    member = ones_where(high(iota((entries, ray_blocks), 0), fanout) == iota((entries, ray_blocks), 1))
    turn = low(iota((entries, fanout), 0), fanout) == iota((entries, fanout), 1)

    def column(table_ref):
        table = table_ref[...].astype(F32).astype(BF16)
        spread = lax.dot_general(member, table, NT, preferred_element_type=F32)
        return jnp.sum(jnp.where(turn, spread, 0.0), axis=1, keepdims=True)

    diagonal = iota((entries, entries), 0) == iota((entries, entries), 1)

    def as_row(col):
        return jnp.sum(jnp.where(diagonal, col, 0.0), axis=0, keepdims=True)

    target = column(device_ref)
    block = column(block_ref)
    target_row = as_row(target)
    earlier = iota((entries, entries), 1) < iota((entries, entries), 0)
    rank = jnp.sum(jnp.where(earlier & (target == target_row), 1.0, 0.0), axis=1, keepdims=True)
    first = target * CHUNK + 2.0 * rank
    to_col = first.astype(jnp.int32)
    to_row = as_row(first).astype(jnp.int32)
    for half in range(2):
        here = slice(half * entries, (half + 1) * entries)
        pick_ref[here, :] = ones_where(iota((entries, rows), 1) == to_col + half)
        place_ref[:, here] = ones_where(iota((rows, entries), 0) == to_row + half)

    same = iota((ray_blocks, ray_blocks), 0) == iota((ray_blocks, ray_blocks), 1)
    counts = jnp.sum(jnp.where(same, counts_ref[...].astype(F32), 0.0), axis=1, keepdims=True)
    mask = jnp.where(iota((ray_blocks, ray_len), 1).astype(F32) < counts, 1.0, 0.0)
    prior = prior_ref[...]
    weights = mask * jnp.sqrt((FREEDOM + 1.0) / (FREEDOM + prior * prior))
    weights_ref[...] = weights
    data = weights * times_ref[...]
    data_ref[...] = data

    operands = spread_rows(weights * data, fanout)
    depth = 2 * fanout
    for b in range(0, ray_blocks, 2):
        operand_ref[b * depth : (b + 2) * depth, :] = jnp.concatenate(operands[b : b + 2], axis=0).astype(BF16)
    ids = jnp.where(iota((entries, LANES), 1).astype(F32) == rank, block + 1.0, 0.0).astype(BF16)
    named_by = ones_where(iota((devices, entries), 0).astype(F32) == target_row)
    zeros = jnp.zeros((devices, LANES), F32)
    rest = norm_row(total(data * data), zeros), matmul(named_by, ids), zeros, zeros
    for j, rows_of in enumerate(rest):
        row_of(stage_ref, NORM_ROW + j)[...] = rows_of
    large.wait()
    for b in range(ray_blocks):
        adjoint_products(tiles_ref, operand_ref[b * depth : (b + 1) * depth, :], partial_ref, b, fanout)
    pack(send_ref, stage_ref, matmul(place_ref[...], stacked(partial_ref[...].astype(BF16))))


def send_field(send_ref, stage_ref, gathered, field, gather_ref):
    cells = [gathered[:, half * LANES : (half + 1) * LANES].T for half in range(2)]
    zeros = jnp.zeros(cells[0].shape, F32)
    norms = norm_row(total(field * field), zeros)
    pack(send_ref, stage_ref, matmul(gather_ref[...], stacked(field).astype(BF16)), norms, zeros, *cells)


def first_model_kernel(received_ref, send_ref, field_ref, state_ref, gather_ref, scatter_ref, stage_ref):
    received = received_ref[...]
    rows = received.shape[0]
    blocks = MB_R * MB_L
    stage_ref[...] = received.astype(F32)
    beta = norm_of(row_of(stage_ref, NORM_ROW)[...])
    ids = row_of(stage_ref, ID_ROW)[...]
    for j in range(CHUNK):
        ident = ids[:, j // 2 : j // 2 + 1] if j < NORM_ROW else 0.0
        row_of(stage_ref, j)[...] = jnp.broadcast_to(ident, ids.shape)
    hit = stage_ref[...] - 1.0 == iota((rows, LANES), 1).astype(F32)
    odd = low(iota((rows, LANES), 0), 2)
    for half in range(2):
        here = slice(half * blocks, (half + 1) * blocks)
        chosen = jnp.where(hit & (odd == half), 1.0, 0.0)
        gather_ref[:, here] = chosen.astype(BF16)
        scatter_ref[here, :] = chosen.T.astype(BF16)

    gathered = unstacked(matmul(scatter_ref[...], received)).astype(BF16).astype(F32)
    field = gathered * (1.0 / beta)
    field_ref[...] = field
    state_ref[...] = scalars_row(beta)
    send_field(send_ref, stage_ref, gathered, field, gather_ref)


def ray_step(
    sweep, rads, received_ref, tiles_ref, pick_ref, links_ref, weights_ref, data_ref, state_ref, cells_ref,
    data_out, alpha_out,
    stage_ref, blocks_ref, partial_ref=None,
):
    received = received_ref[...]
    ray_blocks, ray_len = data_ref.shape
    devices = received.shape[0] // CHUNK
    fanout = blocks_ref.shape[0] // ray_blocks
    blocks_ref[...] = unstacked(matmul(pick_ref[...], received))
    stage_ref[...] = received.astype(F32)
    alpha = norm_of(row_of(stage_ref, NORM_ROW)[...])
    alpha_out[...] = scalars_row(alpha)
    beta = state_ref[0:1, 0:1]
    inverse_alpha, inverse_beta = 1.0 / alpha, 1.0 / beta
    ratio = alpha / beta

    waiting = None
    for start in range(0, ray_blocks, GROUP):
        here = slice(start, start + GROUP)
        products = forward_group(tiles_ref, blocks_ref, start, GROUP, fanout, ray_len)
        weights = weights_ref[here, :]
        data = weights * (products * inverse_alpha) - ratio * data_ref[here, :]
        data_out[here, :] = data
        if partial_ref is not None:
            if waiting is not None:
                adjoint_group(tiles_ref, waiting[0], partial_ref, waiting[1], fanout)
            waiting = weights * data, start
    if partial_ref is not None:
        adjoint_group(tiles_ref, waiting[0], partial_ref, waiting[1], fanout)

    data = data_out[...]
    cell = jnp.concatenate([row_of(stage_ref, CELL_ROW + j)[...] for j in range(2)], axis=0)
    if sweep:
        direction = ((cell + cells_ref[0]) * inverse_beta - beta * cells_ref[1]) * inverse_alpha
        pen = DAMPING * roughen(direction, links_ref, rads) - ratio * cells_ref[2]
    else:
        direction = (cell * inverse_beta) * inverse_alpha
        pen = DAMPING * roughen(direction, links_ref, rads)
    return total(data * data) + total(pen * pen), pen, direction


def ray_kernel(sweep, rads, *refs):
    received_ref, tiles_ref, pick_ref, weights_ref, data_ref, state_ref, place_ref = refs[:7]
    cells_ref = refs[7] if sweep else None
    send_ref, data_out, cells_out, alpha_out, stage_ref, blocks_ref, partial_ref = refs[-7:]
    partial, pen, direction = ray_step(
        sweep, rads, received_ref, tiles_ref, pick_ref, None, weights_ref, data_ref, state_ref, cells_ref, data_out, alpha_out, stage_ref, blocks_ref, partial_ref
    )
    rough = DAMPING * roughen(pen, None, rads)
    for i, kept in enumerate((rough, direction, pen)):
        cells_out[i] = kept
    upper = rough.astype(BF16).astype(F32)
    lower = rough - upper
    half = rough.shape[0] // 2
    pack(
        send_ref, stage_ref, matmul(place_ref[...], stacked(partial_ref[...]).astype(BF16)),
        norm_row(partial, lower[half:]), lower[:half], upper[:half], upper[half:],
    )


def last_ray_kernel(sweep, rads, *refs):
    send_ref, data_out, alpha_out, stage_ref, blocks_ref = refs[-5:]
    partial, _, _ = ray_step(sweep, rads, *refs[:-5], data_out, alpha_out, stage_ref, blocks_ref)
    send_ref[...] = jnp.broadcast_to(partial, send_ref.shape)


def turn(sweep, field_ref, alpha_ref, state_ref, search_ref):
    alpha = alpha_ref[0:1, 0:1]
    direction = field_ref[...] * (1.0 / alpha)
    if sweep == 0:
        return direction, direction, state_ref[0:1, 0:1], alpha
    phi_bar, rho, cosine, sine = [state_ref[0:1, i : i + 1] for i in range(1, 5)]
    return direction, direction - (sine * alpha / rho) * search_ref[...], phi_bar, -cosine * alpha


def model_kernel(sweep, *refs):
    received_ref, scatter_ref, gather_ref, field_ref, alpha_ref, state_ref = refs[:6]
    search_ref, update_ref = refs[6:8] if sweep else (None, None)
    send_ref, field_out, state_out, search_out, update_out, stage_ref = refs[-6:]
    received = received_ref[...]
    gathered = unstacked(matmul(scatter_ref[...], received)).astype(BF16).astype(F32)
    stage_ref[...] = received.astype(F32)
    first = row_of(stage_ref, NORM_ROW)[...]
    beta = norm_of(first)
    lower = [row_of(stage_ref, ID_ROW)[...], jnp.where(iota(first.shape, 1) < 2, 0.0, first)]
    rough = [(row_of(stage_ref, CELL_ROW + j)[...] + lower[j]).T for j in range(2)]
    direction, search, phi_bar, rho_bar = turn(sweep, field_ref, alpha_ref, state_ref, search_ref)
    field = (gathered + jnp.concatenate(rough, axis=1)) * (1.0 / beta) - beta * direction
    field_out[...] = field
    send_field(send_ref, stage_ref, gathered, field, gather_ref)
    rho = jnp.sqrt(rho_bar * rho_bar + beta * beta)
    cosine, sine = rho_bar / rho, beta / rho
    state_out[...] = scalars_row(beta, sine * phi_bar, rho, cosine, sine)
    search_out[...] = search
    update = (cosine * phi_bar / rho) * search
    update_out[...] = update_ref[...] + update if sweep else update


def last_kernel(norms_ref, data_ref, field_ref, alpha_ref, state_ref, search_ref, update_ref, update_out, data_out):
    squares = jnp.sum(norms_ref[...], axis=0, keepdims=True)[:, 0:1]
    _, search, phi_bar, rho_bar = turn(ITERS - 1, field_ref, alpha_ref, state_ref, search_ref)
    step = rho_bar * phi_bar / (rho_bar * rho_bar + squares)
    update_out[...] = update_ref[...] + step * search
    data_out[...] = data_ref[...] * (1.0 / jnp.sqrt(squares))


def call(kernel, name, outputs, scratch, operands, flops=0, space=pltpu.VMEM):
    bytes_accessed = sum(x.size * x.dtype.itemsize for x in operands)
    return pl.pallas_call(
        kernel,
        name=name,
        out_shape=[jax.ShapeDtypeStruct(shape, dtype) for shape, dtype in outputs],
        in_specs=[pl.BlockSpec(memory_space=space)] * len(operands),
        out_specs=[pl.BlockSpec(memory_space=pltpu.VMEM)] * len(outputs),
        scratch_shapes=scratch,
        compiler_params=pltpu.CompilerParams(vmem_limit_bytes=12 << 20),
        cost_estimate=pl.CostEstimate(flops=flops, bytes_accessed=bytes_accessed, transcendentals=0),
    )(*operands)


def exchange(packed, devices):
    rows, lanes = packed.shape
    chunks = packed.reshape(devices, rows // devices, lanes)
    return lax.all_to_all(chunks, AXES, split_axis=0, concat_axis=0, tiled=True).reshape(rows, lanes)


def body(kernel, target_device, target_block, counts, traveltimes, prior_residual):
    rads = lax.axis_size("rad")
    devices = lax.axis_size("lat") * rads
    ray_blocks, fanout, ray_len, cells = kernel.shape
    entries = ray_blocks * fanout
    rows = devices * CHUNK
    blocks = MB_R * MB_L
    flops = 4 * entries * ray_len * cells

    packet = ((rows, LANES), BF16)
    ray = ((ray_blocks, ray_len), F32)
    model = ((blocks, cells), F32)
    scalar = ((8, LANES), F32)
    partials = pltpu.VMEM((entries, cells), F32)

    stage = pltpu.VMEM((rows, LANES), F32)
    send, tiles, weights, data, place, pick, links = call(
        start_kernel, "start",
        [packet, ((entries * ray_len, cells), BF16), ray, ray,
         ((rows, 2 * entries), BF16), ((2 * entries, rows), BF16), ((3 * blocks, 5 * blocks), BF16)],
        [
            pltpu.VMEM((fanout, ray_blocks), jnp.int32), pltpu.VMEM((fanout, ray_blocks), jnp.int32),
            pltpu.VMEM((1, ray_blocks), jnp.int32), pltpu.VMEM((ray_blocks, ray_len), F32),
            pltpu.VMEM((ray_blocks, ray_len), F32), partials, stage,
            pltpu.VMEM((2 * entries, fanout * ray_len), BF16),
            pltpu.SemaphoreType.DMA((5,)), pltpu.SemaphoreType.DMA,
        ],
        tuple(
            pltpu.with_memory_space_constraint(x, pltpu.HBM)
            for x in (kernel.reshape(entries * ray_len, cells), target_device.T, target_block.T,
                      counts.reshape(1, ray_blocks), traveltimes, prior_residual)
        ),
        flops, pltpu.HBM,
    )
    received = exchange(send, devices)
    send, field, state, gather, scatter = call(
        first_model_kernel, "first_model",
        [packet, model, scalar, ((rows, 2 * blocks), BF16), ((2 * blocks, rows), BF16)], [stage], (received,),
    )
    carried, kept = (), ()
    for sweep in range(ITERS):
        received = exchange(send, devices)
        if sweep == ITERS - 1:
            break
        send, data, cell_state, alpha = call(
            functools.partial(ray_kernel, sweep, rads), "ray",
            [packet, ray, ((3, 2 * devices, blocks), F32), scalar], [stage, partials, partials],
            (received, tiles, pick, weights, data, state, place) + kept, flops,
        )
        kept = (cell_state,)
        received = exchange(send, devices)
        send, field, state, *carried = call(
            functools.partial(model_kernel, sweep), "model", [packet, model, scalar, model, model], [stage],
            (received, scatter, gather, field, alpha, state, *carried), flops,
        )
    send, data, alpha = call(
        functools.partial(last_ray_kernel, ITERS - 1, rads), "last_ray", [((devices, LANES), F32), ray, scalar],
        [stage, partials], (received, tiles, pick, links, weights, data, state) + kept, flops,
    )
    norms = exchange(send, devices)
    update, data = call(last_kernel, "last", [model, ray], [], (norms, data, field, alpha, state, *carried))
    return (update.reshape(MB_R, MB_L, cells), data)


def solution(mesh):
    in_specs = (
        P(("lat", "rad"), None, None, None),
        P(("lat", "rad"), None),
        P(("lat", "rad"), None),
        P(("lat", "rad")),
        P(("lat", "rad"), None),
        P(("lat", "rad"), None),
    )
    out_specs = (P("rad", "lat", None), P(("lat", "rad"), None))
    return jax.shard_map(body, mesh=mesh, in_specs=in_specs, out_specs=out_specs, check_vma=False)
```

```python
import functools

import jax
import jax.numpy as jnp
from jax import lax
from jax.experimental import pallas as pl
from jax.experimental.pallas import tpu as pltpu
from jax.sharding import PartitionSpec as P

ITERS = 3
MB_R = 8
MB_L = 16
FREEDOM = 4.0
DAMPING = 0.3

AXES = ("lat", "rad")
CHUNK = 8
NORM_ROW = 4
ID_ROW = 5
CELL_ROW = 6
LANES = 128
GROUP = 16

F32 = jnp.float32
BF16 = jnp.bfloat16
NT = (((1,), (1,)), ((), ()))


def iota(shape, dim):
    return lax.broadcasted_iota(jnp.int32, shape, dim)


def low(index, size):
    assert size & (size - 1) == 0
    return index & (size - 1)


def high(index, size):
    assert size & (size - 1) == 0
    return lax.shift_right_logical(index, jnp.int32(size.bit_length() - 1))


def matmul(a, b):
    return jnp.dot(a, b, preferred_element_type=F32)


def total(x):
    return jnp.sum(jnp.sum(x, axis=1, keepdims=True), axis=0, keepdims=True)


def ones_where(condition):
    return jnp.where(condition, 1.0, 0.0).astype(BF16)


def norm_row(partial, rest):
    upper = partial.astype(BF16).astype(F32)
    lane = iota(rest.shape, 1)
    return jnp.where(lane == 0, upper, jnp.where(lane == 1, partial - upper, rest))


def norm_of(sums):
    sums = jnp.where(iota(sums.shape, 1) < 2, sums, 0.0)
    return jnp.sqrt(total(sums))


def row_of(ref, j):
    return ref.at[pl.ds(j, ref.shape[0] // CHUNK, stride=CHUNK), :]


def pack(send_ref, stage_ref, named, *rest):
    for j, rows in enumerate(rest):
        row_of(stage_ref, NORM_ROW + j)[...] = rows
    data = low(iota(named.shape, 0), CHUNK) < NORM_ROW
    send_ref[...] = jnp.where(data, named, stage_ref[...]).astype(BF16)


def stacked(x):
    return jnp.concatenate([x[:, :LANES], x[:, LANES:]], axis=0)


def unstacked(x):
    half = x.shape[0] // 2
    return jnp.concatenate([x[:half], x[half:]], axis=1)


def forward_group(tiles_ref, blocks_ref, start, count, fanout, ray_len):
    lane = iota((ray_len, LANES), 1)
    sums = jnp.zeros((ray_len, LANES), F32)
    for i in range(count):
        products = None
        for e in range((start + i) * fanout, (start + i + 1) * fanout):
            product = tiles_ref[e * ray_len : (e + 1) * ray_len, :].astype(F32) * blocks_ref[e : e + 1, :]
            product = product[:, :LANES] + product[:, LANES:]
            products = product if products is None else products + product
        sums = jnp.where(lane == i, jnp.sum(products, axis=1, keepdims=True), sums)
    return sums.T[:count]


def spread_rows(y, fanout):
    upper = y.astype(BF16).astype(F32)
    lower = y - upper
    upper = jnp.concatenate([upper] * fanout, axis=1)
    lower = jnp.concatenate([lower] * fanout, axis=1)
    count, width = upper.shape
    row, lane = iota((2 * fanout, width), 0), iota((2 * fanout, width), 1)
    own = high(lane, width // fanout) == low(row, fanout)
    return [
        jnp.where(own, jnp.where(row < fanout, upper[i : i + 1], lower[i : i + 1]), 0.0) for i in range(count)
    ]


def adjoint_products(tiles_ref, lhs, out_ref, b, fanout):
    width = lhs.shape[1]
    both = matmul(lhs, tiles_ref[b * width : (b + 1) * width, :])
    out_ref[b * fanout : (b + 1) * fanout, :] = both[:fanout] + both[fanout:]


def adjoint_group(tiles_ref, y, out_ref, start, fanout):
    for i, lhs in enumerate(spread_rows(y, fanout)):
        adjoint_products(tiles_ref, lhs.astype(BF16), out_ref, start + i, fanout)


def write_links(ref, blocks):
    source, block = iota((blocks, blocks), 0), iota((blocks, blocks), 1)
    place = low(block, MB_L)
    links = (
        (source == block - MB_L) | (source == block + MB_L)
        | ((source == block - 1) & (place > 0)) | ((source == block + 1) & (place < MB_L - 1)),
        source == block + blocks - MB_L,
        source == block - blocks + MB_L,
        (source == block + MB_L - 1) & (place == 0),
        (source == block - MB_L + 1) & (place == MB_L - 1),
    )
    for i, link in enumerate(links):
        for part in range(3):
            ref[part * blocks : (part + 1) * blocks, i * blocks : (i + 1) * blocks] = ones_where(link)


def roughen(cells, links_ref, rads):
    rows, blocks = cells.shape
    devices = rows // 2
    device, block = low(iota(cells.shape, 0), devices), iota(cells.shape, 1)
    rad, place = low(device, rads), low(block, MB_L)
    owner = lambda x, step: pltpu.roll(x, step % rows, 0)
    lanes = lambda step: pltpu.roll(cells, step % blocks, 1)
    if links_ref is None:
        up, down = lanes(MB_L), lanes(-MB_L)
        left, right = lanes(1 - MB_L), lanes(MB_L - 1)
        north = jnp.where(block >= MB_L, up, jnp.where(rad > 0, owner(up, 1), 0.0))
        south = jnp.where(block < blocks - MB_L, down, jnp.where(rad < rads - 1, owner(down, -1), 0.0))
        west = jnp.where(place > 0, lanes(1), jnp.where(device >= rads, owner(left, rads), 0.0))
        east = jnp.where(place < MB_L - 1, lanes(-1), jnp.where(device < devices - rads, owner(right, -rads), 0.0))
        return 4.0 * cells - (south + north + east + west)
    upper = cells.astype(BF16)
    rest = cells - upper.astype(F32)
    middle = rest.astype(BF16)
    lower = (rest - middle.astype(F32)).astype(BF16)
    sums = matmul(jnp.concatenate([upper, middle, lower], axis=1), links_ref[...])
    piece = lambda i, step: owner(sums[:, i * blocks : (i + 1) * blocks], step)
    beside = sums[:, :blocks]
    beside = beside + jnp.where(rad > 0, piece(1, 1), 0.0)
    beside = beside + jnp.where(rad < rads - 1, piece(2, -1), 0.0)
    beside = beside + jnp.where(device >= rads, piece(3, rads), 0.0)
    beside = beside + jnp.where(device < devices - rads, piece(4, -rads), 0.0)
    return 4.0 * cells - beside


def scalars_row(*values):
    lane = iota((8, LANES), 1)
    out = jnp.zeros((8, LANES), F32)
    for i, value in enumerate(values):
        out = jnp.where(lane == i, value, out)
    return out


def start_kernel(
    kernel_hbm, device_hbm, block_hbm, counts_hbm, times_hbm, prior_hbm,
    send_ref, tiles_ref, weights_ref, data_ref, place_ref, pick_ref, links_ref,
    device_ref, block_ref, counts_ref, times_ref, prior_ref, partial_ref, stage_ref, operand_ref, small_sem, tile_sem,
):
    fanout, ray_blocks = device_ref.shape
    ray_len = times_ref.shape[1]
    entries = ray_blocks * fanout
    rows = send_ref.shape[0]
    devices = rows // CHUNK

    small = [
        pltpu.make_async_copy(source, target, small_sem.at[i])
        for i, (source, target) in enumerate(
            ((device_hbm, device_ref), (block_hbm, block_ref), (counts_hbm, counts_ref),
             (times_hbm, times_ref), (prior_hbm, prior_ref))
        )
    ]
    large = pltpu.make_async_copy(kernel_hbm, tiles_ref, tile_sem)
    for copy in small + [large]:
        copy.start()
    write_links(links_ref, links_ref.shape[0] // 3)
    for copy in small:
        copy.wait()

    member = ones_where(high(iota((entries, ray_blocks), 0), fanout) == iota((entries, ray_blocks), 1))
    turn = low(iota((entries, fanout), 0), fanout) == iota((entries, fanout), 1)

    def column(table_ref):
        table = table_ref[...].astype(F32).astype(BF16)
        spread = lax.dot_general(member, table, NT, preferred_element_type=F32)
        return jnp.sum(jnp.where(turn, spread, 0.0), axis=1, keepdims=True)

    diagonal = iota((entries, entries), 0) == iota((entries, entries), 1)

    def as_row(col):
        return jnp.sum(jnp.where(diagonal, col, 0.0), axis=0, keepdims=True)

    target = column(device_ref)
    block = column(block_ref)
    target_row = as_row(target)
    earlier = iota((entries, entries), 1) < iota((entries, entries), 0)
    rank = jnp.sum(jnp.where(earlier & (target == target_row), 1.0, 0.0), axis=1, keepdims=True)
    first = target * CHUNK + 2.0 * rank
    to_col = first.astype(jnp.int32)
    to_row = as_row(first).astype(jnp.int32)
    for half in range(2):
        here = slice(half * entries, (half + 1) * entries)
        pick_ref[here, :] = ones_where(iota((entries, rows), 1) == to_col + half)
        place_ref[:, here] = ones_where(iota((rows, entries), 0) == to_row + half)

    same = iota((ray_blocks, ray_blocks), 0) == iota((ray_blocks, ray_blocks), 1)
    counts = jnp.sum(jnp.where(same, counts_ref[...].astype(F32), 0.0), axis=1, keepdims=True)
    mask = jnp.where(iota((ray_blocks, ray_len), 1).astype(F32) < counts, 1.0, 0.0)
    prior = prior_ref[...]
    weights = mask * jnp.sqrt((FREEDOM + 1.0) / (FREEDOM + prior * prior))
    weights_ref[...] = weights
    data = weights * times_ref[...]
    data_ref[...] = data

    operands = spread_rows(weights * data, fanout)
    depth = 2 * fanout
    for b in range(0, ray_blocks, 2):
        operand_ref[b * depth : (b + 2) * depth, :] = jnp.concatenate(operands[b : b + 2], axis=0).astype(BF16)
    ids = jnp.where(iota((entries, LANES), 1).astype(F32) == rank, block + 1.0, 0.0).astype(BF16)
    named_by = ones_where(iota((devices, entries), 0).astype(F32) == target_row)
    zeros = jnp.zeros((devices, LANES), F32)
    rest = norm_row(total(data * data), zeros), matmul(named_by, ids), zeros, zeros
    for j, rows_of in enumerate(rest):
        row_of(stage_ref, NORM_ROW + j)[...] = rows_of
    large.wait()
    for b in range(ray_blocks):
        adjoint_products(tiles_ref, operand_ref[b * depth : (b + 1) * depth, :], partial_ref, b, fanout)
    pack(send_ref, stage_ref, matmul(place_ref[...], stacked(partial_ref[...].astype(BF16))))


def send_field(send_ref, stage_ref, gathered, field, gather_ref):
    cells = [gathered[:, half * LANES : (half + 1) * LANES].T for half in range(2)]
    zeros = jnp.zeros(cells[0].shape, F32)
    norms = norm_row(total(field * field), zeros)
    pack(send_ref, stage_ref, matmul(gather_ref[...], stacked(field).astype(BF16)), norms, zeros, *cells)


def first_model_kernel(received_ref, send_ref, field_ref, state_ref, gather_ref, scatter_ref, stage_ref):
    received = received_ref[...]
    rows = received.shape[0]
    blocks = MB_R * MB_L
    stage_ref[...] = received.astype(F32)
    beta = norm_of(row_of(stage_ref, NORM_ROW)[...])
    ids = row_of(stage_ref, ID_ROW)[...]
    for j in range(CHUNK):
        ident = ids[:, j // 2 : j // 2 + 1] if j < NORM_ROW else 0.0
        row_of(stage_ref, j)[...] = jnp.broadcast_to(ident, ids.shape)
    hit = stage_ref[...] - 1.0 == iota((rows, LANES), 1).astype(F32)
    odd = low(iota((rows, LANES), 0), 2)
    for half in range(2):
        here = slice(half * blocks, (half + 1) * blocks)
        chosen = jnp.where(hit & (odd == half), 1.0, 0.0)
        gather_ref[:, here] = chosen.astype(BF16)
        scatter_ref[here, :] = chosen.T.astype(BF16)

    gathered = unstacked(matmul(scatter_ref[...], received)).astype(BF16).astype(F32)
    field = gathered * (1.0 / beta)
    field_ref[...] = field
    state_ref[...] = scalars_row(beta)
    send_field(send_ref, stage_ref, gathered, field, gather_ref)


def ray_step(
    sweep, rads, received_ref, tiles_ref, pick_ref, links_ref, weights_ref, data_ref, state_ref, cells_ref,
    data_out, alpha_out,
    stage_ref, blocks_ref, partial_ref=None,
):
    received = received_ref[...]
    ray_blocks, ray_len = data_ref.shape
    devices = received.shape[0] // CHUNK
    fanout = blocks_ref.shape[0] // ray_blocks
    blocks_ref[...] = unstacked(matmul(pick_ref[...], received))
    stage_ref[...] = received.astype(F32)
    alpha = norm_of(row_of(stage_ref, NORM_ROW)[...])
    alpha_out[...] = scalars_row(alpha)
    beta = state_ref[0:1, 0:1]
    inverse_alpha, inverse_beta = 1.0 / alpha, 1.0 / beta
    ratio = alpha / beta

    waiting = None
    for start in range(0, ray_blocks, GROUP):
        here = slice(start, start + GROUP)
        products = forward_group(tiles_ref, blocks_ref, start, GROUP, fanout, ray_len)
        weights = weights_ref[here, :]
        data = weights * (products * inverse_alpha) - ratio * data_ref[here, :]
        data_out[here, :] = data
        if partial_ref is not None:
            if waiting is not None:
                adjoint_group(tiles_ref, waiting[0], partial_ref, waiting[1], fanout)
            waiting = weights * data, start
    if partial_ref is not None:
        adjoint_group(tiles_ref, waiting[0], partial_ref, waiting[1], fanout)

    data = data_out[...]
    cell = jnp.concatenate([row_of(stage_ref, CELL_ROW + j)[...] for j in range(2)], axis=0)
    if sweep:
        direction = ((cell + cells_ref[0]) * inverse_beta - beta * cells_ref[1]) * inverse_alpha
        pen = DAMPING * roughen(direction, links_ref, rads) - ratio * cells_ref[2]
    else:
        direction = (cell * inverse_beta) * inverse_alpha
        pen = DAMPING * roughen(direction, links_ref, rads)
    return total(data * data) + total(pen * pen), pen, direction


def ray_kernel(sweep, rads, *refs):
    inputs, place_ref = refs[:7], refs[7]
    cells_ref = refs[8] if sweep else None
    send_ref, data_out, cells_out, alpha_out, stage_ref, blocks_ref, partial_ref = refs[-7:]
    partial, pen, direction = ray_step(
        sweep, rads, *inputs, cells_ref, data_out, alpha_out, stage_ref, blocks_ref, partial_ref
    )
    rough = DAMPING * roughen(pen, None, rads)
    for i, kept in enumerate((rough, direction, pen)):
        cells_out[i] = kept
    upper = rough.astype(BF16).astype(F32)
    lower = rough - upper
    half = rough.shape[0] // 2
    pack(
        send_ref, stage_ref, matmul(place_ref[...], stacked(partial_ref[...]).astype(BF16)),
        norm_row(partial, lower[half:]), lower[:half], upper[:half], upper[half:],
    )


def last_ray_kernel(sweep, rads, *refs):
    send_ref, data_out, alpha_out, stage_ref, blocks_ref = refs[-5:]
    partial, _, _ = ray_step(sweep, rads, *refs[:-5], data_out, alpha_out, stage_ref, blocks_ref)
    send_ref[...] = jnp.broadcast_to(partial, send_ref.shape)


def turn(sweep, field_ref, alpha_ref, state_ref, search_ref):
    alpha = alpha_ref[0:1, 0:1]
    direction = field_ref[...] * (1.0 / alpha)
    if sweep == 0:
        return direction, direction, state_ref[0:1, 0:1], alpha
    phi_bar, rho, cosine, sine = [state_ref[0:1, i : i + 1] for i in range(1, 5)]
    return direction, direction - (sine * alpha / rho) * search_ref[...], phi_bar, -cosine * alpha


def model_kernel(sweep, *refs):
    received_ref, scatter_ref, gather_ref, field_ref, alpha_ref, state_ref = refs[:6]
    search_ref, update_ref = refs[6:8] if sweep else (None, None)
    send_ref, field_out, state_out, search_out, update_out, stage_ref = refs[-6:]
    received = received_ref[...]
    gathered = unstacked(matmul(scatter_ref[...], received)).astype(BF16).astype(F32)
    stage_ref[...] = received.astype(F32)
    first = row_of(stage_ref, NORM_ROW)[...]
    beta = norm_of(first)
    lower = [row_of(stage_ref, ID_ROW)[...], jnp.where(iota(first.shape, 1) < 2, 0.0, first)]
    rough = [(row_of(stage_ref, CELL_ROW + j)[...] + lower[j]).T for j in range(2)]
    direction, search, phi_bar, rho_bar = turn(sweep, field_ref, alpha_ref, state_ref, search_ref)
    field = (gathered + jnp.concatenate(rough, axis=1)) * (1.0 / beta) - beta * direction
    field_out[...] = field
    send_field(send_ref, stage_ref, gathered, field, gather_ref)
    rho = jnp.sqrt(rho_bar * rho_bar + beta * beta)
    cosine, sine = rho_bar / rho, beta / rho
    state_out[...] = scalars_row(beta, sine * phi_bar, rho, cosine, sine)
    search_out[...] = search
    update = (cosine * phi_bar / rho) * search
    update_out[...] = update_ref[...] + update if sweep else update


def last_kernel(norms_ref, data_ref, field_ref, alpha_ref, state_ref, search_ref, update_ref, update_out, data_out):
    squares = jnp.sum(norms_ref[...], axis=0, keepdims=True)[:, 0:1]
    _, search, phi_bar, rho_bar = turn(ITERS - 1, field_ref, alpha_ref, state_ref, search_ref)
    step = rho_bar * phi_bar / (rho_bar * rho_bar + squares)
    update_out[...] = update_ref[...] + step * search
    data_out[...] = data_ref[...] * (1.0 / jnp.sqrt(squares))


def call(kernel, name, outputs, scratch, operands, flops=0, space=pltpu.VMEM):
    bytes_accessed = sum(x.size * x.dtype.itemsize for x in operands)
    return pl.pallas_call(
        kernel,
        name=name,
        out_shape=[jax.ShapeDtypeStruct(shape, dtype) for shape, dtype in outputs],
        in_specs=[pl.BlockSpec(memory_space=space)] * len(operands),
        out_specs=[pl.BlockSpec(memory_space=pltpu.VMEM)] * len(outputs),
        scratch_shapes=scratch,
        compiler_params=pltpu.CompilerParams(vmem_limit_bytes=12 << 20),
        cost_estimate=pl.CostEstimate(flops=flops, bytes_accessed=bytes_accessed, transcendentals=0),
    )(*operands)


def exchange(packed, devices):
    rows, lanes = packed.shape
    chunks = packed.reshape(devices, rows // devices, lanes)
    return lax.all_to_all(chunks, AXES, split_axis=0, concat_axis=0, tiled=True).reshape(rows, lanes)


def body(kernel, target_device, target_block, counts, traveltimes, prior_residual):
    rads = lax.axis_size("rad")
    devices = lax.axis_size("lat") * rads
    ray_blocks, fanout, ray_len, cells = kernel.shape
    entries = ray_blocks * fanout
    rows = devices * CHUNK
    blocks = MB_R * MB_L
    flops = 4 * entries * ray_len * cells

    packet = ((rows, LANES), BF16)
    ray = ((ray_blocks, ray_len), F32)
    model = ((blocks, cells), F32)
    scalar = ((8, LANES), F32)
    partials = pltpu.VMEM((entries, cells), F32)

    stage = pltpu.VMEM((rows, LANES), F32)
    send, tiles, weights, data, place, pick, links = call(
        start_kernel, "start",
        [packet, ((entries * ray_len, cells), BF16), ray, ray,
         ((rows, 2 * entries), BF16), ((2 * entries, rows), BF16), ((3 * blocks, 5 * blocks), BF16)],
        [
            pltpu.VMEM((fanout, ray_blocks), jnp.int32), pltpu.VMEM((fanout, ray_blocks), jnp.int32),
            pltpu.VMEM((1, ray_blocks), jnp.int32), pltpu.VMEM((ray_blocks, ray_len), F32),
            pltpu.VMEM((ray_blocks, ray_len), F32), partials, stage,
            pltpu.VMEM((2 * entries, fanout * ray_len), BF16),
            pltpu.SemaphoreType.DMA((5,)), pltpu.SemaphoreType.DMA,
        ],
        tuple(
            pltpu.with_memory_space_constraint(x, pltpu.HBM)
            for x in (kernel.reshape(entries * ray_len, cells), target_device.T, target_block.T,
                      counts.reshape(1, ray_blocks), traveltimes, prior_residual)
        ),
        flops, pltpu.HBM,
    )
    received = exchange(send, devices)
    send, field, state, gather, scatter = call(
        first_model_kernel, "first_model",
        [packet, model, scalar, ((rows, 2 * blocks), BF16), ((2 * blocks, rows), BF16)], [stage], (received,),
    )
    carried, kept = (), ()
    for sweep in range(ITERS):
        received = exchange(send, devices)
        if sweep == ITERS - 1:
            break
        send, data, cell_state, alpha = call(
            functools.partial(ray_kernel, sweep, rads), "ray",
            [packet, ray, ((3, 2 * devices, blocks), F32), scalar], [stage, partials, partials],
            (received, tiles, pick, links, weights, data, state, place) + kept, flops,
        )
        kept = (cell_state,)
        received = exchange(send, devices)
        send, field, state, *carried = call(
            functools.partial(model_kernel, sweep), "model", [packet, model, scalar, model, model], [stage],
            (received, scatter, gather, field, alpha, state, *carried), flops,
        )
    send, data, alpha = call(
        functools.partial(last_ray_kernel, ITERS - 1, rads), "last_ray", [((devices, LANES), F32), ray, scalar],
        [stage, partials], (received, tiles, pick, links, weights, data, state) + kept, flops,
    )
    norms = exchange(send, devices)
    update, data = call(last_kernel, "last", [model, ray], [], (norms, data, field, alpha, state, *carried))
    return (update.reshape(MB_R, MB_L, cells), data)


def solution(mesh):
    in_specs = (
        P(("lat", "rad"), None, None, None),
        P(("lat", "rad"), None),
        P(("lat", "rad"), None),
        P(("lat", "rad")),
        P(("lat", "rad"), None),
        P(("lat", "rad"), None),
    )
    out_specs = (P("rad", "lat", None), P(("lat", "rad"), None))
    return jax.shard_map(body, mesh=mesh, in_specs=in_specs, out_specs=out_specs, check_vma=False)
```
